32 devices in a mesh: req: 4 (over z), mlp: 8 (over y, x, core).
Axes of the slice: x: 2, y: 2, z: 4, core: 2. Of those that a mesh axis runs over, the one named last changes fastest.
Arguments:
- tokens: bfloat16 [2048, 5120], P(('req', 'mlp')), may hold values from -6 to 6
- norm_scale: float32 [5120], replicated, may hold values from 0.25 to 1.75
- gate_matrix: bfloat16 [5120, 14336], P(None, 'mlp'), may hold values from -0.078125 to 0.078125
- up_matrix: bfloat16 [5120, 14336], P(None, 'mlp'), may hold values from -0.078125 to 0.078125
- down_matrix: bfloat16 [14336, 5120], P('mlp', 'req'), may hold values from -0.046875 to 0.046875
- adapter_down_maps: bfloat16 [8, 32, 5120], P('mlp'), may hold values from -0.078125 to 0.078125
- adapter_gate_up_out: bfloat16 [2, 128, 14336], P(None, None, 'mlp'), may hold values from -1.5 to 1.5
- adapter_down_proj_in: bfloat16 [128, 14336], P(None, 'mlp'), may hold values from -0.046875 to 0.046875
- adapter_down_proj_out: bfloat16 [128, 5120], replicated, may hold values from -1.5 to 1.5
- token_adapters: int32 [2048, 1], P(('req', 'mlp')), may hold values from 0 to 7; in each aligned block of 64 rows (0 to 63, 64 to 127, ...) at most 16 rows name the same one
Outputs:
- mixed: bfloat16 [2048, 5120], P(('req', 'mlp'))
The draws below stay inside these ranges and needn't reach their ends.
Inputs may be any that keep to these rules, and one draw needn't show every extreme that they name: `token_adapters`: among the 64 rows of one device no adapter is named by more than 16 rows, and in every draw some device has an adapter named by exactly 16 of its rows.
All inputs are finite; a program needn't handle non-finite values.
Results may differ from the reference program's by a relative error of at most 0.013.
Values may be sent and summed in bfloat16 or wider, within the bound.
A program may use at most 192 MiB of HBM per device.

```python
import math
import jax
import jax.numpy as jnp
import numpy as np
from jax import lax

MODEL_DIM = 5120
HIDDEN_UNITS = 14336
ADAPTER_RANK = 16
TOK_DEV = 64
CAP = 16
ADAPTER_COUNT = 8
TOKENS = 2048
N_REQ = 4
N_MLP = 8


def level_of(key, dims, split, low, high):
    gain, own = 1.0, jax.random.fold_in(key, 6)
    for axis_at, blocks in split:
        draws = jnp.exp(jax.random.uniform(jax.random.fold_in(own, axis_at), (blocks,), jnp.float32, low / len(split), high / len(split)))
        gain = gain * jnp.repeat(draws, dims[axis_at] // blocks).reshape([-1 if axis == axis_at else 1 for axis in range(len(dims))])
    return gain


def assign_block(key, own, number, rows, amount, top, reach, slope):
    ranking = jax.random.permutation(key, amount)
    packed, usual = shares(amount, rows * top, reach, slope, True), shares(amount, rows * top, reach, slope, False)
    places = jnp.arange(amount)

    def named(lengths, rotation):
        used = int((lengths > 0).sum())
        fixed = max(1, used // 4)
        moved = fixed + (places - fixed + rotation * (used - fixed)) % max(1, amount - fixed)
        return jnp.zeros((amount,), jnp.int32).at[ranking[jnp.where(places < fixed, places, moved)]].set(jnp.asarray(lengths, jnp.int32))

    lengths = jnp.where(number % 4 == 0, named(packed, number // 4), named(usual, number - number // 4 - 1))
    mixed = jax.random.permutation(jax.random.fold_in(own, 3), amount)
    giver, receiver = mixed[0:amount // 2 * 2:2], mixed[1:amount // 2 * 2:2]
    room = jnp.minimum(lengths[giver] - 1, reach - lengths[receiver]) // 2
    room = jnp.where((giver == ranking[0]) | (receiver == ranking[0]) | (lengths[receiver] == 0), 0, jnp.maximum(room, 0))
    moved = jax.random.randint(jax.random.fold_in(own, 4), (amount // 2,), 0, 1 << 20) % (room + 1)
    lengths = lengths.at[giver].add(-moved).at[receiver].add(moved)
    labels = jnp.searchsorted(jnp.cumsum(lengths), jnp.arange(rows * top), side="right").astype(jnp.int32)
    grid = labels.reshape(top, rows).T
    grid = grid[jax.random.permutation(jax.random.fold_in(own, 1), rows)]
    rotation = jax.random.randint(jax.random.fold_in(own, 2), (rows, 1), 0, top)
    return jnp.take_along_axis(grid, (jnp.arange(top)[None, :] + rotation) % top, axis=1)


def shares(number_of, total, bound, lean, full):
    loads = [(1 << 20) // math.isqrt(standing ** lean) + 1 for standing in range(1, number_of + 1)]
    largest = bound if full else min(bound, max(-(-total // number_of), total * loads[0] // sum(loads)))
    least = 1 if total - largest >= number_of - 1 else 0
    given, spare = [largest] + [least] * (number_of - 1), total - largest - least * (number_of - 1)
    while spare > 0:
        movable = [i for i in range(1, number_of) if given[i] < largest] or [i for i in range(1, number_of) if given[i] < bound]
        mass, budget = sum([loads[i] for i in movable]), spare
        for i in movable:
            more = min(bound - given[i], max(1, budget * loads[i] // mass), spare)
            given[i] = given[i] + more
            spare = spare - more
    return np.array(given)


def gaussian(stream_key, shape, scale, most, split=(), kind=jnp.bfloat16):
    values = scale * jax.random.normal(stream_key, shape, jnp.float32)
    if split:
        values = values * level_of(stream_key, shape, split, -0.22, 0.18)
    return jnp.clip(values, -most, most).astype(kind)


def setup_inputs(seed: int = 0) -> dict:
    seeds = jax.random.split(jax.random.key(seed), 11)
    tokens = gaussian(seeds[0], (TOKENS, MODEL_DIM), 1.0, 6.0, ((0, 32),))
    norm_scale = jnp.clip(1.0 + 0.15 * jax.random.normal(seeds[1], (MODEL_DIM,), jnp.float32), 0.25, 1.75)
    gate_matrix = gaussian(seeds[2], (MODEL_DIM, HIDDEN_UNITS), MODEL_DIM ** -0.5, 0.078125, ((1, 8),))
    up_matrix = gaussian(seeds[3], (MODEL_DIM, HIDDEN_UNITS), MODEL_DIM ** -0.5, 0.078125, ((1, 8),))
    down_matrix = gaussian(seeds[4], (HIDDEN_UNITS, MODEL_DIM), HIDDEN_UNITS ** -0.5, 0.046875, ((0, 8), (1, 4)))
    adapter_down_maps = gaussian(seeds[5], (ADAPTER_COUNT, 2 * ADAPTER_RANK, MODEL_DIM), MODEL_DIM ** -0.5, 0.078125, ((0, 8),))
    adapter_gate_up_out = gaussian(seeds[6], (2, ADAPTER_COUNT * ADAPTER_RANK, HIDDEN_UNITS), ADAPTER_RANK ** -0.5, 1.5, ((2, 8),))
    adapter_down_proj_in = gaussian(seeds[7], (ADAPTER_COUNT * ADAPTER_RANK, HIDDEN_UNITS), HIDDEN_UNITS ** -0.5, 0.046875, ((1, 8),))
    adapter_down_proj_out = gaussian(seeds[8], (ADAPTER_COUNT * ADAPTER_RANK, MODEL_DIM), ADAPTER_RANK ** -0.5, 1.5)
    token_adapters_keys = jax.random.split(jax.random.fold_in(seeds[9], 1), TOKENS // TOK_DEV)
    token_adapters_turns = jax.random.permutation(jax.random.fold_in(seeds[9], 3), TOKENS // TOK_DEV)
    token_adapters = jax.vmap(lambda own, number: assign_block(jax.random.fold_in(seeds[9], 2), own, number, TOK_DEV, ADAPTER_COUNT, 1, CAP, 2))(token_adapters_keys, token_adapters_turns).reshape((TOKENS, 1))
    return {"tokens": tokens, "norm_scale": norm_scale, "gate_matrix": gate_matrix, "up_matrix": up_matrix, "down_matrix": down_matrix, "adapter_down_maps": adapter_down_maps, "adapter_gate_up_out": adapter_gate_up_out, "adapter_down_proj_in": adapter_down_proj_in, "adapter_down_proj_out": adapter_down_proj_out, "token_adapters": token_adapters}


EPS = 1e-06

def normalize(tokens, norm_scale):
    widened = tokens.astype(jnp.float32)
    mean_square = lax.optimization_barrier(jnp.mean(widened * widened, axis=-1, keepdims=True))
    return (widened * lax.rsqrt(mean_square + EPS) * norm_scale.astype(jnp.float32)).astype(jnp.bfloat16)

def reference(tokens, norm_scale, gate_matrix, up_matrix, down_matrix, adapter_down_maps, adapter_gate_up_out, adapter_down_proj_in, adapter_down_proj_out, token_adapters):
    normed_input = normalize(tokens, norm_scale)
    adapter_lookup = token_adapters[:, 0]
    selector = adapter_lookup[:, None] == jnp.arange(ADAPTER_COUNT, dtype=jnp.int32)[None, :]
    projected_rows = jnp.dot(normed_input, adapter_down_maps.reshape(ADAPTER_COUNT * 2 * ADAPTER_RANK, MODEL_DIM).T, preferred_element_type=jnp.float32)
    projected_rows = projected_rows.reshape(TOKENS, ADAPTER_COUNT, 2 * ADAPTER_RANK)
    ranks = lax.optimization_barrier(jnp.sum(jnp.where(selector[:, :, None], projected_rows, jnp.float32(0.0)), axis=1)).astype(jnp.bfloat16)
    spread = jnp.where(selector[:, :, None], ranks[:, None, :], jnp.zeros((), jnp.bfloat16))
    gate_rank_values = spread[:, :, :ADAPTER_RANK].reshape(TOKENS, ADAPTER_COUNT * ADAPTER_RANK)
    up_rank_values = spread[:, :, ADAPTER_RANK:].reshape(TOKENS, ADAPTER_COUNT * ADAPTER_RANK)
    picker = jnp.repeat(selector, ADAPTER_RANK, axis=1)
    hidden_slice = HIDDEN_UNITS // N_MLP
    group_rows = TOKENS // N_REQ

    def one_group(group_items):
        grouped_tokens, gate_portion, up_portion, group_picker = group_items
        gate_total = jnp.dot(grouped_tokens, gate_matrix, preferred_element_type=jnp.float32) + jnp.dot(gate_portion, adapter_gate_up_out[0], preferred_element_type=jnp.float32)
        up_total = jnp.dot(grouped_tokens, up_matrix, preferred_element_type=jnp.float32) + jnp.dot(up_portion, adapter_gate_up_out[1], preferred_element_type=jnp.float32)
        hidden_state = (jax.nn.silu(gate_total) * up_total).astype(jnp.bfloat16)

        def add_block(running, block_index):
            down_total, total_rank = running
            leading_unit = (block_index * hidden_slice).astype(jnp.int32)
            hidden_block = lax.dynamic_slice_in_dim(hidden_state, leading_unit, hidden_slice, 1)
            down_block = lax.dynamic_slice_in_dim(down_matrix, leading_unit, hidden_slice, 0)
            adapter_slice = lax.dynamic_slice_in_dim(adapter_down_proj_in, leading_unit, hidden_slice, 1)
            down_term = jnp.dot(hidden_block, down_block, preferred_element_type=jnp.float32)
            rank_term = lax.dot_general(hidden_block, adapter_slice, (((1,), (1,)), ((), ())), preferred_element_type=jnp.float32)
            rank_term = jnp.where(group_picker, rank_term, jnp.float32(0.0))
            down_total = down_total + lax.optimization_barrier(down_term.astype(jnp.bfloat16)).astype(jnp.float32)
            total_rank = total_rank + lax.optimization_barrier(rank_term.astype(jnp.bfloat16)).astype(jnp.float32)
            return ((down_total, total_rank), None)
        start_sums = (jnp.zeros((group_rows, MODEL_DIM), jnp.float32), jnp.zeros((group_rows, ADAPTER_COUNT * ADAPTER_RANK), jnp.float32))
        (down_total, total_rank), _ = lax.scan(add_block, start_sums, jnp.arange(N_MLP, dtype=jnp.int32))
        return (down_total, total_rank)
    projected_down, rank_sum = lax.map(one_group, (normed_input.reshape(N_REQ, group_rows, MODEL_DIM), gate_rank_values.reshape(N_REQ, group_rows, ADAPTER_COUNT * ADAPTER_RANK), up_rank_values.reshape(N_REQ, group_rows, ADAPTER_COUNT * ADAPTER_RANK), picker.reshape(N_REQ, group_rows, ADAPTER_COUNT * ADAPTER_RANK)))
    projected_down = projected_down.reshape(TOKENS, MODEL_DIM)
    down_rank_values = rank_sum.reshape(TOKENS, ADAPTER_COUNT * ADAPTER_RANK).astype(jnp.bfloat16)
    adapter_down_term = jnp.dot(down_rank_values, adapter_down_proj_out, preferred_element_type=jnp.float32)
    return (tokens.astype(jnp.float32) + projected_down + adapter_down_term).astype(jnp.bfloat16)
```

```python
import functools

import jax
import jax.numpy as jnp
from jax import lax
from jax.experimental import pallas as pl
from jax.experimental.pallas import tpu as pltpu
from jax.sharding import PartitionSpec as P

EPS = 1e-06
MESH = pl.DeviceIdType.MESH
F32 = jnp.float32
BF16 = jnp.bfloat16


def tile_of(width):
    return 256 if width % 256 == 0 else 128


def block_kernel(
    n_req,
    n_mlp,
    tokens,
    scale,
    names,
    gate_hbm,
    up_hbm,
    down_hbm,
    maps,
    ups,
    downs_in,
    downs_out,
    out,
    parts,
    x_all,
    a_all,
    w_gate,
    w_up,
    w_down,
    hid,
    acc,
    piece,
    z_in,
    rk_out,
    rk_in,
    w_sem,
    d_sem,
    c_sem,
    a_send,
    a_recv,
    x_send,
    x_recv,
    h_send,
    h_recv,
    p_send,
    p_recv,
    k_send,
    k_recv,
    e_send,
    e_recv,
):
    r = lax.axis_index("req")
    m = lax.axis_index("mlp")
    rows, dim = tokens.shape
    hidden = gate_hbm.shape[1]
    columns = down_hbm.shape[1]
    span = maps.shape[0]
    half = span // 2
    bits = n_mlp.bit_length() - 1
    tile = tile_of(hidden)
    tiles = hidden // tile
    group = n_req * rows

    def flip(index, bit):
        power = 1 << bit
        return index + power * (1 - 2 * ((index // power) % 2))

    def peer(slot):
        index = m
        for stage in range(bits):
            if (slot >> stage) & 1:
                index = flip(index, (stage + 1) % bits)
        return index

    def weight_copies(t):
        at = pl.ds(pl.multiple_of(t * tile, tile), tile)
        return (
            pltpu.make_async_copy(gate_hbm.at[:, at], w_gate.at[:, at], w_sem.at[0, t]),
            pltpu.make_async_copy(up_hbm.at[:, at], w_up.at[:, at], w_sem.at[1, t]),
        )

    for t in range(tiles):
        for copy in weight_copies(t):
            copy.start()
    down_copy = pltpu.make_async_copy(down_hbm, w_down, d_sem)
    down_copy.start()

    barrier = pltpu.get_barrier_semaphore()
    for slot in range(1, n_mlp):
        pl.semaphore_signal(barrier, inc=1, device_id=(r, peer(slot)), device_id_type=MESH)
    for step in range(1, n_req):
        pl.semaphore_signal(
            barrier, inc=1, device_id=((r + step) % n_req, m), device_id_type=MESH
        )
    pl.semaphore_wait(barrier, n_mlp - 1 + n_req - 1)

    def remote(src, dst, send, recv, device):
        return pltpu.make_async_remote_copy(
            src_ref=src,
            dst_ref=dst,
            send_sem=send,
            recv_sem=recv,
            device_id=device,
            device_id_type=MESH,
        )

    own_maps = pl.ds(pl.multiple_of(m * span, span), span)
    map_copies = [
        remote(maps, a_all.at[own_maps, :], a_send.at[s], a_recv.at[s], (r, peer(s)))
        for s in range(1, n_mlp)
    ]
    for copy in map_copies:
        copy.start()
    a_all[own_maps, :] = maps[...]

    def norm_step(i, carry):
        at = pl.ds(pl.multiple_of(i * 16, 16), 16)
        wide = tokens[at, :].astype(F32)
        mean_square = jnp.mean(wide * wide, axis=-1, keepdims=True)
        x_all[at, 0:dim] = (wide * lax.rsqrt(mean_square + EPS) * scale[...]).astype(BF16)
        x_all[at, dim : dim + 128] = jnp.broadcast_to(
            names[at, :].astype(F32), (16, 128)
        ).astype(BF16)
        return carry

    lax.fori_loop(0, rows // 16, norm_step, 0)

    def gather_copy(stage):
        size = rows << stage
        return remote(
            x_all.at[pl.ds(0, size), :],
            x_all.at[pl.ds(size, size), :],
            x_send.at[stage],
            x_recv.at[stage],
            (r, flip(m, (stage + 1) % bits)),
        )

    gather_copy(0).start()
    for copy in map_copies:
        copy.wait_recv()

    def hop(way, step, slot):
        at = pl.ds(slot * rows, rows)
        sign = 1 if way == 0 else -1
        block = r - sign * (step - 1)
        ok = (block >= 0) & (block <= n_req - 1) & (r + sign >= 0) & (r + sign <= n_req - 1)

        def make():
            return remote(
                hid.at[block, at, :],
                hid.at[block, at, :],
                h_send.at[way, step - 1, slot],
                h_recv.at[way, step - 1, slot],
                (r + sign, m),
            )

        return ok, make

    def hop_start(way, step, slot):
        ok, make = hop(way, step, slot)

        @pl.when(ok)
        def _():
            make().start()

    def hop_arrival(way, step, slot):
        at = pl.ds(slot * rows, rows)
        sign = 1 if way == 0 else -1
        block = r - sign * step

        @pl.when((block >= 0) & (block <= n_req - 1))
        def _():
            remote(
                hid.at[block, at, :],
                hid.at[block, at, :],
                h_send.at[way, step - 1, slot],
                h_recv.at[way, step - 1, slot],
                (r - sign, m),
            ).wait_recv()

    middle = n_mlp // 2
    order = [*range(middle), *range(middle + 1, n_mlp), middle]

    def tick(k):
        for step in range(n_req - 1, 0, -1):
            if 0 <= k - step < n_mlp:
                slot = order[k - step]
                for way in (0, 1):
                    hop_arrival(way, step, slot)
                    if step < n_req - 1:
                        hop_start(way, step + 1, slot)

    def rank_copy(slot):
        return remote(
            rk_out.at[slot], rk_in.at[slot], k_send.at[slot], k_recv.at[slot], (r, peer(slot))
        )

    def compute(first, count, wait, ticks):
        size = count * rows
        at = pl.ds(first * rows, size)
        normed = x_all[at, 0:dim]
        adapter = x_all[at, dim : dim + 128].astype(F32)[:, 0:1]
        ranks = lax.dot_general(
            normed, a_all[...], (((1,), (1,)), ((), ())), preferred_element_type=F32
        )
        lane = lax.broadcasted_iota(jnp.int32, ranks.shape, 1)
        mine = adapter == (lane // span).astype(F32)
        low = (lane // half) % 2 == 0
        gate_ranks = jnp.where(mine & low, ranks, 0.0).astype(BF16)
        up_ranks = jnp.where(mine & jnp.logical_not(low), ranks, 0.0).astype(BF16)

        def step(t, carry):
            if wait:
                for copy in weight_copies(t):
                    copy.wait()
            cols = pl.ds(pl.multiple_of(t * tile, tile), tile)
            table = ups[:, cols]
            gate_sum = jnp.dot(
                x_all[at, 0:dim], w_gate[:, cols], preferred_element_type=F32
            ) + jnp.dot(gate_ranks, table, preferred_element_type=F32)
            up_sum = jnp.dot(
                x_all[at, 0:dim], w_up[:, cols], preferred_element_type=F32
            ) + jnp.dot(up_ranks, table, preferred_element_type=F32)
            value = gate_sum / (1.0 + jnp.exp(-gate_sum)) * up_sum
            hid[r, at, cols] = value.astype(BF16)
            return carry

        reached = 0
        for i, k in enumerate(ticks):
            limit = tiles * (i + 1) // (len(ticks) + 1)
            lax.fori_loop(reached, limit, step, 0)
            reached = limit
            tick(k)
        lax.fori_loop(reached, tiles, step, 0)
        for slot in order[first : first + count]:
            hop_start(0, 1, slot)
            hop_start(1, 1, slot)
        terms = lax.dot_general(
            hid[r, at, :], downs_in[...], (((1,), (1,)), ((), ())), preferred_element_type=F32
        )
        lane = lax.broadcasted_iota(jnp.int32, terms.shape, 1)
        terms = jnp.where(adapter == (lane // half).astype(F32), terms, 0.0).astype(BF16)
        for slot in range(first, first + count):
            low_row = (slot - first) * rows
            term = terms[low_row : low_row + rows]
            if slot == 0:
                rk_in[0] = term
            else:
                rk_out[slot] = term
                rank_copy(slot).start()

    gather_copy(0).wait_recv()
    gather_copy(1).start()
    compute(0, 2, True, ())
    done = 0
    for stage in range(1, bits):
        gather_copy(stage).wait_recv()
        if stage + 1 < bits:
            gather_copy(stage + 1).start()
        compute(1 << stage, 1 << stage, False, (done + 1, done + 2))
        done = done + 2

    down_copy.wait()
    narrow = tile_of(columns)

    def staging(slot):
        low_row = slot * group
        if low_row + group <= dim:
            return w_gate.at[pl.ds(low_row, group), pl.ds(0, columns)]
        low_row = (slot - dim // group) * group
        return w_up.at[pl.ds(low_row, group), pl.ds(0, columns)]

    def part_copy(slot):
        return remote(
            staging(slot), parts.at[slot], p_send.at[slot], p_recv.at[slot], (r, peer(slot))
        )

    def down(slot):
        place = staging(slot)
        at = pl.ds(slot * rows, rows)

        def step(t, carry):
            cols = pl.ds(pl.multiple_of(t * narrow, narrow), narrow)
            left = hid[:, at, :].reshape(group, hidden)
            term = jnp.dot(left, w_down[:, cols], preferred_element_type=F32).astype(BF16)
            if slot == 0:
                acc[:, cols] = term.astype(F32)
            else:
                place[:, cols] = term
            return carry

        lax.fori_loop(0, columns // narrow, step, 0)
        if slot > 0:
            part_copy(slot).start()

    def collect(slot):
        part_copy(slot).wait_recv()
        copy = pltpu.make_async_copy(parts.at[slot], piece, c_sem)
        copy.start()
        copy.wait()
        acc[...] += piece[...].astype(F32)

    finished = 0
    for k in range(done, n_mlp + n_req - 1):
        if k > done:
            tick(k)
        while finished <= k - (n_req - 1) and finished < n_mlp:
            down(order[finished])
            if finished >= 3:
                collect(order[finished - 2])
            finished += 1
    for slot in order[n_mlp - 2 :]:
        collect(slot)

    piece[...] = acc[...].astype(BF16)

    def exchange(step):
        target = (r + step) % n_req
        return remote(
            piece.at[pl.ds(pl.multiple_of(target * rows, rows), rows), :],
            z_in.at[r],
            e_send.at[step],
            e_recv.at[step],
            (target, m),
        )

    for step in range(1, n_req):
        exchange(step).start()
    z_in[r] = piece[pl.ds(pl.multiple_of(r * rows, rows), rows), :]
    total = rk_in[0].astype(F32)
    for slot in range(1, n_mlp):
        rank_copy(slot).wait_recv()
        total = total + rk_in[slot].astype(F32)
    total = total.astype(BF16)
    for step in range(1, n_req):
        source = (r + n_req - step) % n_req
        remote(
            piece.at[pl.ds(0, rows), :],
            z_in.at[source],
            e_send.at[step],
            e_recv.at[step],
            (source, m),
        ).wait_recv()
    for c in range(n_req):
        cols = slice(c * columns, (c + 1) * columns)
        out[:, cols] = (
            tokens[:, cols].astype(F32)
            + z_in[c].astype(F32)
            + jnp.dot(total, downs_out[:, cols], preferred_element_type=F32)
        ).astype(BF16)

    for copy in map_copies:
        copy.wait_send()
    for stage in range(bits):
        gather_copy(stage).wait_send()
    for slot in range(n_mlp):
        for way in (0, 1):
            for step in range(1, n_req):
                ok, make = hop(way, step, slot)

                @pl.when(ok)
                def _():
                    make().wait_send()

    for slot in range(1, n_mlp):
        rank_copy(slot).wait_send()
        part_copy(slot).wait_send()
    for step in range(1, n_req):
        exchange(step).wait_send()


def pair_kernel(
    n_req,
    n_mlp,
    tokens_hbm,
    scale,
    names,
    gate_hbm,
    up_hbm,
    down_hbm,
    maps_hbm,
    ups_hbm,
    ins_hbm,
    outs_hbm,
    out,
    far,
    tokens,
    w_gate,
    w_up,
    w_down,
    ups,
    downs_in,
    x_own,
    hid_own,
    hid_near,
    hid_far,
    part,
    core_in,
    one_in,
    two_in,
    z_out,
    z_in,
    pick,
    gate_low,
    up_low,
    rank_in,
    rank_sum,
    rank_far,
    term,
    term_in,
    w_sem,
    l_sem,
    s_sem,
    r_sem,
):
    r = lax.axis_index("req")
    m = lax.axis_index("mlp")
    rows, dim = tokens.shape
    hidden = gate_hbm.shape[1]
    columns = down_hbm.shape[1]
    span = maps_hbm.shape[0]
    half = span // 2
    lanes = pick.shape[0]
    chips = n_mlp // 2
    size = chips * rows
    piece = rows // 2
    tile = tile_of(hidden)
    tiles = hidden // tile
    narrow = tile_of(columns)
    c = m % 2
    q = m // 2

    def flip(index, bit):
        power = 1 << bit
        return index + power * (1 - 2 * ((index // power) % 2))

    def apart(index, bits):
        for bit in range(3):
            if (bits >> bit) & 1:
                index = flip(index, bit)
        return index

    qx, qy, qd = flip(q, 0), flip(q, 1), apart(q, 3)
    first = qx * (1 - c) + qy * c
    second = qy * (1 - c) + qx * c
    near = flip(r, 0)
    across = n_req - 1 - r
    skip = flip(r, 1)
    inner = (r == 1) | (r == 2)
    outer = (r == 0) | (r == 3)
    kind = 1 - (r + r // 2) % 2

    ids = {}

    def sid(*key):
        return ids.setdefault(key, len(ids))

    far_base = [sid("rt", i) for i in range(4)][0]
    z_base = [sid("zr", i) for i in range(n_req)][0]

    def remote(src, dst, send, recv, device):
        return pltpu.make_async_remote_copy(
            src_ref=src,
            dst_ref=dst,
            send_sem=s_sem.at[send],
            recv_sem=r_sem.at[recv],
            device_id=device,
            device_id_type=MESH,
        )

    def on(k, fn):
        pl.when(c == k)(fn)

    def at_rows(block, offset=0, count=None):
        return pl.ds(pl.multiple_of(block * rows + offset, piece), count or rows)

    def plane(s, k):
        return x_own.at[k] if s == 0 else far.at[s - 1, k]

    tok_copy = pltpu.make_async_copy(tokens_hbm, tokens, l_sem.at[0])
    ups_copy = pltpu.make_async_copy(ups_hbm, ups, l_sem.at[1])
    ins_copy = pltpu.make_async_copy(ins_hbm, downs_in, l_sem.at[2])
    down_copy = pltpu.make_async_copy(down_hbm, w_down, l_sem.at[3])
    outs_at = x_own.at[0, pl.ds(0, lanes), pl.ds(0, dim)]
    outs_copy = pltpu.make_async_copy(outs_hbm, outs_at, l_sem.at[4])
    quarter = dim // 4

    def maps_ref(i):
        return part.at[1, i // 2, pl.ds((i % 2) * lanes, lanes), :]

    map_copies = [
        pltpu.make_async_copy(
            maps_hbm.at[:, pl.ds(i * quarter, quarter)],
            part.at[1, i // 2, pl.ds((i % 2) * lanes + e * span, span), :],
            l_sem.at[9 + i * 4 + e],
        )
        for i in range(4)
        for e in range(4)
    ]

    def load(s, k):
        return pltpu.make_async_copy(far.at[s - 1, k], x_own.at[k], l_sem.at[5 + (s - 1) * 2 + k])

    def weight_copies(t):
        at = pl.ds(pl.multiple_of(t * tile, tile), tile)
        return (
            pltpu.make_async_copy(gate_hbm.at[:, at], w_gate.at[:, at], w_sem.at[0, t]),
            pltpu.make_async_copy(up_hbm.at[:, at], w_up.at[:, at], w_sem.at[1, t]),
        )

    tok_copy.start()
    barrier = pltpu.get_barrier_semaphore()
    for d in range(1, n_mlp):
        pl.semaphore_signal(barrier, inc=1, device_id=(r, apart(m, d)), device_id_type=MESH)
    for d in range(1, n_req):
        pl.semaphore_signal(barrier, inc=1, device_id=(apart(r, d), m), device_id_type=MESH)
    for copy in map_copies:
        copy.start()
    ups_copy.start()
    for t in range(tiles):
        for copy in weight_copies(t):
            copy.start()
    ins_copy.start()
    down_copy.start()

    lane = lax.broadcasted_iota(jnp.int32, (lanes, 8 * lanes), 1)
    row = lax.broadcasted_iota(jnp.int32, (lanes, 8 * lanes), 0)
    block, inside = lane // (2 * lanes), lane % (2 * lanes)
    source = block * span + inside % half + half * (inside // lanes)
    pick[...] = jnp.where(row == source, 1.0, 0.0).astype(BF16)

    tok_copy.wait()
    eye = lax.broadcasted_iota(jnp.int32, (rows, rows), 0) == lax.broadcasted_iota(
        jnp.int32, (rows, rows), 1
    )
    spread_names = jnp.broadcast_to(names[...].astype(F32), (rows, rows))
    name_column = jnp.sum(jnp.where(eye, spread_names, 0.0), axis=1, keepdims=True)
    x_own[c, at_rows(q), dim : dim + 128] = jnp.broadcast_to(name_column, (rows, 128)).astype(BF16)

    def norm_step(i, carry):
        at = pl.ds(pl.multiple_of(i * 16, 16), 16)
        to = pl.ds(pl.multiple_of(q * rows + i * 16, 16), 16)
        wide = tokens[at, :].astype(F32)
        mean_square = jnp.mean(wide * wide, axis=-1, keepdims=True)
        x_own[c, to, 0:dim] = (wide * lax.rsqrt(mean_square + EPS) * scale[...]).astype(BF16)
        return carry

    lax.fori_loop(0, rows // 16, norm_step, 0)
    pl.semaphore_wait(barrier, n_mlp - 1 + n_req - 1)

    def gather(s, k, name, landing=False):
        ref = plane(s, k)
        other = (r, q * 2 + 1 - k)
        to_x, to_y = (r, qx * 2 + k), (r, qy * 2 + k)
        at, device, lands = {
            "n1": (at_rows(q), to_x, at_rows(qx)),
            "n2": (at_rows(q), to_y, at_rows(qy)),
            "f1": (at_rows(qx, 0, piece), to_y, at_rows(qd, 0, piece)),
            "f2": (at_rows(qy, piece, piece), to_x, at_rows(qd, piece, piece)),
            "c0": (at_rows(q), other, at_rows(q)),
            "c1": (at_rows(qx), other, at_rows(qx)),
            "c2": (at_rows(qy), other, at_rows(qy)),
            "c3": (at_rows(qd), other, at_rows(qd)),
        }[name]
        i = sid("g", s, k, name)
        if landing:
            return remote(ref.at[lands, :], ref.at[lands, :], i, i, device)
        return remote(ref.at[at, :], ref.at[at, :], i, i, device)

    names_of_gather = ("n1", "n2", "c0", "f1", "c1", "f2", "c2", "c3")

    def z_wait(w, p):
        at = at_rows(q, p * piece, piece)
        i = sid("z", w, p)
        remote(far.at[w, c, at, :], far.at[w, c, at, :], i, i, (near, m)).wait_recv()

    def lead_start(s, k):
        if s > 0:

            @pl.when(outer)
            def _():
                for p in range(2):
                    z_wait(s - 1, p)

        for name in ("n1", "n2", "c0"):
            gather(s, k, name).start()

    def lead_forward(s, k):
        gather(s, k, "n1", True).wait_recv()
        gather(s, k, "f1").start()
        gather(s, k, "c1").start()
        gather(s, k, "n2", True).wait_recv()
        gather(s, k, "f2").start()
        gather(s, k, "c2").start()

    def lead_finish(s, k):
        gather(s, k, "f1", True).wait_recv()
        gather(s, k, "f2", True).wait_recv()
        gather(s, k, "c3").start()

    def follow_most(s, k):
        for name in ("c0", "c1", "c2"):
            gather(s, k, name, True).wait_recv()

    def follow_rest(s, k):
        gather(s, k, "c3", True).wait_recv()

    def z_own(p, in_inner):
        at = at_rows(q, p * piece, piece)
        w = 0 if in_inner else 1
        target = across if in_inner else skip
        return remote(
            x_own.at[c, at, :], far.at[w, c, at, :], sid("zs", p), sid("z", w, p), (target, m)
        )

    def z_next(w, p):
        at = at_rows(q, p * piece, piece)
        return remote(
            far.at[w, c, at, :], far.at[w, c, at, :], sid("zf", w, p), sid("z", w, p), (near, m)
        )

    def z_forward(w, p):
        @pl.when(inner)
        def _():
            z_wait(w, p)
            z_next(w, p).start()

    def z_send(in_inner):
        @pl.when(inner if in_inner else outer)
        def _():
            for p in range(2):
                z_own(p, in_inner).start()

    def rank_copy(k, d):
        i = sid("rx", k, d)
        return remote(rank_in.at[k, 0], rank_in.at[k, d], i, i, (r, apart(m, d)))

    def project(k):
        total = jnp.zeros((size, lanes), F32)
        for i in range(4):
            total = total + lax.dot_general(
                x_own[k, :, i * quarter : (i + 1) * quarter],
                maps_ref(i)[...],
                (((1,), (1,)), ((), ())),
                preferred_element_type=F32,
            )
        adapter = x_own[k, :, dim : dim + 128].astype(F32)
        at_lane = lax.broadcasted_iota(jnp.int32, (rows, lanes), 1) // span
        packed = jnp.zeros((rows, lanes), F32)
        for b in range(chips):
            low = slice(b * rows, (b + 1) * rows)
            mine = (at_lane == b) & (adapter[low] == m.astype(F32))
            packed = packed + jnp.where(mine, total[low], 0.0)
        rank_in[k, 0] = packed.astype(BF16)
        for d in range(1, n_mlp):
            rank_copy(k, d).start()

    def far_rank_copy(k, e):
        target = across if e == 0 else skip
        return remote(
            rank_sum.at[k],
            rank_far.at[kind, k],
            sid("rts", k, e),
            far_base + kind * 2 + k,
            (target, m),
        )

    def sum_ranks(k):
        total = rank_in[k, 0].astype(F32)
        for d in range(1, n_mlp):
            rank_copy(k, d).wait_recv()
            total = total + rank_in[k, d].astype(F32)
        rank_sum[k] = total.astype(BF16)
        for e in range(2):
            far_rank_copy(k, e).start()

    def wait_far_ranks(w, k):
        i = far_base + w * 2 + k
        remote(rank_sum.at[k], rank_far.at[w, k], i, i, (across, m)).wait_recv()

    def compute(k, ranks, hid, ticks, wait_weights=False):
        adapter = x_own[k, :, dim : dim + 128].astype(F32)
        values = jnp.dot(ranks[...], pick[...], preferred_element_type=F32)
        at_lane = lax.broadcasted_iota(jnp.int32, (rows, lanes), 1) // half
        for b in range(chips):
            low = slice(b * rows, (b + 1) * rows)
            mine = adapter[low] == at_lane.astype(F32)
            base = 2 * b * lanes
            gate_low[low, :] = jnp.where(mine, values[:, base : base + lanes], 0.0).astype(BF16)
            up_low[low, :] = jnp.where(
                mine, values[:, base + lanes : base + 2 * lanes], 0.0
            ).astype(BF16)

        def step(t, carry):
            for i in sorted(ticks):

                @pl.when(t == i)
                def _(i=i):
                    for fn in ticks[i]:
                        fn()

            if wait_weights:
                for copy in weight_copies(t):
                    copy.wait()
            cols = pl.ds(pl.multiple_of(t * tile, tile), tile)
            gate_sum = jnp.dot(
                x_own[k, :, 0:dim], w_gate[:, cols], preferred_element_type=F32
            ) + jnp.dot(gate_low[...], ups[0, :, cols], preferred_element_type=F32)
            up_sum = jnp.dot(
                x_own[k, :, 0:dim], w_up[:, cols], preferred_element_type=F32
            ) + jnp.dot(up_low[...], ups[1, :, cols], preferred_element_type=F32)
            hid[k, :, cols] = (gate_sum / (1.0 + jnp.exp(-gate_sum)) * up_sum).astype(BF16)
            return carry

        lax.fori_loop(0, tiles, step, 0)

    def near_copy(k):
        i = sid("h", k)
        return remote(hid_own.at[k], hid_near.at[k], i, i, (near, m))

    def term_copy(k, slot):
        i = sid("k", slot)
        target = apart(q, slot // 2)
        return remote(
            term.at[k, at_rows(target), :], term_in.at[slot], i, i, (r, target * 2 + k)
        )

    def terms(k):
        values = lax.dot_general(
            hid_own[k], downs_in[...], (((1,), (1,)), ((), ())), preferred_element_type=F32
        )
        adapter = x_own[k, :, dim : dim + 128].astype(F32)
        at_lane = lax.broadcasted_iota(jnp.int32, values.shape, 1) // half
        term[k] = jnp.where(adapter == at_lane.astype(F32), values, 0.0).astype(BF16)

        def same():
            term_in[0] = term[k, at_rows(q), :]
            for e in range(1, chips):
                term_copy(k, 2 * e).start()

        def other():
            for e in range(chips):
                term_copy(k, 2 * e + 1).start()

        on(k, same)
        on(1 - k, other)

    def down(b, hid):
        def step(t, carry):
            cols = pl.ds(pl.multiple_of(t * narrow, narrow), narrow)
            value = jnp.dot(
                hid[...].reshape(2 * size, hidden), w_down[:, cols], preferred_element_type=F32
            ).astype(BF16)
            part[b, 0, :, cols] = value[0:size]
            part[b, 1, :, cols] = value[size : 2 * size]
            return carry

        lax.fori_loop(0, columns // narrow, step, 0)

    def down_chunk(b, k, hid):
        def step(t, carry):
            cols = pl.ds(pl.multiple_of(t * narrow, narrow), narrow)
            value = jnp.dot(hid[k], w_down[:, cols], preferred_element_type=F32)
            part[b, k, :, cols] = value.astype(BF16)
            return carry

        lax.fori_loop(0, columns // narrow, step, 0)

    def core_copy(j):
        i = sid("rc", j)
        return remote(part.at[j % 2, 1 - c], core_in.at[j], i, i, (r, q * 2 + 1 - c))

    def one_copy(j, e):
        i = sid("r1", j, e)
        at = at_rows(first) if e == 0 else at_rows(qd)
        return remote(part.at[j % 2, c, at, :], one_in.at[j, e], i, i, (r, first * 2 + c))

    def two_copy(j):
        i = sid("r2", j)
        return remote(
            part.at[j % 2, c, at_rows(second), :], two_in.at[j], i, i, (r, second * 2 + c)
        )

    def home(j):
        if j == 2:
            return near
        return 2 - r // 2 if j == 1 else 3 * (1 - r // 2)

    def z_copy(j):
        return remote(z_out.at[j - 1], z_in.at[r], sid("zo", j), z_base + r, (home(j), m))

    def sum_cores(j):
        core_copy(j).wait_recv()
        b = j % 2
        part[b, c] = (part[b, c].astype(F32) + core_in[j].astype(F32)).astype(BF16)
        for e in range(2):
            one_copy(j, e).start()

    def sum_first(j):
        one_copy(j, 1).wait_recv()
        b, at = j % 2, at_rows(second)
        part[b, c, at, :] = (part[b, c, at, :].astype(F32) + one_in[j, 1].astype(F32)).astype(BF16)
        two_copy(j).start()

    def sum_second(j):
        one_copy(j, 0).wait_recv()
        two_copy(j).wait_recv()
        value = (
            part[j % 2, c, at_rows(q), :].astype(F32)
            + one_in[j, 0].astype(F32)
            + two_in[j].astype(F32)
        ).astype(BF16)
        if j == 0:
            z_in[r] = value
        else:
            z_out[j - 1] = value
            z_copy(j).start()

    def part_free(j):
        core_copy(j).wait_send()
        for e in range(2):
            one_copy(j, e).wait_send()
        two_copy(j).wait_send()

    def take(s, k):
        load(s, k).start()

    def own_free(k):
        def fn():
            for name in names_of_gather:
                gather(0, k, name).wait_send()
            for p in range(2):

                @pl.when(inner)
                def _(p=p):
                    z_own(p, True).wait_send()

                @pl.when(outer)
                def _(p=p):
                    z_own(p, False).wait_send()

        on(k, fn)

    def tick(fn, *args):
        return lambda: fn(*args)

    def tick_on(core, fn, *args):
        return lambda: on(core, lambda: fn(*args))

    on(0, lambda: lead_start(0, 0))
    z_send(True)

    def lead_first():
        lead_forward(0, 0)
        lead_finish(0, 0)

    def follow_first():
        follow_most(0, 0)
        lead_start(0, 1)
        follow_rest(0, 0)

    on(0, lead_first)
    on(1, follow_first)
    for copy in map_copies:
        copy.wait()
    project(0)
    z_send(False)
    z_forward(0, 0)
    ups_copy.wait()
    sum_ranks(0)
    z_forward(0, 1)

    compute(
        0,
        rank_sum.at[0],
        hid_own,
        {
            1: [tick_on(1, lead_forward, 0, 1)],
            3: [tick_on(1, lead_finish, 0, 1)],
            5: [tick_on(0, follow_most, 0, 1), tick_on(0, follow_rest, 0, 1), tick(project, 1)],
            6: [tick_on(0, lead_start, 1, 0)],
        },
        True,
    )
    near_copy(0).start()
    ins_copy.wait()
    terms(0)
    sum_ranks(1)
    compute(
        1,
        rank_sum.at[1],
        hid_own,
        {
            1: [tick(z_forward, 1, 0)],
            3: [tick_on(0, lead_forward, 1, 0), tick(z_forward, 1, 1)],
            4: [tick_on(1, follow_most, 1, 0), tick_on(1, lead_start, 1, 1)],
            5: [tick_on(0, lead_finish, 1, 0)],
            6: [tick_on(1, follow_rest, 1, 0), tick(own_free, 0), tick(take, 1, 0)],
        },
    )
    near_copy(1).start()
    terms(1)
    down_copy.wait()
    down(0, hid_own)
    core_copy(0).start()
    load(1, 0).wait()
    wait_far_ranks(0, 0)
    compute(
        0,
        rank_far.at[0, 0],
        hid_far,
        {
            1: [tick_on(1, lead_forward, 1, 1), tick(sum_cores, 0)],
            3: [tick_on(1, lead_finish, 1, 1), tick(sum_first, 0)],
            4: [tick_on(0, lead_start, 2, 0)],
            5: [
                tick_on(0, follow_most, 1, 1),
                tick_on(0, follow_rest, 1, 1),
                tick(own_free, 1),
                tick(take, 1, 1),
                tick(sum_second, 0),
            ],
        },
    )
    load(1, 1).wait()
    wait_far_ranks(0, 1)
    compute(
        1,
        rank_far.at[0, 1],
        hid_far,
        {
            1: [tick_on(0, lead_forward, 2, 0)],
            2: [tick_on(1, follow_most, 2, 0), tick_on(1, lead_start, 2, 1)],
            4: [tick_on(0, lead_finish, 2, 0)],
            5: [tick_on(1, follow_rest, 2, 0), tick(take, 2, 0)],
        },
    )
    down(1, hid_far)
    core_copy(1).start()
    load(2, 0).wait()
    wait_far_ranks(1, 0)
    compute(
        0,
        rank_far.at[1, 0],
        hid_far,
        {
            1: [tick_on(1, lead_forward, 2, 1), tick(sum_cores, 1)],
            3: [tick_on(1, lead_finish, 2, 1), tick(sum_first, 1)],
            5: [
                tick_on(0, follow_most, 2, 1),
                tick_on(0, follow_rest, 2, 1),
                tick(take, 2, 1),
                tick(sum_second, 1),
            ],
        },
    )
    outs_copy.start()
    part_free(0)
    near_copy(0).wait_recv()
    near_copy(1).wait_recv()
    down(0, hid_near)
    core_copy(2).start()
    part_free(1)
    down_chunk(1, 0, hid_far)
    on(1, lambda: core_copy(3).start())
    load(2, 1).wait()
    wait_far_ranks(1, 1)
    compute(
        1,
        rank_far.at[1, 1],
        hid_far,
        {
            1: [tick(sum_cores, 2)],
            2: [tick_on(0, sum_cores, 3)],
            3: [tick(sum_first, 2)],
            4: [tick_on(0, sum_first, 3)],
            5: [tick(sum_second, 2)],
            6: [tick_on(0, sum_second, 3)],
        },
    )
    down_chunk(1, 1, hid_far)
    on(0, lambda: core_copy(3).start())
    total = term_in[0].astype(F32)
    for slot in range(1, n_mlp):
        term_copy(0, slot).wait_recv()
        total = total + term_in[slot].astype(F32)
    total = total.astype(BF16)
    outs_copy.wait()
    def last():
        sum_cores(3)
        sum_first(3)
        sum_second(3)

    on(1, last)

    for step in range(1, n_req):
        source = apart(r, step)
        remote(
            z_out.at[0], z_in.at[source], z_base + source, z_base + source, (source, m)
        ).wait_recv()
    for b in range(n_req):
        cols = slice(b * columns, (b + 1) * columns)
        out[:, cols] = (
            tokens[:, cols].astype(F32)
            + z_in[b].astype(F32)
            + jnp.dot(total, outs_at[:, cols], preferred_element_type=F32)
        ).astype(BF16)

    def gather_sent(s, k):
        for name in names_of_gather:
            gather(s, k, name).wait_send()

    def terms_sent(k, slots):
        for slot in slots:
            term_copy(k, slot).wait_send()

    for s in (1, 2):
        for k in range(2):
            tick_on(k, gather_sent, s, k)()

    @pl.when(inner)
    def _():
        for w in range(2):
            for p in range(2):
                z_next(w, p).wait_send()

    for k in range(2):
        for d in range(1, n_mlp):
            rank_copy(k, d).wait_send()
        for e in range(2):
            far_rank_copy(k, e).wait_send()
        near_copy(k).wait_send()
        tick_on(k, terms_sent, k, range(2, n_mlp, 2))()
        tick_on(1 - k, terms_sent, k, range(1, n_mlp, 2))()
    part_free(2)
    part_free(3)
    for j in range(1, 4):
        z_copy(j).wait_send()
    assert len(ids) <= s_sem.shape[0], len(ids)


def pair_call(
    tokens,
    norm_scale,
    gate_matrix,
    up_matrix,
    down_matrix,
    adapter_down_maps,
    adapter_gate_up_out,
    adapter_down_proj_in,
    adapter_down_proj_out,
    token_adapters,
):
    n_req, n_mlp = lax.axis_size("req"), lax.axis_size("mlp")
    rows, dim = tokens.shape
    hidden = gate_matrix.shape[1]
    columns = down_matrix.shape[1]
    lanes = adapter_down_proj_in.shape[0]
    chips = n_mlp // 2
    size = chips * rows
    vmem = pl.BlockSpec(memory_space=pltpu.VMEM)
    hbm = pl.BlockSpec(memory_space=pltpu.HBM)
    dma = pltpu.SemaphoreType.DMA
    out, _ = pl.pallas_call(
        functools.partial(pair_kernel, n_req, n_mlp),
        out_shape=(
            jax.ShapeDtypeStruct((rows, dim), BF16),
            jax.ShapeDtypeStruct((2, 2, size, dim + 128), BF16),
        ),
        in_specs=[hbm, vmem, vmem, hbm, hbm, hbm, hbm, hbm, hbm, hbm],
        out_specs=(vmem, hbm),
        scratch_shapes=[
            pltpu.VMEM((rows, dim), BF16),
            pltpu.VMEM((dim, hidden), BF16),
            pltpu.VMEM((dim, hidden), BF16),
            pltpu.VMEM((hidden, columns), BF16),
            pltpu.VMEM((2, lanes, hidden), BF16),
            pltpu.VMEM((lanes, hidden), BF16),
            pltpu.VMEM((2, size, dim + 128), BF16),
            pltpu.VMEM((2, size, hidden), BF16),
            pltpu.VMEM((2, size, hidden), BF16),
            pltpu.VMEM((2, size, hidden), BF16),
            pltpu.VMEM((2, 2, size, columns), BF16),
            pltpu.VMEM((4, size, columns), BF16),
            pltpu.VMEM((4, 2, rows, columns), BF16),
            pltpu.VMEM((4, rows, columns), BF16),
            pltpu.VMEM((3, rows, columns), BF16),
            pltpu.VMEM((n_req, rows, columns), BF16),
            pltpu.VMEM((lanes, 2 * chips * lanes), BF16),
            pltpu.VMEM((size, lanes), BF16),
            pltpu.VMEM((size, lanes), BF16),
            pltpu.VMEM((2, n_mlp, rows, lanes), BF16),
            pltpu.VMEM((2, rows, lanes), BF16),
            pltpu.VMEM((2, 2, rows, lanes), BF16),
            pltpu.VMEM((2, size, lanes), BF16),
            pltpu.VMEM((n_mlp, rows, lanes), BF16),
            dma((2, hidden // tile_of(hidden))),
            dma((25,)),
            dma((128,)),
            dma((128,)),
        ],
        compiler_params=pltpu.CompilerParams(
            collective_id=0, has_side_effects=True, vmem_limit_bytes=67043328
        ),
    )(
        tokens,
        norm_scale.reshape(1, dim),
        token_adapters.reshape(1, rows),
        gate_matrix,
        up_matrix,
        down_matrix,
        adapter_down_maps[0],
        adapter_gate_up_out,
        adapter_down_proj_in,
        adapter_down_proj_out,
    )
    return out


def block_call(
    tokens,
    norm_scale,
    gate_matrix,
    up_matrix,
    down_matrix,
    adapter_down_maps,
    adapter_gate_up_out,
    adapter_down_proj_in,
    adapter_down_proj_out,
    token_adapters,
):
    n_req, n_mlp = lax.axis_size("req"), lax.axis_size("mlp")
    rows, dim = tokens.shape
    hidden = gate_matrix.shape[1]
    columns = down_matrix.shape[1]
    span = adapter_down_maps.shape[1]
    half = span // 2
    ranks = adapter_down_proj_in.shape[0]
    bits = n_mlp.bit_length() - 1
    group = n_req * rows
    ups = adapter_gate_up_out.reshape(2, n_mlp, half, hidden)
    ups = ups.transpose(1, 0, 2, 3).reshape(n_mlp * span, hidden)
    vmem = pl.BlockSpec(memory_space=pltpu.VMEM)
    hbm = pl.BlockSpec(memory_space=pltpu.HBM)
    dma = pltpu.SemaphoreType.DMA
    out, _ = pl.pallas_call(
        functools.partial(block_kernel, n_req, n_mlp),
        out_shape=(
            jax.ShapeDtypeStruct((rows, dim), BF16),
            jax.ShapeDtypeStruct((n_mlp, group, columns), BF16),
        ),
        in_specs=[vmem, vmem, vmem, hbm, hbm, hbm, vmem, vmem, vmem, vmem],
        out_specs=(vmem, hbm),
        scratch_shapes=[
            pltpu.VMEM((n_mlp * rows, dim + 128), BF16),
            pltpu.VMEM((n_mlp * span, dim), BF16),
            pltpu.VMEM((dim, hidden), BF16),
            pltpu.VMEM((dim, hidden), BF16),
            pltpu.VMEM((hidden, columns), BF16),
            pltpu.VMEM((n_req, n_mlp * rows, hidden), BF16),
            pltpu.VMEM((group, columns), F32),
            pltpu.VMEM((group, columns), BF16),
            pltpu.VMEM((n_req, rows, columns), BF16),
            pltpu.VMEM((n_mlp, rows, ranks), BF16),
            pltpu.VMEM((n_mlp, rows, ranks), BF16),
            dma((2, hidden // tile_of(hidden))),
            dma,
            dma,
            dma((n_mlp,)),
            dma((n_mlp,)),
            dma((bits,)),
            dma((bits,)),
            dma((2, n_req - 1, n_mlp)),
            dma((2, n_req - 1, n_mlp)),
            dma((n_mlp,)),
            dma((n_mlp,)),
            dma((n_mlp,)),
            dma((n_mlp,)),
            dma((n_req,)),
            dma((n_req,)),
        ],
        compiler_params=pltpu.CompilerParams(
            collective_id=0, has_side_effects=True, vmem_limit_bytes=67043328
        ),
    )(
        tokens,
        norm_scale.reshape(1, dim),
        token_adapters,
        gate_matrix,
        up_matrix,
        down_matrix,
        adapter_down_maps[0],
        ups,
        adapter_down_proj_in,
        adapter_down_proj_out,
    )
    return out


def solution(mesh):
    per_device = pair_call if (mesh.shape["req"], mesh.shape["mlp"]) == (4, 8) else block_call
    return jax.shard_map(
        per_device,
        mesh=mesh,
        in_specs=(
            P(("req", "mlp"), None),
            P(),
            P(None, "mlp"),
            P(None, "mlp"),
            P("mlp", "req"),
            P("mlp", None, None),
            P(None, None, "mlp"),
            P(None, "mlp"),
            P(),
            P(("req", "mlp"), None),
        ),
        out_specs=P(("req", "mlp"), None),
        check_vma=False,
    )
```

```python
import functools

import jax
import jax.numpy as jnp
from jax import lax
from jax.experimental import pallas as pl
from jax.experimental.pallas import tpu as pltpu
from jax.sharding import PartitionSpec as P

EPS = 1e-06
MESH = pl.DeviceIdType.MESH
F32 = jnp.float32
BF16 = jnp.bfloat16


def tile_of(width):
    return 256 if width % 256 == 0 else 128


def block_kernel(
    n_req,
    n_mlp,
    tokens,
    scale,
    names,
    gate_hbm,
    up_hbm,
    down_hbm,
    maps,
    ups,
    downs_in,
    downs_out,
    out,
    parts,
    x_all,
    a_all,
    w_gate,
    w_up,
    w_down,
    hid,
    acc,
    piece,
    z_in,
    rk_out,
    rk_in,
    w_sem,
    d_sem,
    c_sem,
    a_send,
    a_recv,
    x_send,
    x_recv,
    h_send,
    h_recv,
    p_send,
    p_recv,
    k_send,
    k_recv,
    e_send,
    e_recv,
):
    r = lax.axis_index("req")
    m = lax.axis_index("mlp")
    rows, dim = tokens.shape
    hidden = gate_hbm.shape[1]
    columns = down_hbm.shape[1]
    span = maps.shape[0]
    half = span // 2
    bits = n_mlp.bit_length() - 1
    tile = tile_of(hidden)
    tiles = hidden // tile
    group = n_req * rows

    def flip(index, bit):
        power = 1 << bit
        return index + power * (1 - 2 * ((index // power) % 2))

    def peer(slot):
        index = m
        for stage in range(bits):
            if (slot >> stage) & 1:
                index = flip(index, (stage + 1) % bits)
        return index

    def weight_copies(t):
        at = pl.ds(pl.multiple_of(t * tile, tile), tile)
        return (
            pltpu.make_async_copy(gate_hbm.at[:, at], w_gate.at[:, at], w_sem.at[0, t]),
            pltpu.make_async_copy(up_hbm.at[:, at], w_up.at[:, at], w_sem.at[1, t]),
        )

    for t in range(tiles):
        for copy in weight_copies(t):
            copy.start()
    down_copy = pltpu.make_async_copy(down_hbm, w_down, d_sem)
    down_copy.start()

    barrier = pltpu.get_barrier_semaphore()
    for slot in range(1, n_mlp):
        pl.semaphore_signal(barrier, inc=1, device_id=(r, peer(slot)), device_id_type=MESH)
    for step in range(1, n_req):
        pl.semaphore_signal(
            barrier, inc=1, device_id=((r + step) % n_req, m), device_id_type=MESH
        )
    pl.semaphore_wait(barrier, n_mlp - 1 + n_req - 1)

    def remote(src, dst, send, recv, device):
        return pltpu.make_async_remote_copy(
            src_ref=src,
            dst_ref=dst,
            send_sem=send,
            recv_sem=recv,
            device_id=device,
            device_id_type=MESH,
        )

    own_maps = pl.ds(pl.multiple_of(m * span, span), span)
    map_copies = [
        remote(maps, a_all.at[own_maps, :], a_send.at[s], a_recv.at[s], (r, peer(s)))
        for s in range(1, n_mlp)
    ]
    for copy in map_copies:
        copy.start()
    a_all[own_maps, :] = maps[...]

    def norm_step(i, carry):
        at = pl.ds(pl.multiple_of(i * 16, 16), 16)
        wide = tokens[at, :].astype(F32)
        mean_square = jnp.mean(wide * wide, axis=-1, keepdims=True)
        x_all[at, 0:dim] = (wide * lax.rsqrt(mean_square + EPS) * scale[...]).astype(BF16)
        x_all[at, dim : dim + 128] = jnp.broadcast_to(
            names[at, :].astype(F32), (16, 128)
        ).astype(BF16)
        return carry

    lax.fori_loop(0, rows // 16, norm_step, 0)

    def gather_copy(stage):
        size = rows << stage
        return remote(
            x_all.at[pl.ds(0, size), :],
            x_all.at[pl.ds(size, size), :],
            x_send.at[stage],
            x_recv.at[stage],
            (r, flip(m, (stage + 1) % bits)),
        )

    gather_copy(0).start()
    for copy in map_copies:
        copy.wait_recv()

    def hop(way, step, slot):
        at = pl.ds(slot * rows, rows)
        sign = 1 if way == 0 else -1
        block = r - sign * (step - 1)
        ok = (block >= 0) & (block <= n_req - 1) & (r + sign >= 0) & (r + sign <= n_req - 1)

        def make():
            return remote(
                hid.at[block, at, :],
                hid.at[block, at, :],
                h_send.at[way, step - 1, slot],
                h_recv.at[way, step - 1, slot],
                (r + sign, m),
            )

        return ok, make

    def hop_start(way, step, slot):
        ok, make = hop(way, step, slot)

        @pl.when(ok)
        def _():
            make().start()

    def hop_arrival(way, step, slot):
        at = pl.ds(slot * rows, rows)
        sign = 1 if way == 0 else -1
        block = r - sign * step

        @pl.when((block >= 0) & (block <= n_req - 1))
        def _():
            remote(
                hid.at[block, at, :],
                hid.at[block, at, :],
                h_send.at[way, step - 1, slot],
                h_recv.at[way, step - 1, slot],
                (r - sign, m),
            ).wait_recv()

    middle = n_mlp // 2
    order = [*range(middle), *range(middle + 1, n_mlp), middle]

    def tick(k):
        for step in range(n_req - 1, 0, -1):
            if 0 <= k - step < n_mlp:
                slot = order[k - step]
                for way in (0, 1):
                    hop_arrival(way, step, slot)
                    if step < n_req - 1:
                        hop_start(way, step + 1, slot)

    def rank_copy(slot):
        return remote(
            rk_out.at[slot], rk_in.at[slot], k_send.at[slot], k_recv.at[slot], (r, peer(slot))
        )

    def compute(first, count, wait, ticks):
        size = count * rows
        at = pl.ds(first * rows, size)
        normed = x_all[at, 0:dim]
        adapter = x_all[at, dim : dim + 128].astype(F32)[:, 0:1]
        ranks = lax.dot_general(
            normed, a_all[...], (((1,), (1,)), ((), ())), preferred_element_type=F32
        )
        lane = lax.broadcasted_iota(jnp.int32, ranks.shape, 1)
        mine = adapter == (lane // span).astype(F32)
        low = (lane // half) % 2 == 0
        gate_ranks = jnp.where(mine & low, ranks, 0.0).astype(BF16)
        up_ranks = jnp.where(mine & jnp.logical_not(low), ranks, 0.0).astype(BF16)

        def step(t, carry):
            if wait:
                for copy in weight_copies(t):
                    copy.wait()
            cols = pl.ds(pl.multiple_of(t * tile, tile), tile)
            table = ups[:, cols]
            gate_sum = jnp.dot(
                x_all[at, 0:dim], w_gate[:, cols], preferred_element_type=F32
            ) + jnp.dot(gate_ranks, table, preferred_element_type=F32)
            up_sum = jnp.dot(
                x_all[at, 0:dim], w_up[:, cols], preferred_element_type=F32
            ) + jnp.dot(up_ranks, table, preferred_element_type=F32)
            value = gate_sum / (1.0 + jnp.exp(-gate_sum)) * up_sum
            hid[r, at, cols] = value.astype(BF16)
            return carry

        reached = 0
        for i, k in enumerate(ticks):
            limit = tiles * (i + 1) // (len(ticks) + 1)
            lax.fori_loop(reached, limit, step, 0)
            reached = limit
            tick(k)
        lax.fori_loop(reached, tiles, step, 0)
        for slot in order[first : first + count]:
            hop_start(0, 1, slot)
            hop_start(1, 1, slot)
        terms = lax.dot_general(
            hid[r, at, :], downs_in[...], (((1,), (1,)), ((), ())), preferred_element_type=F32
        )
        lane = lax.broadcasted_iota(jnp.int32, terms.shape, 1)
        terms = jnp.where(adapter == (lane // half).astype(F32), terms, 0.0).astype(BF16)
        for slot in range(first, first + count):
            low_row = (slot - first) * rows
            term = terms[low_row : low_row + rows]
            if slot == 0:
                rk_in[0] = term
            else:
                rk_out[slot] = term
                rank_copy(slot).start()

    gather_copy(0).wait_recv()
    gather_copy(1).start()
    compute(0, 2, True, ())
    done = 0
    for stage in range(1, bits):
        gather_copy(stage).wait_recv()
        if stage + 1 < bits:
            gather_copy(stage + 1).start()
        compute(1 << stage, 1 << stage, False, (done + 1, done + 2))
        done = done + 2

    down_copy.wait()
    narrow = tile_of(columns)

    def staging(slot):
        low_row = slot * group
        if low_row + group <= dim:
            return w_gate.at[pl.ds(low_row, group), pl.ds(0, columns)]
        low_row = (slot - dim // group) * group
        return w_up.at[pl.ds(low_row, group), pl.ds(0, columns)]

    def part_copy(slot):
        return remote(
            staging(slot), parts.at[slot], p_send.at[slot], p_recv.at[slot], (r, peer(slot))
        )

    def down(slot):
        place = staging(slot)
        at = pl.ds(slot * rows, rows)

        def step(t, carry):
            cols = pl.ds(pl.multiple_of(t * narrow, narrow), narrow)
            left = hid[:, at, :].reshape(group, hidden)
            term = jnp.dot(left, w_down[:, cols], preferred_element_type=F32).astype(BF16)
            if slot == 0:
                acc[:, cols] = term.astype(F32)
            else:
                place[:, cols] = term
            return carry

        lax.fori_loop(0, columns // narrow, step, 0)
        if slot > 0:
            part_copy(slot).start()

    def collect(slot):
        part_copy(slot).wait_recv()
        copy = pltpu.make_async_copy(parts.at[slot], piece, c_sem)
        copy.start()
        copy.wait()
        acc[...] += piece[...].astype(F32)

    finished = 0
    for k in range(done, n_mlp + n_req - 1):
        if k > done:
            tick(k)
        while finished <= k - (n_req - 1) and finished < n_mlp:
            down(order[finished])
            if finished >= 3:
                collect(order[finished - 2])
            finished += 1
    for slot in order[n_mlp - 2 :]:
        collect(slot)

    piece[...] = acc[...].astype(BF16)

    def exchange(step):
        target = (r + step) % n_req
        return remote(
            piece.at[pl.ds(pl.multiple_of(target * rows, rows), rows), :],
            z_in.at[r],
            e_send.at[step],
            e_recv.at[step],
            (target, m),
        )

    for step in range(1, n_req):
        exchange(step).start()
    z_in[r] = piece[pl.ds(pl.multiple_of(r * rows, rows), rows), :]
    total = rk_in[0].astype(F32)
    for slot in range(1, n_mlp):
        rank_copy(slot).wait_recv()
        total = total + rk_in[slot].astype(F32)
    total = total.astype(BF16)
    for step in range(1, n_req):
        source = (r + n_req - step) % n_req
        remote(
            piece.at[pl.ds(0, rows), :],
            z_in.at[source],
            e_send.at[step],
            e_recv.at[step],
            (source, m),
        ).wait_recv()
    for c in range(n_req):
        cols = slice(c * columns, (c + 1) * columns)
        out[:, cols] = (
            tokens[:, cols].astype(F32)
            + z_in[c].astype(F32)
            + jnp.dot(total, downs_out[:, cols], preferred_element_type=F32)
        ).astype(BF16)

    for copy in map_copies:
        copy.wait_send()
    for stage in range(bits):
        gather_copy(stage).wait_send()
    for slot in range(n_mlp):
        for way in (0, 1):
            for step in range(1, n_req):
                ok, make = hop(way, step, slot)

                @pl.when(ok)
                def _():
                    make().wait_send()

    for slot in range(1, n_mlp):
        rank_copy(slot).wait_send()
        part_copy(slot).wait_send()
    for step in range(1, n_req):
        exchange(step).wait_send()


def pair_kernel(
    n_req,
    n_mlp,
    tokens_hbm,
    scale,
    names,
    gate_hbm,
    up_hbm,
    down_hbm,
    maps_hbm,
    ups_hbm,
    ins_hbm,
    outs_hbm,
    out,
    far,
    tokens,
    w_gate,
    w_up,
    w_down,
    ups,
    downs_in,
    x_own,
    hid_own,
    hid_near,
    hid_far,
    part,
    core_in,
    one_in,
    two_in,
    z_out,
    z_in,
    pick,
    gate_low,
    up_low,
    rank_in,
    rank_sum,
    rank_far,
    term,
    term_in,
    w_sem,
    l_sem,
    s_sem,
    r_sem,
):
    r = lax.axis_index("req")
    m = lax.axis_index("mlp")
    rows, dim = tokens.shape
    hidden = gate_hbm.shape[1]
    columns = down_hbm.shape[1]
    span = maps_hbm.shape[0]
    half = span // 2
    lanes = pick.shape[0]
    chips = n_mlp // 2
    size = chips * rows
    piece = rows // 2
    tile = tile_of(hidden)
    tiles = hidden // tile
    narrow = tile_of(columns)
    c = m % 2
    q = m // 2

    def flip(index, bit):
        power = 1 << bit
        return index + power * (1 - 2 * ((index // power) % 2))

    def apart(index, bits):
        for bit in range(3):
            if (bits >> bit) & 1:
                index = flip(index, bit)
        return index

    qx, qy, qd = flip(q, 0), flip(q, 1), apart(q, 3)
    first = qx * (1 - c) + qy * c
    second = qy * (1 - c) + qx * c
    near = flip(r, 0)
    across = n_req - 1 - r
    skip = flip(r, 1)
    inner = (r == 1) | (r == 2)
    outer = (r == 0) | (r == 3)
    kind = 1 - (r + r // 2) % 2

    ids = {}

    def sid(*key):
        return ids.setdefault(key, len(ids))

    far_base = [sid("rt", i) for i in range(4)][0]
    z_base = [sid("zr", i) for i in range(n_req)][0]

    def remote(src, dst, send, recv, device):
        return pltpu.make_async_remote_copy(
            src_ref=src,
            dst_ref=dst,
            send_sem=s_sem.at[send],
            recv_sem=r_sem.at[recv],
            device_id=device,
            device_id_type=MESH,
        )

    def on(k, fn):
        pl.when(c == k)(fn)

    def at_rows(block, offset=0, count=None):
        return pl.ds(pl.multiple_of(block * rows + offset, piece), count or rows)

    def plane(s, k):
        return x_own.at[k] if s == 0 else far.at[s - 1, k]

    tok_copy = pltpu.make_async_copy(tokens_hbm, tokens, l_sem.at[0])
    ups_copy = pltpu.make_async_copy(ups_hbm, ups, l_sem.at[1])
    ins_copy = pltpu.make_async_copy(ins_hbm, downs_in, l_sem.at[2])
    down_copy = pltpu.make_async_copy(down_hbm, w_down, l_sem.at[3])
    outs_at = x_own.at[0, pl.ds(0, lanes), pl.ds(0, dim)]
    outs_copy = pltpu.make_async_copy(outs_hbm, outs_at, l_sem.at[4])
    quarter = dim // 4

    def maps_ref(i):
        return part.at[1, i // 2, pl.ds((i % 2) * lanes, lanes), :]

    map_copies = [
        pltpu.make_async_copy(
            maps_hbm.at[:, pl.ds(i * quarter, quarter)],
            part.at[1, i // 2, pl.ds((i % 2) * lanes + e * span, span), :],
            l_sem.at[9 + i * 4 + e],
        )
        for i in range(4)
        for e in range(4)
    ]

    def load(s, k, i):
        at = at_rows((q, qx, qy, qd)[i])
        return pltpu.make_async_copy(
            far.at[s - 1, k, at, :],
            x_own.at[k, at, :],
            l_sem.at[25 + ((s - 1) * 2 + k) * 4 + i],
        )

    def take_most(s, k):
        for i in range(3):
            load(s, k, i).start()

    def take_rest(s, k):
        load(s, k, 3).start()

    def loaded(s, k):
        for i in range(4):
            load(s, k, i).wait()

    def weight_copies(t):
        at = pl.ds(pl.multiple_of(t * tile, tile), tile)
        return (
            pltpu.make_async_copy(gate_hbm.at[:, at], w_gate.at[:, at], w_sem.at[0, t]),
            pltpu.make_async_copy(up_hbm.at[:, at], w_up.at[:, at], w_sem.at[1, t]),
        )

    tok_copy.start()
    barrier = pltpu.get_barrier_semaphore()
    for d in range(1, n_mlp):
        pl.semaphore_signal(barrier, inc=1, device_id=(r, apart(m, d)), device_id_type=MESH)
    for d in range(1, n_req):
        pl.semaphore_signal(barrier, inc=1, device_id=(apart(r, d), m), device_id_type=MESH)
    for copy in map_copies:
        copy.start()
    ups_copy.start()
    for t in range(tiles):
        for copy in weight_copies(t):
            copy.start()
    ins_copy.start()
    down_copy.start()

    lane = lax.broadcasted_iota(jnp.int32, (lanes, 8 * lanes), 1)
    row = lax.broadcasted_iota(jnp.int32, (lanes, 8 * lanes), 0)
    block, inside = lane // (2 * lanes), lane % (2 * lanes)
    source = block * span + inside % half + half * (inside // lanes)
    pick[...] = jnp.where(row == source, 1.0, 0.0).astype(BF16)

    tok_copy.wait()
    eye = lax.broadcasted_iota(jnp.int32, (rows, rows), 0) == lax.broadcasted_iota(
        jnp.int32, (rows, rows), 1
    )
    spread_names = jnp.broadcast_to(names[...].astype(F32), (rows, rows))
    name_column = jnp.sum(jnp.where(eye, spread_names, 0.0), axis=1, keepdims=True)
    x_own[c, at_rows(q), dim : dim + 128] = jnp.broadcast_to(name_column, (rows, 128)).astype(BF16)

    def norm_step(i, carry):
        at = pl.ds(pl.multiple_of(i * 16, 16), 16)
        to = pl.ds(pl.multiple_of(q * rows + i * 16, 16), 16)
        wide = tokens[at, :].astype(F32)
        mean_square = jnp.mean(wide * wide, axis=-1, keepdims=True)
        x_own[c, to, 0:dim] = (wide * lax.rsqrt(mean_square + EPS) * scale[...]).astype(BF16)
        return carry

    lax.fori_loop(0, rows // 16, norm_step, 0)
    pl.semaphore_wait(barrier, n_mlp - 1 + n_req - 1)

    def gather(s, k, name, landing=False):
        ref = plane(s, k)
        other = (r, q * 2 + 1 - k)
        to_x, to_y = (r, qx * 2 + k), (r, qy * 2 + k)
        at, device, lands = {
            "n1a": (at_rows(q, 0, piece), to_x, at_rows(qx, 0, piece)),
            "n1b": (at_rows(q, piece, piece), to_x, at_rows(qx, piece, piece)),
            "n2a": (at_rows(q, 0, piece), to_y, at_rows(qy, 0, piece)),
            "n2b": (at_rows(q, piece, piece), to_y, at_rows(qy, piece, piece)),
            "f1": (at_rows(qx, 0, piece), to_y, at_rows(qd, 0, piece)),
            "f2": (at_rows(qy, piece, piece), to_x, at_rows(qd, piece, piece)),
            "c0": (at_rows(q), other, at_rows(q)),
            "c1": (at_rows(qx), other, at_rows(qx)),
            "c2": (at_rows(qy), other, at_rows(qy)),
            "c3": (at_rows(qd), other, at_rows(qd)),
        }[name]
        i = sid("g", s, k, name)
        if landing:
            return remote(ref.at[lands, :], ref.at[lands, :], i, i, device)
        return remote(ref.at[at, :], ref.at[at, :], i, i, device)

    names_of_gather = ("n1a", "n2b", "n1b", "n2a", "c0", "f1", "f2", "c1", "c2", "c3")

    def z_wait(w, p):
        at = at_rows(q, p * piece, piece)
        i = sid("z", w, p)
        remote(far.at[w, c, at, :], far.at[w, c, at, :], i, i, (near, m)).wait_recv()

    def lead_start(s, k):
        if s > 0:

            @pl.when(outer)
            def _():
                for p in range(2):
                    z_wait(s - 1, p)

        for name in names_of_gather[:5]:
            gather(s, k, name).start()

    def lead_forward(s, k):
        gather(s, k, "n1a", True).wait_recv()
        gather(s, k, "f1").start()
        gather(s, k, "n2b", True).wait_recv()
        gather(s, k, "f2").start()

    def lead_share(s, k):
        gather(s, k, "n1b", True).wait_recv()
        gather(s, k, "c1").start()
        gather(s, k, "n2a", True).wait_recv()
        gather(s, k, "c2").start()
        if s > 0:
            take_most(s, k)

    def lead_finish(s, k):
        gather(s, k, "f1", True).wait_recv()
        gather(s, k, "f2", True).wait_recv()
        gather(s, k, "c3").start()
        if s > 0:
            take_rest(s, k)

    def follow_most(s, k):
        for name in ("c0", "c1", "c2"):
            gather(s, k, name, True).wait_recv()
        if s > 0:
            take_most(s, k)

    def follow_rest(s, k):
        gather(s, k, "c3", True).wait_recv()
        if s > 0:
            take_rest(s, k)

    def z_own(p, in_inner):
        at = at_rows(q, p * piece, piece)
        w = 0 if in_inner else 1
        target = across if in_inner else skip
        return remote(
            x_own.at[c, at, :], far.at[w, c, at, :], sid("zs", p), sid("z", w, p), (target, m)
        )

    def z_next(w, p):
        at = at_rows(q, p * piece, piece)
        return remote(
            far.at[w, c, at, :], far.at[w, c, at, :], sid("zf", w, p), sid("z", w, p), (near, m)
        )

    def z_forward(w, p):
        @pl.when(inner)
        def _():
            z_wait(w, p)
            z_next(w, p).start()

    def z_send(in_inner):
        @pl.when(inner if in_inner else outer)
        def _():
            for p in range(2):
                z_own(p, in_inner).start()

    def rank_copy(k, d):
        i = sid("rx", k, d)
        return remote(rank_in.at[k, 0], rank_in.at[k, d], i, i, (r, apart(m, d)))

    def project(k):
        total = jnp.zeros((size, lanes), F32)
        for i in range(4):
            total = total + lax.dot_general(
                x_own[k, :, i * quarter : (i + 1) * quarter],
                maps_ref(i)[...],
                (((1,), (1,)), ((), ())),
                preferred_element_type=F32,
            )
        adapter = x_own[k, :, dim : dim + 128].astype(F32)
        at_lane = lax.broadcasted_iota(jnp.int32, (rows, lanes), 1) // span
        packed = jnp.zeros((rows, lanes), F32)
        for b in range(chips):
            low = slice(b * rows, (b + 1) * rows)
            mine = (at_lane == b) & (adapter[low] == m.astype(F32))
            packed = packed + jnp.where(mine, total[low], 0.0)
        rank_in[k, 0] = packed.astype(BF16)
        for d in range(1, n_mlp):
            rank_copy(k, d).start()

    def far_rank_copy(k, e):
        target = across if e == 0 else skip
        return remote(
            rank_sum.at[k],
            rank_far.at[kind, k],
            sid("rts", k, e),
            far_base + kind * 2 + k,
            (target, m),
        )

    def sum_ranks(k):
        total = rank_in[k, 0].astype(F32)
        for d in range(1, n_mlp):
            rank_copy(k, d).wait_recv()
            total = total + rank_in[k, d].astype(F32)
        rank_sum[k] = total.astype(BF16)
        for e in range(2):
            far_rank_copy(k, e).start()

    def wait_far_ranks(w, k):
        i = far_base + w * 2 + k
        remote(rank_sum.at[k], rank_far.at[w, k], i, i, (across, m)).wait_recv()

    def compute(k, ranks, hid, ticks, wait_weights=False):
        adapter = x_own[k, :, dim : dim + 128].astype(F32)
        values = jnp.dot(ranks[...], pick[...], preferred_element_type=F32)
        at_lane = lax.broadcasted_iota(jnp.int32, (rows, lanes), 1) // half
        for b in range(chips):
            low = slice(b * rows, (b + 1) * rows)
            mine = adapter[low] == at_lane.astype(F32)
            base = 2 * b * lanes
            gate_low[low, :] = jnp.where(mine, values[:, base : base + lanes], 0.0).astype(BF16)
            up_low[low, :] = jnp.where(
                mine, values[:, base + lanes : base + 2 * lanes], 0.0
            ).astype(BF16)

        def step(t, carry):
            for i in sorted(ticks):

                @pl.when(t == i)
                def _(i=i):
                    for fn in ticks[i]:
                        fn()

            if wait_weights:
                for copy in weight_copies(t):
                    copy.wait()
            cols = pl.ds(pl.multiple_of(t * tile, tile), tile)
            gate_sum = jnp.dot(
                x_own[k, :, 0:dim], w_gate[:, cols], preferred_element_type=F32
            ) + jnp.dot(gate_low[...], ups[0, :, cols], preferred_element_type=F32)
            up_sum = jnp.dot(
                x_own[k, :, 0:dim], w_up[:, cols], preferred_element_type=F32
            ) + jnp.dot(up_low[...], ups[1, :, cols], preferred_element_type=F32)
            hid[k, :, cols] = (gate_sum / (1.0 + jnp.exp(-gate_sum)) * up_sum).astype(BF16)
            return carry

        lax.fori_loop(0, tiles, step, 0)

    def near_copy(k):
        i = sid("h", k)
        return remote(hid_own.at[k], hid_near.at[k], i, i, (near, m))

    def term_copy(k, slot):
        i = sid("k", slot)
        target = apart(q, slot // 2)
        return remote(
            term.at[k, at_rows(target), :], term_in.at[slot], i, i, (r, target * 2 + k)
        )

    def terms(k):
        values = lax.dot_general(
            hid_own[k], downs_in[...], (((1,), (1,)), ((), ())), preferred_element_type=F32
        )
        adapter = x_own[k, :, dim : dim + 128].astype(F32)
        at_lane = lax.broadcasted_iota(jnp.int32, values.shape, 1) // half
        term[k] = jnp.where(adapter == at_lane.astype(F32), values, 0.0).astype(BF16)

        def same():
            term_in[0] = term[k, at_rows(q), :]
            for e in range(1, chips):
                term_copy(k, 2 * e).start()

        def other():
            for e in range(chips):
                term_copy(k, 2 * e + 1).start()

        on(k, same)
        on(1 - k, other)

    def down(b, hid):
        def step(t, carry):
            cols = pl.ds(pl.multiple_of(t * narrow, narrow), narrow)
            value = jnp.dot(
                hid[...].reshape(2 * size, hidden), w_down[:, cols], preferred_element_type=F32
            ).astype(BF16)
            part[b, 0, :, cols] = value[0:size]
            part[b, 1, :, cols] = value[size : 2 * size]
            return carry

        lax.fori_loop(0, columns // narrow, step, 0)

    def down_chunk(b, k, hid):
        def step(t, carry):
            cols = pl.ds(pl.multiple_of(t * narrow, narrow), narrow)
            value = jnp.dot(hid[k], w_down[:, cols], preferred_element_type=F32)
            part[b, k, :, cols] = value.astype(BF16)
            return carry

        lax.fori_loop(0, columns // narrow, step, 0)

    def core_copy(j):
        i = sid("rc", j)
        return remote(part.at[j % 2, 1 - c], core_in.at[j], i, i, (r, q * 2 + 1 - c))

    def one_copy(j, e):
        i = sid("r1", j, e)
        at = at_rows(first) if e == 0 else at_rows(qd)
        return remote(part.at[j % 2, c, at, :], one_in.at[j, e], i, i, (r, first * 2 + c))

    def two_copy(j):
        i = sid("r2", j)
        return remote(
            part.at[j % 2, c, at_rows(second), :], two_in.at[j], i, i, (r, second * 2 + c)
        )

    def home(j):
        if j == 2:
            return near
        return 2 - r // 2 if j == 1 else 3 * (1 - r // 2)

    def z_copy(j):
        return remote(z_out.at[j - 1], z_in.at[r], sid("zo", j), z_base + r, (home(j), m))

    def sum_cores(j):
        core_copy(j).wait_recv()
        b = j % 2
        part[b, c] = (part[b, c].astype(F32) + core_in[j].astype(F32)).astype(BF16)
        for e in range(2):
            one_copy(j, e).start()

    def sum_first(j):
        one_copy(j, 1).wait_recv()
        b, at = j % 2, at_rows(second)
        part[b, c, at, :] = (part[b, c, at, :].astype(F32) + one_in[j, 1].astype(F32)).astype(BF16)
        two_copy(j).start()

    def sum_second(j):
        one_copy(j, 0).wait_recv()
        two_copy(j).wait_recv()
        value = (
            part[j % 2, c, at_rows(q), :].astype(F32)
            + one_in[j, 0].astype(F32)
            + two_in[j].astype(F32)
        ).astype(BF16)
        if j == 0:
            z_in[r] = value
        else:
            z_out[j - 1] = value
            z_copy(j).start()

    def part_free(j):
        core_copy(j).wait_send()
        for e in range(2):
            one_copy(j, e).wait_send()
        two_copy(j).wait_send()

    def own_free(k):
        def fn():
            for name in names_of_gather:
                gather(0, k, name).wait_send()
            for p in range(2):

                @pl.when(inner)
                def _(p=p):
                    z_own(p, True).wait_send()

                @pl.when(outer)
                def _(p=p):
                    z_own(p, False).wait_send()

        on(k, fn)

    def tick(fn, *args):
        return lambda: fn(*args)

    def tick_on(core, fn, *args):
        return lambda: on(core, lambda: fn(*args))

    def lead_first():
        lead_start(0, 0)
        lead_forward(0, 0)
        z_send(True)
        lead_share(0, 0)
        lead_finish(0, 0)

    def follow_first():
        z_send(True)
        follow_most(0, 0)
        follow_rest(0, 0)

    on(0, lead_first)
    on(1, follow_first)
    for copy in map_copies:
        copy.wait()
    project(0)
    tick_on(1, lead_start, 0, 1)()
    z_send(False)
    z_forward(0, 0)
    ups_copy.wait()
    sum_ranks(0)

    compute(
        0,
        rank_sum.at[0],
        hid_own,
        {
            0: [tick(z_forward, 0, 1)],
            3: [tick_on(1, lead_forward, 0, 1)],
            5: [tick_on(1, lead_share, 0, 1)],
            6: [tick_on(1, lead_finish, 0, 1), tick_on(0, follow_most, 0, 1)],
        },
        True,
    )
    near_copy(0).start()
    tick_on(0, follow_rest, 0, 1)()
    project(1)
    tick_on(0, lead_start, 1, 0)()
    ins_copy.wait()
    terms(0)
    down_copy.wait()
    down_chunk(0, 0, hid_own)
    sum_ranks(1)
    compute(
        1,
        rank_sum.at[1],
        hid_own,
        {
            1: [tick(z_forward, 1, 0)],
            2: [tick(z_forward, 1, 1)],
            3: [tick_on(0, lead_forward, 1, 0)],
            5: [tick(own_free, 0), tick_on(0, lead_share, 1, 0), tick_on(1, lead_start, 1, 1)],
            6: [tick_on(1, follow_most, 1, 0)],
        },
    )
    near_copy(1).start()
    tick_on(0, lead_finish, 1, 0)()
    terms(1)
    down_chunk(0, 1, hid_own)
    core_copy(0).start()
    tick_on(1, follow_rest, 1, 0)()
    wait_far_ranks(0, 0)
    loaded(1, 0)
    compute(
        0,
        rank_far.at[0, 0],
        hid_far,
        {
            1: [tick_on(1, lead_forward, 1, 1)],
            2: [tick(sum_cores, 0)],
            4: [tick(own_free, 1), tick_on(1, lead_share, 1, 1)],
            5: [tick_on(1, lead_finish, 1, 1), tick_on(0, follow_most, 1, 1)],
            6: [tick_on(0, follow_rest, 1, 1), tick(sum_first, 0), tick_on(0, lead_start, 2, 0)],
        },
    )
    wait_far_ranks(0, 1)
    loaded(1, 1)
    compute(
        1,
        rank_far.at[0, 1],
        hid_far,
        {
            2: [tick(sum_second, 0)],
            3: [tick_on(0, lead_forward, 2, 0)],
            5: [tick_on(0, lead_share, 2, 0), tick_on(1, lead_start, 2, 1)],
            6: [tick_on(1, follow_most, 2, 0)],
        },
    )
    tick_on(0, lead_finish, 2, 0)()
    down(1, hid_far)
    core_copy(1).start()
    tick_on(1, follow_rest, 2, 0)()
    wait_far_ranks(1, 0)
    loaded(2, 0)
    compute(
        0,
        rank_far.at[1, 0],
        hid_far,
        {
            1: [tick_on(1, lead_forward, 2, 1)],
            2: [tick(sum_cores, 1)],
            4: [tick_on(1, lead_share, 2, 1)],
            5: [tick_on(1, lead_finish, 2, 1), tick_on(0, follow_most, 2, 1)],
            6: [tick_on(0, follow_rest, 2, 1), tick(sum_first, 1)],
        },
    )
    outs_copy.start()
    part_free(0)
    near_copy(0).wait_recv()
    near_copy(1).wait_recv()
    down(0, hid_near)
    core_copy(2).start()
    sum_second(1)
    part_free(1)
    down_chunk(1, 0, hid_far)
    on(1, lambda: core_copy(3).start())
    wait_far_ranks(1, 1)
    loaded(2, 1)
    compute(
        1,
        rank_far.at[1, 1],
        hid_far,
        {
            0: [tick(sum_cores, 2)],
            1: [tick_on(0, sum_cores, 3)],
            4: [tick(sum_first, 2)],
            5: [tick_on(0, sum_first, 3)],
            6: [tick(sum_second, 2)],
        },
    )
    down_chunk(1, 1, hid_far)
    on(0, lambda: core_copy(3).start())
    tick_on(0, sum_second, 3)()
    total = term_in[0].astype(F32)
    for slot in range(1, n_mlp):
        term_copy(0, slot).wait_recv()
        total = total + term_in[slot].astype(F32)
    total = total.astype(BF16)
    outs_copy.wait()
    def last():
        sum_cores(3)
        sum_first(3)
        sum_second(3)

    on(1, last)

    for step in range(1, n_req):
        source = apart(r, step)
        remote(
            z_out.at[0], z_in.at[source], z_base + source, z_base + source, (source, m)
        ).wait_recv()
    for b in range(n_req):
        cols = slice(b * columns, (b + 1) * columns)
        out[:, cols] = (
            tokens[:, cols].astype(F32)
            + z_in[b].astype(F32)
            + jnp.dot(total, outs_at[:, cols], preferred_element_type=F32)
        ).astype(BF16)

    def gather_sent(s, k):
        for name in names_of_gather:
            gather(s, k, name).wait_send()

    def terms_sent(k, slots):
        for slot in slots:
            term_copy(k, slot).wait_send()

    for s in (1, 2):
        for k in range(2):
            tick_on(k, gather_sent, s, k)()

    @pl.when(inner)
    def _():
        for w in range(2):
            for p in range(2):
                z_next(w, p).wait_send()

    for k in range(2):
        for d in range(1, n_mlp):
            rank_copy(k, d).wait_send()
        for e in range(2):
            far_rank_copy(k, e).wait_send()
        near_copy(k).wait_send()
        tick_on(k, terms_sent, k, range(2, n_mlp, 2))()
        tick_on(1 - k, terms_sent, k, range(1, n_mlp, 2))()
    part_free(2)
    part_free(3)
    for j in range(1, 4):
        z_copy(j).wait_send()
    assert len(ids) <= s_sem.shape[0], len(ids)


def pair_call(
    tokens,
    norm_scale,
    gate_matrix,
    up_matrix,
    down_matrix,
    adapter_down_maps,
    adapter_gate_up_out,
    adapter_down_proj_in,
    adapter_down_proj_out,
    token_adapters,
):
    n_req, n_mlp = lax.axis_size("req"), lax.axis_size("mlp")
    rows, dim = tokens.shape
    hidden = gate_matrix.shape[1]
    columns = down_matrix.shape[1]
    lanes = adapter_down_proj_in.shape[0]
    chips = n_mlp // 2
    size = chips * rows
    vmem = pl.BlockSpec(memory_space=pltpu.VMEM)
    hbm = pl.BlockSpec(memory_space=pltpu.HBM)
    dma = pltpu.SemaphoreType.DMA
    out, _ = pl.pallas_call(
        functools.partial(pair_kernel, n_req, n_mlp),
        out_shape=(
            jax.ShapeDtypeStruct((rows, dim), BF16),
            jax.ShapeDtypeStruct((2, 2, size, dim + 128), BF16),
        ),
        in_specs=[hbm, vmem, vmem, hbm, hbm, hbm, hbm, hbm, hbm, hbm],
        out_specs=(vmem, hbm),
        scratch_shapes=[
            pltpu.VMEM((rows, dim), BF16),
            pltpu.VMEM((dim, hidden), BF16),
            pltpu.VMEM((dim, hidden), BF16),
            pltpu.VMEM((hidden, columns), BF16),
            pltpu.VMEM((2, lanes, hidden), BF16),
            pltpu.VMEM((lanes, hidden), BF16),
            pltpu.VMEM((2, size, dim + 128), BF16),
            pltpu.VMEM((2, size, hidden), BF16),
            pltpu.VMEM((2, size, hidden), BF16),
            pltpu.VMEM((2, size, hidden), BF16),
            pltpu.VMEM((2, 2, size, columns), BF16),
            pltpu.VMEM((4, size, columns), BF16),
            pltpu.VMEM((4, 2, rows, columns), BF16),
            pltpu.VMEM((4, rows, columns), BF16),
            pltpu.VMEM((3, rows, columns), BF16),
            pltpu.VMEM((n_req, rows, columns), BF16),
            pltpu.VMEM((lanes, 2 * chips * lanes), BF16),
            pltpu.VMEM((size, lanes), BF16),
            pltpu.VMEM((size, lanes), BF16),
            pltpu.VMEM((2, n_mlp, rows, lanes), BF16),
            pltpu.VMEM((2, rows, lanes), BF16),
            pltpu.VMEM((2, 2, rows, lanes), BF16),
            pltpu.VMEM((2, size, lanes), BF16),
            pltpu.VMEM((n_mlp, rows, lanes), BF16),
            dma((2, hidden // tile_of(hidden))),
            dma((41,)),
            dma((128,)),
            dma((128,)),
        ],
        compiler_params=pltpu.CompilerParams(
            collective_id=0, has_side_effects=True, vmem_limit_bytes=67043328
        ),
    )(
        tokens,
        norm_scale.reshape(1, dim),
        token_adapters.reshape(1, rows),
        gate_matrix,
        up_matrix,
        down_matrix,
        adapter_down_maps[0],
        adapter_gate_up_out,
        adapter_down_proj_in,
        adapter_down_proj_out,
    )
    return out


def block_call(
    tokens,
    norm_scale,
    gate_matrix,
    up_matrix,
    down_matrix,
    adapter_down_maps,
    adapter_gate_up_out,
    adapter_down_proj_in,
    adapter_down_proj_out,
    token_adapters,
):
    n_req, n_mlp = lax.axis_size("req"), lax.axis_size("mlp")
    rows, dim = tokens.shape
    hidden = gate_matrix.shape[1]
    columns = down_matrix.shape[1]
    span = adapter_down_maps.shape[1]
    half = span // 2
    ranks = adapter_down_proj_in.shape[0]
    bits = n_mlp.bit_length() - 1
    group = n_req * rows
    ups = adapter_gate_up_out.reshape(2, n_mlp, half, hidden)
    ups = ups.transpose(1, 0, 2, 3).reshape(n_mlp * span, hidden)
    vmem = pl.BlockSpec(memory_space=pltpu.VMEM)
    hbm = pl.BlockSpec(memory_space=pltpu.HBM)
    dma = pltpu.SemaphoreType.DMA
    out, _ = pl.pallas_call(
        functools.partial(block_kernel, n_req, n_mlp),
        out_shape=(
            jax.ShapeDtypeStruct((rows, dim), BF16),
            jax.ShapeDtypeStruct((n_mlp, group, columns), BF16),
        ),
        in_specs=[vmem, vmem, vmem, hbm, hbm, hbm, vmem, vmem, vmem, vmem],
        out_specs=(vmem, hbm),
        scratch_shapes=[
            pltpu.VMEM((n_mlp * rows, dim + 128), BF16),
            pltpu.VMEM((n_mlp * span, dim), BF16),
            pltpu.VMEM((dim, hidden), BF16),
            pltpu.VMEM((dim, hidden), BF16),
            pltpu.VMEM((hidden, columns), BF16),
            pltpu.VMEM((n_req, n_mlp * rows, hidden), BF16),
            pltpu.VMEM((group, columns), F32),
            pltpu.VMEM((group, columns), BF16),
            pltpu.VMEM((n_req, rows, columns), BF16),
            pltpu.VMEM((n_mlp, rows, ranks), BF16),
            pltpu.VMEM((n_mlp, rows, ranks), BF16),
            dma((2, hidden // tile_of(hidden))),
            dma,
            dma,
            dma((n_mlp,)),
            dma((n_mlp,)),
            dma((bits,)),
            dma((bits,)),
            dma((2, n_req - 1, n_mlp)),
            dma((2, n_req - 1, n_mlp)),
            dma((n_mlp,)),
            dma((n_mlp,)),
            dma((n_mlp,)),
            dma((n_mlp,)),
            dma((n_req,)),
            dma((n_req,)),
        ],
        compiler_params=pltpu.CompilerParams(
            collective_id=0, has_side_effects=True, vmem_limit_bytes=67043328
        ),
    )(
        tokens,
        norm_scale.reshape(1, dim),
        token_adapters,
        gate_matrix,
        up_matrix,
        down_matrix,
        adapter_down_maps[0],
        ups,
        adapter_down_proj_in,
        adapter_down_proj_out,
    )
    return out


def solution(mesh):
    per_device = pair_call if (mesh.shape["req"], mesh.shape["mlp"]) == (4, 8) else block_call
    return jax.shard_map(
        per_device,
        mesh=mesh,
        in_specs=(
            P(("req", "mlp"), None),
            P(),
            P(None, "mlp"),
            P(None, "mlp"),
            P("mlp", "req"),
            P("mlp", None, None),
            P(None, None, "mlp"),
            P(None, "mlp"),
            P(),
            P(("req", "mlp"), None),
        ),
        out_specs=P(("req", "mlp"), None),
        check_vma=False,
    )
```

```python
import functools

import jax
import jax.numpy as jnp
from jax import lax
from jax.experimental import pallas as pl
from jax.experimental.pallas import tpu as pltpu
from jax.sharding import PartitionSpec as P

EPS = 1e-06
MESH = pl.DeviceIdType.MESH
F32 = jnp.float32
BF16 = jnp.bfloat16


def tile_of(width):
    return 256 if width % 256 == 0 else 128


def block_kernel(
    n_req,
    n_mlp,
    tokens,
    scale,
    names,
    gate_hbm,
    up_hbm,
    down_hbm,
    maps,
    ups,
    downs_in,
    downs_out,
    out,
    parts,
    x_all,
    a_all,
    w_gate,
    w_up,
    w_down,
    hid,
    acc,
    piece,
    z_in,
    rk_out,
    rk_in,
    w_sem,
    d_sem,
    c_sem,
    a_send,
    a_recv,
    x_send,
    x_recv,
    h_send,
    h_recv,
    p_send,
    p_recv,
    k_send,
    k_recv,
    e_send,
    e_recv,
):
    r = lax.axis_index("req")
    m = lax.axis_index("mlp")
    rows, dim = tokens.shape
    hidden = gate_hbm.shape[1]
    columns = down_hbm.shape[1]
    span = maps.shape[0]
    half = span // 2
    bits = n_mlp.bit_length() - 1
    tile = tile_of(hidden)
    tiles = hidden // tile
    group = n_req * rows

    def flip(index, bit):
        power = 1 << bit
        return index + power * (1 - 2 * ((index // power) % 2))

    def peer(slot):
        index = m
        for stage in range(bits):
            if (slot >> stage) & 1:
                index = flip(index, (stage + 1) % bits)
        return index

    def weight_copies(t):
        at = pl.ds(pl.multiple_of(t * tile, tile), tile)
        return (
            pltpu.make_async_copy(gate_hbm.at[:, at], w_gate.at[:, at], w_sem.at[0, t]),
            pltpu.make_async_copy(up_hbm.at[:, at], w_up.at[:, at], w_sem.at[1, t]),
        )

    for t in range(tiles):
        for copy in weight_copies(t):
            copy.start()
    down_copy = pltpu.make_async_copy(down_hbm, w_down, d_sem)
    down_copy.start()

    barrier = pltpu.get_barrier_semaphore()
    for slot in range(1, n_mlp):
        pl.semaphore_signal(barrier, inc=1, device_id=(r, peer(slot)), device_id_type=MESH)
    for step in range(1, n_req):
        pl.semaphore_signal(
            barrier, inc=1, device_id=((r + step) % n_req, m), device_id_type=MESH
        )
    pl.semaphore_wait(barrier, n_mlp - 1 + n_req - 1)

    def remote(src, dst, send, recv, device):
        return pltpu.make_async_remote_copy(
            src_ref=src,
            dst_ref=dst,
            send_sem=send,
            recv_sem=recv,
            device_id=device,
            device_id_type=MESH,
        )

    own_maps = pl.ds(pl.multiple_of(m * span, span), span)
    map_copies = [
        remote(maps, a_all.at[own_maps, :], a_send.at[s], a_recv.at[s], (r, peer(s)))
        for s in range(1, n_mlp)
    ]
    for copy in map_copies:
        copy.start()
    a_all[own_maps, :] = maps[...]

    def norm_step(i, carry):
        at = pl.ds(pl.multiple_of(i * 16, 16), 16)
        wide = tokens[at, :].astype(F32)
        mean_square = jnp.mean(wide * wide, axis=-1, keepdims=True)
        x_all[at, 0:dim] = (wide * lax.rsqrt(mean_square + EPS) * scale[...]).astype(BF16)
        x_all[at, dim : dim + 128] = jnp.broadcast_to(
            names[at, :].astype(F32), (16, 128)
        ).astype(BF16)
        return carry

    lax.fori_loop(0, rows // 16, norm_step, 0)

    def gather_copy(stage):
        size = rows << stage
        return remote(
            x_all.at[pl.ds(0, size), :],
            x_all.at[pl.ds(size, size), :],
            x_send.at[stage],
            x_recv.at[stage],
            (r, flip(m, (stage + 1) % bits)),
        )

    gather_copy(0).start()
    for copy in map_copies:
        copy.wait_recv()

    def hop(way, step, slot):
        at = pl.ds(slot * rows, rows)
        sign = 1 if way == 0 else -1
        block = r - sign * (step - 1)
        ok = (block >= 0) & (block <= n_req - 1) & (r + sign >= 0) & (r + sign <= n_req - 1)

        def make():
            return remote(
                hid.at[block, at, :],
                hid.at[block, at, :],
                h_send.at[way, step - 1, slot],
                h_recv.at[way, step - 1, slot],
                (r + sign, m),
            )

        return ok, make

    def hop_start(way, step, slot):
        ok, make = hop(way, step, slot)

        @pl.when(ok)
        def _():
            make().start()

    def hop_arrival(way, step, slot):
        at = pl.ds(slot * rows, rows)
        sign = 1 if way == 0 else -1
        block = r - sign * step

        @pl.when((block >= 0) & (block <= n_req - 1))
        def _():
            remote(
                hid.at[block, at, :],
                hid.at[block, at, :],
                h_send.at[way, step - 1, slot],
                h_recv.at[way, step - 1, slot],
                (r - sign, m),
            ).wait_recv()

    middle = n_mlp // 2
    order = [*range(middle), *range(middle + 1, n_mlp), middle]

    def tick(k):
        for step in range(n_req - 1, 0, -1):
            if 0 <= k - step < n_mlp:
                slot = order[k - step]
                for way in (0, 1):
                    hop_arrival(way, step, slot)
                    if step < n_req - 1:
                        hop_start(way, step + 1, slot)

    def rank_copy(slot):
        return remote(
            rk_out.at[slot], rk_in.at[slot], k_send.at[slot], k_recv.at[slot], (r, peer(slot))
        )

    def compute(first, count, wait, ticks):
        size = count * rows
        at = pl.ds(first * rows, size)
        normed = x_all[at, 0:dim]
        adapter = x_all[at, dim : dim + 128].astype(F32)[:, 0:1]
        ranks = lax.dot_general(
            normed, a_all[...], (((1,), (1,)), ((), ())), preferred_element_type=F32
        )
        lane = lax.broadcasted_iota(jnp.int32, ranks.shape, 1)
        mine = adapter == (lane // span).astype(F32)
        low = (lane // half) % 2 == 0
        gate_ranks = jnp.where(mine & low, ranks, 0.0).astype(BF16)
        up_ranks = jnp.where(mine & jnp.logical_not(low), ranks, 0.0).astype(BF16)

        def step(t, carry):
            if wait:
                for copy in weight_copies(t):
                    copy.wait()
            cols = pl.ds(pl.multiple_of(t * tile, tile), tile)
            table = ups[:, cols]
            gate_sum = jnp.dot(
                x_all[at, 0:dim], w_gate[:, cols], preferred_element_type=F32
            ) + jnp.dot(gate_ranks, table, preferred_element_type=F32)
            up_sum = jnp.dot(
                x_all[at, 0:dim], w_up[:, cols], preferred_element_type=F32
            ) + jnp.dot(up_ranks, table, preferred_element_type=F32)
            value = gate_sum / (1.0 + jnp.exp(-gate_sum)) * up_sum
            hid[r, at, cols] = value.astype(BF16)
            return carry

        reached = 0
        for i, k in enumerate(ticks):
            limit = tiles * (i + 1) // (len(ticks) + 1)
            lax.fori_loop(reached, limit, step, 0)
            reached = limit
            tick(k)
        lax.fori_loop(reached, tiles, step, 0)
        for slot in order[first : first + count]:
            hop_start(0, 1, slot)
            hop_start(1, 1, slot)
        terms = lax.dot_general(
            hid[r, at, :], downs_in[...], (((1,), (1,)), ((), ())), preferred_element_type=F32
        )
        lane = lax.broadcasted_iota(jnp.int32, terms.shape, 1)
        terms = jnp.where(adapter == (lane // half).astype(F32), terms, 0.0).astype(BF16)
        for slot in range(first, first + count):
            low_row = (slot - first) * rows
            term = terms[low_row : low_row + rows]
            if slot == 0:
                rk_in[0] = term
            else:
                rk_out[slot] = term
                rank_copy(slot).start()

    gather_copy(0).wait_recv()
    gather_copy(1).start()
    compute(0, 2, True, ())
    done = 0
    for stage in range(1, bits):
        gather_copy(stage).wait_recv()
        if stage + 1 < bits:
            gather_copy(stage + 1).start()
        compute(1 << stage, 1 << stage, False, (done + 1, done + 2))
        done = done + 2

    down_copy.wait()
    narrow = tile_of(columns)

    def staging(slot):
        low_row = slot * group
        if low_row + group <= dim:
            return w_gate.at[pl.ds(low_row, group), pl.ds(0, columns)]
        low_row = (slot - dim // group) * group
        return w_up.at[pl.ds(low_row, group), pl.ds(0, columns)]

    def part_copy(slot):
        return remote(
            staging(slot), parts.at[slot], p_send.at[slot], p_recv.at[slot], (r, peer(slot))
        )

    def down(slot):
        place = staging(slot)
        at = pl.ds(slot * rows, rows)

        def step(t, carry):
            cols = pl.ds(pl.multiple_of(t * narrow, narrow), narrow)
            left = hid[:, at, :].reshape(group, hidden)
            term = jnp.dot(left, w_down[:, cols], preferred_element_type=F32).astype(BF16)
            if slot == 0:
                acc[:, cols] = term.astype(F32)
            else:
                place[:, cols] = term
            return carry

        lax.fori_loop(0, columns // narrow, step, 0)
        if slot > 0:
            part_copy(slot).start()

    def collect(slot):
        part_copy(slot).wait_recv()
        copy = pltpu.make_async_copy(parts.at[slot], piece, c_sem)
        copy.start()
        copy.wait()
        acc[...] += piece[...].astype(F32)

    finished = 0
    for k in range(done, n_mlp + n_req - 1):
        if k > done:
            tick(k)
        while finished <= k - (n_req - 1) and finished < n_mlp:
            down(order[finished])
            if finished >= 3:
                collect(order[finished - 2])
            finished += 1
    for slot in order[n_mlp - 2 :]:
        collect(slot)

    piece[...] = acc[...].astype(BF16)

    def exchange(step):
        target = (r + step) % n_req
        return remote(
            piece.at[pl.ds(pl.multiple_of(target * rows, rows), rows), :],
            z_in.at[r],
            e_send.at[step],
            e_recv.at[step],
            (target, m),
        )

    for step in range(1, n_req):
        exchange(step).start()
    z_in[r] = piece[pl.ds(pl.multiple_of(r * rows, rows), rows), :]
    total = rk_in[0].astype(F32)
    for slot in range(1, n_mlp):
        rank_copy(slot).wait_recv()
        total = total + rk_in[slot].astype(F32)
    total = total.astype(BF16)
    for step in range(1, n_req):
        source = (r + n_req - step) % n_req
        remote(
            piece.at[pl.ds(0, rows), :],
            z_in.at[source],
            e_send.at[step],
            e_recv.at[step],
            (source, m),
        ).wait_recv()
    for c in range(n_req):
        cols = slice(c * columns, (c + 1) * columns)
        out[:, cols] = (
            tokens[:, cols].astype(F32)
            + z_in[c].astype(F32)
            + jnp.dot(total, downs_out[:, cols], preferred_element_type=F32)
        ).astype(BF16)

    for copy in map_copies:
        copy.wait_send()
    for stage in range(bits):
        gather_copy(stage).wait_send()
    for slot in range(n_mlp):
        for way in (0, 1):
            for step in range(1, n_req):
                ok, make = hop(way, step, slot)

                @pl.when(ok)
                def _():
                    make().wait_send()

    for slot in range(1, n_mlp):
        rank_copy(slot).wait_send()
        part_copy(slot).wait_send()
    for step in range(1, n_req):
        exchange(step).wait_send()


def pair_kernel(
    n_req,
    n_mlp,
    tokens_hbm,
    scale,
    names,
    gate_hbm,
    up_hbm,
    down_hbm,
    maps_hbm,
    ups_hbm,
    ins_hbm,
    outs_hbm,
    out,
    far,
    w_gate,
    w_up,
    w_down,
    ups,
    downs_in,
    x_own,
    hid,
    hid_near,
    part,
    core_in,
    one_in,
    two_in,
    z_out,
    z_in,
    pick,
    gate_low,
    up_low,
    rank_in,
    ranks,
    term,
    term_in,
    tail_out,
    w_sem,
    l_sem,
    s_sem,
    r_sem,
):
    r = lax.axis_index("req")
    m = lax.axis_index("mlp")
    rows, dim = tokens_hbm.shape
    hidden = gate_hbm.shape[1]
    columns = down_hbm.shape[1]
    span = maps_hbm.shape[0]
    half = span // 2
    lanes = pick.shape[0]
    chips = n_mlp // 2
    size = chips * rows
    piece = rows // 2
    tile = tile_of(hidden)
    tiles = hidden // tile
    narrow = tile_of(columns)
    early, late = 2, tiles - 2
    c = m % 2
    q = m // 2

    def flip(index, bit):
        power = 1 << bit
        return index + power * (1 - 2 * ((index // power) % 2))

    def apart(index, bits):
        for bit in range(3):
            if (bits >> bit) & 1:
                index = flip(index, bit)
        return index

    qx, qy, qd = flip(q, 0), flip(q, 1), apart(q, 3)
    first = qx * (1 - c) + qy * c
    second = qy * (1 - c) + qx * c
    near = flip(r, 0)
    across = n_req - 1 - r
    skip = flip(r, 1)
    inner = (r == 1) | (r == 2)
    outer = (r == 0) | (r == 3)
    kind = 1 - (r + r // 2) % 2

    hid_own, hid_far = hid.at[0], hid.at[1]
    rank_sum = ranks.at[0]

    ids = {}

    def sid(*key):
        return ids.setdefault(key, len(ids))

    far_base = [sid("rt", i) for i in range(4)][0]
    z_base = [sid("zr", i) for i in range(n_req)][0]
    half_base = [sid("zt", i) for i in range(2 * n_req)][0]

    def remote(src, dst, send, recv, device):
        return pltpu.make_async_remote_copy(
            src_ref=src,
            dst_ref=dst,
            send_sem=s_sem.at[send],
            recv_sem=r_sem.at[recv],
            device_id=device,
            device_id_type=MESH,
        )

    def on(k, fn):
        pl.when(c == k)(fn)

    def at_rows(block, offset=0, count=None):
        return pl.ds(pl.multiple_of(block * rows + offset, piece), count or rows)

    def plane(s, k):
        return x_own.at[k] if s == 0 else far.at[s - 1, k]

    quarter = dim // 4
    tok_copies = [
        pltpu.make_async_copy(
            tokens_hbm.at[:, pl.ds(i * quarter, quarter)],
            part.at[0, 0, pl.ds(i * rows, rows), :],
            l_sem.at[41 + i],
        )
        for i in range(4)
    ]
    ups_copy = pltpu.make_async_copy(ups_hbm, ups, l_sem.at[1])
    ins_copy = pltpu.make_async_copy(ins_hbm, downs_in, l_sem.at[2])
    down_copy = pltpu.make_async_copy(down_hbm, w_down, l_sem.at[3])
    outs_at = x_own.at[0, pl.ds(0, lanes), pl.ds(0, dim)]
    outs_copy = pltpu.make_async_copy(outs_hbm, outs_at, l_sem.at[4])
    tokens = x_own.at[0, pl.ds(lanes, rows), pl.ds(0, dim)]
    tok_again = pltpu.make_async_copy(tokens_hbm, tokens, l_sem.at[0])
    def maps_ref(i):
        return part.at[1, i // 2, pl.ds((i % 2) * lanes, lanes), :]

    map_copies = [
        pltpu.make_async_copy(
            maps_hbm.at[:, pl.ds(i * quarter, quarter)],
            part.at[1, i // 2, pl.ds((i % 2) * lanes + e * span, span), :],
            l_sem.at[9 + i * 4 + e],
        )
        for i in range(4)
        for e in range(4)
    ]

    def load(s, k, i):
        at = at_rows((q, qx, qy, qd)[i])
        return pltpu.make_async_copy(
            far.at[s - 1, k, at, :],
            x_own.at[k, at, :],
            l_sem.at[25 + ((s - 1) * 2 + k) * 4 + i],
        )

    def take_most(s, k):
        for i in range(3):
            load(s, k, i).start()

    def take_rest(s, k):
        load(s, k, 3).start()

    def loaded(s, k):
        for i in range(4):
            load(s, k, i).wait()

    def weight_copies(t):
        at = pl.ds(pl.multiple_of(t * tile, tile), tile)
        return (
            pltpu.make_async_copy(gate_hbm.at[:, at], w_gate.at[:, at], w_sem.at[0, t]),
            pltpu.make_async_copy(up_hbm.at[:, at], w_up.at[:, at], w_sem.at[1, t]),
        )

    for copy in tok_copies:
        copy.start()
    barrier = pltpu.get_barrier_semaphore()
    for d in range(1, n_mlp):
        pl.semaphore_signal(barrier, inc=1, device_id=(r, apart(m, d)), device_id_type=MESH)
    for d in range(1, n_req):
        pl.semaphore_signal(barrier, inc=1, device_id=(apart(r, d), m), device_id_type=MESH)
    for d in (2, 3):
        device = (apart(r, d), flip(m, 0))
        pl.semaphore_signal(barrier, inc=1, device_id=device, device_id_type=MESH)
    for copy in map_copies:
        copy.start()
    ups_copy.start()
    for t in range(tiles):
        for copy in weight_copies(t):
            copy.start()
    ins_copy.start()
    down_copy.start()

    for b in range(2 * chips):
        inside = lax.broadcasted_iota(jnp.int32, (lanes, lanes), 1)
        row = lax.broadcasted_iota(jnp.int32, (lanes, lanes), 0)
        source = (b // 2) * span + half * (b % 2) + inside % half
        pick[:, b * lanes : (b + 1) * lanes] = jnp.where(row == source, 1.0, 0.0).astype(BF16)

    for copy in tok_copies:
        copy.wait()
    eye = lax.broadcasted_iota(jnp.int32, (rows, rows), 0) == lax.broadcasted_iota(
        jnp.int32, (rows, rows), 1
    )
    spread_names = jnp.broadcast_to(names[...].astype(F32), (rows, rows))
    name_column = jnp.sum(jnp.where(eye, spread_names, 0.0), axis=1, keepdims=True)
    x_own[c, at_rows(q), dim : dim + 128] = jnp.broadcast_to(name_column, (rows, 128)).astype(BF16)

    def norm_step(i, carry):
        to = pl.ds(pl.multiple_of(q * rows + i * 16, 16), 16)
        wide = [
            part[0, 0, pl.ds(pl.multiple_of(e * rows + i * 16, 16), 16), :].astype(F32)
            for e in range(4)
        ]
        square = sum(jnp.sum(one * one, axis=-1, keepdims=True) for one in wide)
        gain = lax.rsqrt(square / dim + EPS)
        for e in range(4):
            cols = slice(e * quarter, (e + 1) * quarter)
            x_own[c, to, cols] = (wide[e] * gain * scale[:, cols]).astype(BF16)
        return carry

    lax.fori_loop(0, rows // 16, norm_step, 0)
    pl.semaphore_wait(barrier, n_mlp - 1 + n_req - 1 + 2)

    def gather(s, k, name, landing=False):
        ref = plane(s, k)
        other = (r, q * 2 + 1 - k)
        to_x, to_y = (r, qx * 2 + k), (r, qy * 2 + k)
        at, device, lands = {
            "n1a": (at_rows(q, 0, piece), to_x, at_rows(qx, 0, piece)),
            "n1b": (at_rows(q, piece, piece), to_x, at_rows(qx, piece, piece)),
            "n2a": (at_rows(q, 0, piece), to_y, at_rows(qy, 0, piece)),
            "n2b": (at_rows(q, piece, piece), to_y, at_rows(qy, piece, piece)),
            "f1": (at_rows(qx, 0, piece), to_y, at_rows(qd, 0, piece)),
            "f2": (at_rows(qy, piece, piece), to_x, at_rows(qd, piece, piece)),
            "c0": (at_rows(q), other, at_rows(q)),
            "c1": (at_rows(qx), other, at_rows(qx)),
            "c2": (at_rows(qy), other, at_rows(qy)),
            "c3": (at_rows(qd), other, at_rows(qd)),
        }[name]
        i = sid("g", s, k, name)
        if landing:
            return remote(ref.at[lands, :], ref.at[lands, :], i, i, device)
        return remote(ref.at[at, :], ref.at[at, :], i, i, device)

    names_of_gather = ("n1a", "n2b", "n1b", "n2a", "c0", "f1", "f2", "c1", "c2", "c3")

    def z_wait(w, p):
        at = at_rows(q, p * piece, piece)
        i = sid("z", w, p)
        remote(far.at[w, c, at, :], far.at[w, c, at, :], i, i, (near, m)).wait_recv()

    def lead_start(s, k):
        if s > 0:

            @pl.when(outer)
            def _():
                for p in range(2):
                    z_wait(s - 1, p)

        for name in names_of_gather[:5]:
            gather(s, k, name).start()

    def lead_forward(s, k):
        gather(s, k, "n1a", True).wait_recv()
        gather(s, k, "f1").start()
        gather(s, k, "n2b", True).wait_recv()
        gather(s, k, "f2").start()

    def lead_share(s, k):
        gather(s, k, "n1b", True).wait_recv()
        gather(s, k, "c1").start()
        gather(s, k, "n2a", True).wait_recv()
        gather(s, k, "c2").start()
        if s > 0:
            take_most(s, k)

    def lead_finish(s, k):
        gather(s, k, "f1", True).wait_recv()
        gather(s, k, "f2", True).wait_recv()
        gather(s, k, "c3").start()
        if s > 0:
            take_rest(s, k)

    def follow_most(s, k):
        for name in ("c0", "c1", "c2"):
            gather(s, k, name, True).wait_recv()
        if s > 0:
            take_most(s, k)

    def follow_rest(s, k):
        gather(s, k, "c3", True).wait_recv()
        if s > 0:
            take_rest(s, k)

    def z_own(p, in_inner):
        at = at_rows(q, p * piece, piece)
        w = 0 if in_inner else 1
        target = across if in_inner else skip
        return remote(
            x_own.at[c, at, :], far.at[w, c, at, :], sid("zs", p), sid("z", w, p), (target, m)
        )

    def z_next(w, p):
        at = at_rows(q, p * piece, piece)
        return remote(
            far.at[w, c, at, :], far.at[w, c, at, :], sid("zf", w, p), sid("z", w, p), (near, m)
        )

    def z_forward(w, p):
        @pl.when(inner)
        def _():
            z_wait(w, p)
            z_next(w, p).start()

    def z_send(in_inner):
        @pl.when(inner if in_inner else outer)
        def _():
            for p in range(2):
                z_own(p, in_inner).start()

    def rank_copy(k, d):
        i = sid("rx", k, d)
        return remote(rank_in.at[k, 0], rank_in.at[k, d], i, i, (r, apart(m, d)))

    def project(k):
        total = jnp.zeros((size, lanes), F32)
        for i in range(4):
            total = total + lax.dot_general(
                x_own[k, :, i * quarter : (i + 1) * quarter],
                maps_ref(i)[...],
                (((1,), (1,)), ((), ())),
                preferred_element_type=F32,
            )
        adapter = x_own[k, :, dim : dim + 128].astype(F32)
        at_lane = lax.broadcasted_iota(jnp.int32, (rows, lanes), 1) // span
        packed = jnp.zeros((rows, lanes), F32)
        for b in range(chips):
            low = slice(b * rows, (b + 1) * rows)
            mine = (at_lane == b) & (adapter[low] == m.astype(F32))
            packed = packed + jnp.where(mine, total[low], 0.0)
        rank_in[k, 0] = packed.astype(BF16)
        for d in range(1, n_mlp):
            rank_copy(k, d).start()

    def far_rank_copy(k, e):
        target = across if e == 0 else skip
        return remote(
            rank_sum.at[k],
            ranks.at[1 + kind, k],
            sid("rts", k, e),
            far_base + kind * 2 + k,
            (target, m),
        )

    def sum_ranks(k):
        total = rank_in[k, 0].astype(F32)
        for d in range(1, n_mlp):
            rank_copy(k, d).wait_recv()
            total = total + rank_in[k, d].astype(F32)
        rank_sum[k] = total.astype(BF16)
        for e in range(2):
            far_rank_copy(k, e).start()

    def wait_far_ranks(w, k):
        i = far_base + w * 2 + k
        remote(rank_sum.at[k], ranks.at[1 + w, k], i, i, (across, m)).wait_recv()

    def spread(g, k):
        adapter = x_own[k, :, dim : dim + 128].astype(F32)
        at_lane = lax.broadcasted_iota(jnp.int32, (rows, lanes), 1) // half
        for b in range(chips):
            low = slice(b * rows, (b + 1) * rows)
            mine = adapter[low] == at_lane.astype(F32)
            start = 2 * b * lanes
            values = jnp.dot(
                ranks[g, k], pick[:, start : start + 2 * lanes], preferred_element_type=F32
            )
            gate_low[low, :] = jnp.where(mine, values[:, 0:lanes], 0.0).astype(BF16)
            up_low[low, :] = jnp.where(mine, values[:, lanes:], 0.0).astype(BF16)

    def wide_sums(k, cols):
        return (
            jnp.dot(x_own[k, :, 0:dim], w_gate[:, cols], preferred_element_type=F32),
            jnp.dot(x_own[k, :, 0:dim], w_up[:, cols], preferred_element_type=F32),
        )

    def finish_tile(g, k, cols, sums):
        gate_sum = sums[0] + jnp.dot(gate_low[...], ups[0, :, cols], preferred_element_type=F32)
        up_sum = sums[1] + jnp.dot(up_low[...], ups[1, :, cols], preferred_element_type=F32)
        hid[g, k, :, cols] = (gate_sum / (1.0 + jnp.exp(-gate_sum)) * up_sum).astype(BF16)

    def need_weights(low, high):
        for t in range(low, high):
            for copy in weight_copies(t):
                copy.wait()

    def segment(g, k, low, high):
        for t in range(low, high):
            cols = slice(t * tile, (t + 1) * tile)
            finish_tile(g, k, cols, wide_sums(k, cols))

    def near_copy(k):
        i = sid("h", k)
        return remote(hid_own.at[k], hid_near.at[k], i, i, (near, m))

    def term_copy(k, slot):
        i = sid("k", slot)
        target = apart(q, slot // 2)
        return remote(
            term.at[k, at_rows(target), :], term_in.at[slot], i, i, (r, target * 2 + k)
        )

    def terms(k):
        values = lax.dot_general(
            hid_own[k], downs_in[...], (((1,), (1,)), ((), ())), preferred_element_type=F32
        )
        adapter = x_own[k, :, dim : dim + 128].astype(F32)
        at_lane = lax.broadcasted_iota(jnp.int32, values.shape, 1) // half
        term[k] = jnp.where(adapter == at_lane.astype(F32), values, 0.0).astype(BF16)

        def same():
            term_in[0] = term[k, at_rows(q), :]
            for e in range(1, chips):
                term_copy(k, 2 * e).start()

        def other():
            for e in range(chips):
                term_copy(k, 2 * e + 1).start()

        on(k, same)
        on(1 - k, other)

    def down_near(b):
        for k in range(2):
            for t in range(columns // narrow):
                cols = slice(t * narrow, (t + 1) * narrow)
                value = jnp.dot(hid_near[k], w_down[:, cols], preferred_element_type=F32)
                part[b, k, :, cols] = value.astype(BF16)

    def down_chunk(b, g, k):
        for t in range(columns // narrow):
            cols = slice(t * narrow, (t + 1) * narrow)
            value = jnp.dot(hid[g, k], w_down[:, cols], preferred_element_type=F32)
            part[b, k, :, cols] = value.astype(BF16)

    def core_copy(j):
        i = sid("rc", j)
        return remote(part.at[j % 2, 1 - c], core_in.at[j], i, i, (r, q * 2 + 1 - c))

    def one_copy(j, e):
        i = sid("r1", j, e)
        at = at_rows(first) if e == 0 else at_rows(qd)
        return remote(part.at[j % 2, c, at, :], one_in.at[j, e], i, i, (r, first * 2 + c))

    def two_copy(j):
        i = sid("r2", j)
        return remote(
            part.at[j % 2, c, at_rows(second), :], two_in.at[j], i, i, (r, second * 2 + c)
        )

    def home(j):
        if j == 2:
            return near
        return 2 - r // 2 if j == 1 else 3 * (1 - r // 2)

    def z_copy(j):
        return remote(z_out.at[j - 1], z_in.at[r], sid("zo", j), z_base + r, (home(j), m))

    def sum_cores(j):
        core_copy(j).wait_recv()
        b = j % 2

        def add(e, carry):
            at = pl.ds(pl.multiple_of(e * 16, 16), 16)
            value = part[b, c, at, :].astype(F32) + core_in[j, at, :].astype(F32)
            part[b, c, at, :] = value.astype(BF16)
            return carry

        lax.fori_loop(0, size // 16, add, 0)
        for e in range(2):
            one_copy(j, e).start()

    def sum_first(j):
        one_copy(j, 1).wait_recv()
        b, at = j % 2, at_rows(second)
        part[b, c, at, :] = (part[b, c, at, :].astype(F32) + one_in[j, 1].astype(F32)).astype(BF16)
        two_copy(j).start()

    def sum_second(j):
        one_copy(j, 0).wait_recv()
        two_copy(j).wait_recv()
        value = (
            part[j % 2, c, at_rows(q), :].astype(F32)
            + one_in[j, 0].astype(F32)
            + two_in[j].astype(F32)
        ).astype(BF16)
        if j == 0:
            z_in[r] = value
        else:
            z_out[j - 1] = value
            z_copy(j).start()

    low_half = pl.ds(0, columns // 2)
    tail_in = core_in.at[0, :, low_half]
    tail_one = one_in.at[0, :, :, low_half]
    tail_two = two_in.at[0, :, low_half]

    def half_at(h):
        return pl.ds(pl.multiple_of(h * (columns // 2), columns // 2), columns // 2)

    def tail_down(h):
        value = jnp.dot(hid_far[1], w_down[:, half_at(h)], preferred_element_type=F32)
        part[1, 1, :, half_at(h)] = value.astype(BF16)

    def tail_swap():
        i = sid("tc")
        return remote(part.at[1, 1, :, half_at(1 - c)], tail_in, i, i, (r, q * 2 + 1 - c))

    def tail_one_copy(e):
        i = sid("t1", e)
        at = at_rows(first) if e == 0 else at_rows(qd)
        return remote(part.at[1, 1, at, half_at(c)], tail_one.at[e], i, i, (r, first * 2 + c))

    def tail_two_copy():
        i = sid("t2")
        at = at_rows(second)
        return remote(part.at[1, 1, at, half_at(c)], tail_two, i, i, (r, second * 2 + c))

    def tail_z_copy():
        return remote(
            tail_out,
            z_in.at[r, :, half_at(c)],
            sid("tz"),
            half_base + c * n_req + r,
            (home(3), q * 2 + 1),
        )

    def tail_cores():
        tail_swap().wait_recv()
        at = half_at(c)
        part[1, 1, :, at] = (part[1, 1, :, at].astype(F32) + tail_in[...].astype(F32)).astype(BF16)
        for e in range(2):
            tail_one_copy(e).start()

    def tail_first():
        tail_one_copy(1).wait_recv()
        rows_at, at = at_rows(second), half_at(c)
        part[1, 1, rows_at, at] = (
            part[1, 1, rows_at, at].astype(F32) + tail_one[1].astype(F32)
        ).astype(BF16)
        tail_two_copy().start()

    def tail_second():
        tail_one_copy(0).wait_recv()
        tail_two_copy().wait_recv()
        tail_out[...] = (
            part[1, 1, at_rows(q), half_at(c)].astype(F32)
            + tail_one[0].astype(F32)
            + tail_two[...].astype(F32)
        ).astype(BF16)
        tail_z_copy().start()

    def sum_terms():
        total = term_in[0].astype(F32)
        for slot in range(1, n_mlp):
            term_copy(0, slot).wait_recv()
            total = total + term_in[slot].astype(F32)
        term_in[0] = total.astype(BF16)
        outs_copy.wait()
        tok_again.wait()

    def z_arrival(step):
        source = apart(r, step)
        whole = z_in.at[source]

        def wait_whole():
            i = z_base + source
            remote(whole, whole, i, i, (source, m)).wait_recv()

        def wait_halves():
            for h in range(2):
                i = half_base + h * n_req + source
                part_of = z_in.at[source, :, half_at(h)]
                remote(part_of, part_of, i, i, (source, m)).wait_recv()

        if step == 1:
            wait_whole()
        else:
            pl.when(outer & (c == 1))(wait_halves)
            pl.when(inner | (c == 0))(wait_whole)

    def part_free(j):
        core_copy(j).wait_send()
        for e in range(2):
            one_copy(j, e).wait_send()
        two_copy(j).wait_send()

    def own_free(k):
        def fn():
            for name in names_of_gather:
                gather(0, k, name).wait_send()
            for p in range(2):

                @pl.when(inner)
                def _(p=p):
                    z_own(p, True).wait_send()

                @pl.when(outer)
                def _(p=p):
                    z_own(p, False).wait_send()

        on(k, fn)

    def tick(fn, *args):
        return lambda: fn(*args)

    def tick_on(core, fn, *args):
        return lambda: on(core, lambda: fn(*args))

    def lead_first():
        lead_start(0, 0)
        lead_forward(0, 0)
        z_send(True)
        lead_share(0, 0)
        lead_finish(0, 0)

    def follow_first():
        z_send(True)
        follow_most(0, 0)
        follow_rest(0, 0)

    on(0, lead_first)
    on(1, follow_first)
    for copy in map_copies:
        copy.wait()
    project(0)
    tick_on(1, lead_start, 0, 1)()
    z_send(False)
    z_forward(0, 0)
    ups_copy.wait()
    z_forward(0, 1)
    sum_ranks(0)
    need_weights(0, early)

    events = {
        0: (
            [],
            [tick(need_weights, early, late)],
            [
                tick(need_weights, late, tiles),
                tick_on(1, lead_forward, 0, 1),
                tick_on(1, lead_share, 0, 1),
            ],
            [
                ins_copy.wait,
                tick(terms, 0),
                tick_on(1, lead_finish, 0, 1),
                tick_on(0, follow_most, 0, 1),
                tick_on(0, follow_rest, 0, 1),
                tick(project, 1),
                tick_on(0, lead_start, 1, 0),
                down_copy.wait,
            ],
            [tick(sum_ranks, 1)],
        ),
        1: (
            [tick(z_forward, 1, 0), tick(z_forward, 1, 1)],
            [tick_on(0, lead_forward, 1, 0)],
            [
                tick(own_free, 0),
                tick_on(0, lead_share, 1, 0),
                tick_on(1, lead_start, 1, 1),
                lambda: near_copy(0).start(),
            ],
            [
                tick_on(1, follow_most, 1, 0),
                tick_on(0, lead_finish, 1, 0),
                lambda: near_copy(1).start(),
                tick(terms, 1),
            ],
            [
                lambda: core_copy(0).start(),
                tick_on(1, follow_rest, 1, 0),
                tick(wait_far_ranks, 0, 0),
                tick(loaded, 1, 0),
            ],
        ),
        2: (
            [tick(own_free, 1), tick_on(1, lead_forward, 1, 1)],
            [tick_on(1, lead_share, 1, 1), tick(sum_cores, 0)],
            [
                tick_on(1, lead_finish, 1, 1),
                tick_on(0, follow_most, 1, 1),
                tick_on(0, lead_start, 2, 0),
            ],
            [tick_on(0, follow_rest, 1, 1), tick(sum_first, 0)],
            [tick(wait_far_ranks, 0, 1), tick(loaded, 1, 1)],
        ),
        3: (
            [],
            [tick_on(0, lead_forward, 2, 0), tick_on(0, lead_share, 2, 0)],
            [
                tick(sum_second, 0),
                tick_on(1, follow_most, 2, 0),
                tick_on(1, lead_start, 2, 1),
            ],
            [tick_on(0, lead_finish, 2, 0)],
            [
                lambda: core_copy(1).start(),
                tick_on(1, follow_rest, 2, 0),
                tick(wait_far_ranks, 1, 0),
                tick(loaded, 2, 0),
            ],
        ),
        4: (
            [],
            [
                tick(sum_cores, 1),
                tick_on(1, lead_forward, 2, 1),
                tick_on(1, lead_share, 2, 1),
            ],
            [tick_on(0, follow_most, 2, 1)],
            [
                tick(sum_first, 1),
                tick_on(1, lead_finish, 2, 1),
                outs_copy.start,
                tok_again.start,
                tick(part_free, 0),
                lambda: near_copy(0).wait_recv(),
                lambda: near_copy(1).wait_recv(),
                tick(down_near, 0),
                lambda: core_copy(2).start(),
                tick_on(0, follow_rest, 2, 1),
                tick(sum_second, 1),
                tick(part_free, 1),
            ],
            [
                tick_on(1, lambda: core_copy(3).start()),
                tick(wait_far_ranks, 1, 1),
                tick(loaded, 2, 1),
            ],
        ),
        5: (
            [],
            [tick(sum_cores, 2)],
            [tick(sum_first, 2), tick_on(0, sum_cores, 3)],
            [],
            [],
        ),
    }
    chunks = len(events)

    def chunk_step(i, carry):
        k, group = i % 2, i // 2
        g = (group + 1) // 2

        def happen(place):
            for number in range(chunks):
                if events[number][place]:

                    @pl.when(i == number)
                    def _(number=number):
                        for fn in events[number][place]:
                            fn()

        happen(0)

        spread(group, k)
        segment(g, k, 0, early)
        happen(1)
        segment(g, k, early, late)
        happen(2)
        segment(g, k, late, tiles)
        happen(3)

        @pl.when(i < chunks - 1)
        def _():
            down_chunk(g, g, k)

        happen(4)
        return carry

    lax.fori_loop(0, chunks, chunk_step, 0)
    tail_down(1 - c)
    tail_swap().start()
    tail_down(c)
    tail_cores()
    sum_second(2)
    tick_on(0, sum_first, 3)()
    sum_terms()
    tail_first()
    tick_on(0, sum_second, 3)()
    tail_second()

    def gather_sent(s, k):
        for name in names_of_gather:
            gather(s, k, name).wait_send()

    def terms_sent(k, slots):
        for slot in slots:
            term_copy(k, slot).wait_send()

    for s in (1, 2):
        for k in range(2):
            tick_on(k, gather_sent, s, k)()

    @pl.when(inner)
    def _():
        for w in range(2):
            for p in range(2):
                z_next(w, p).wait_send()

    for k in range(2):
        for d in range(1, n_mlp):
            rank_copy(k, d).wait_send()
        for e in range(2):
            far_rank_copy(k, e).wait_send()
        near_copy(k).wait_send()
        tick_on(k, terms_sent, k, range(2, n_mlp, 2))()
        tick_on(1 - k, terms_sent, k, range(1, n_mlp, 2))()
    part_free(2)
    on(1, lambda: core_copy(3).wait_send())

    def last_sent():
        for e in range(2):
            one_copy(3, e).wait_send()
        two_copy(3).wait_send()
        z_copy(3).wait_send()

    on(0, last_sent)
    z_copy(1).wait_send()
    z_copy(2).wait_send()
    for step in range(1, n_req):
        z_arrival(step)
    for b in range(n_req):
        cols = slice(b * columns, (b + 1) * columns)
        out[:, cols] = (
            tokens[:, cols].astype(F32)
            + z_in[b].astype(F32)
            + jnp.dot(term_in[0], outs_at[:, cols], preferred_element_type=F32)
        ).astype(BF16)
    tail_swap().wait_send()
    for e in range(2):
        tail_one_copy(e).wait_send()
    tail_two_copy().wait_send()
    tail_z_copy().wait_send()
    assert len(ids) <= s_sem.shape[0], len(ids)


def pair_call(
    tokens,
    norm_scale,
    gate_matrix,
    up_matrix,
    down_matrix,
    adapter_down_maps,
    adapter_gate_up_out,
    adapter_down_proj_in,
    adapter_down_proj_out,
    token_adapters,
):
    n_req, n_mlp = lax.axis_size("req"), lax.axis_size("mlp")
    rows, dim = tokens.shape
    hidden = gate_matrix.shape[1]
    columns = down_matrix.shape[1]
    lanes = adapter_down_proj_in.shape[0]
    chips = n_mlp // 2
    size = chips * rows
    vmem = pl.BlockSpec(memory_space=pltpu.VMEM)
    hbm = pl.BlockSpec(memory_space=pltpu.HBM)
    dma = pltpu.SemaphoreType.DMA
    out, _ = pl.pallas_call(
        functools.partial(pair_kernel, n_req, n_mlp),
        out_shape=(
            jax.ShapeDtypeStruct((rows, dim), BF16),
            jax.ShapeDtypeStruct((2, 2, size, dim + 128), BF16),
        ),
        in_specs=[hbm, vmem, vmem, hbm, hbm, hbm, hbm, hbm, hbm, hbm],
        out_specs=(vmem, hbm),
        scratch_shapes=[
            pltpu.VMEM((dim, hidden), BF16),
            pltpu.VMEM((dim, hidden), BF16),
            pltpu.VMEM((hidden, columns), BF16),
            pltpu.VMEM((2, lanes, hidden), BF16),
            pltpu.VMEM((lanes, hidden), BF16),
            pltpu.VMEM((2, size, dim + 128), BF16),
            pltpu.VMEM((2, 2, size, hidden), BF16),
            pltpu.VMEM((2, size, hidden), BF16),
            pltpu.VMEM((2, 2, size, columns), BF16),
            pltpu.VMEM((4, size, columns), BF16),
            pltpu.VMEM((4, 2, rows, columns), BF16),
            pltpu.VMEM((4, rows, columns), BF16),
            pltpu.VMEM((3, rows, columns), BF16),
            pltpu.VMEM((n_req, rows, columns), BF16),
            pltpu.VMEM((lanes, 2 * chips * lanes), BF16),
            pltpu.VMEM((size, lanes), BF16),
            pltpu.VMEM((size, lanes), BF16),
            pltpu.VMEM((2, n_mlp, rows, lanes), BF16),
            pltpu.VMEM((3, 2, rows, lanes), BF16),
            pltpu.VMEM((2, size, lanes), BF16),
            pltpu.VMEM((n_mlp, rows, lanes), BF16),
            pltpu.VMEM((rows, columns // 2), BF16),
            dma((2, hidden // tile_of(hidden))),
            dma((45,)),
            dma((144,)),
            dma((144,)),
        ],
        compiler_params=pltpu.CompilerParams(
            collective_id=0, has_side_effects=True, vmem_limit_bytes=67043328
        ),
    )(
        tokens,
        norm_scale.reshape(1, dim),
        token_adapters.reshape(1, rows),
        gate_matrix,
        up_matrix,
        down_matrix,
        adapter_down_maps[0],
        adapter_gate_up_out,
        adapter_down_proj_in,
        adapter_down_proj_out,
    )
    return out


def block_call(
    tokens,
    norm_scale,
    gate_matrix,
    up_matrix,
    down_matrix,
    adapter_down_maps,
    adapter_gate_up_out,
    adapter_down_proj_in,
    adapter_down_proj_out,
    token_adapters,
):
    n_req, n_mlp = lax.axis_size("req"), lax.axis_size("mlp")
    rows, dim = tokens.shape
    hidden = gate_matrix.shape[1]
    columns = down_matrix.shape[1]
    span = adapter_down_maps.shape[1]
    half = span // 2
    ranks = adapter_down_proj_in.shape[0]
    bits = n_mlp.bit_length() - 1
    group = n_req * rows
    ups = adapter_gate_up_out.reshape(2, n_mlp, half, hidden)
    ups = ups.transpose(1, 0, 2, 3).reshape(n_mlp * span, hidden)
    vmem = pl.BlockSpec(memory_space=pltpu.VMEM)
    hbm = pl.BlockSpec(memory_space=pltpu.HBM)
    dma = pltpu.SemaphoreType.DMA
    out, _ = pl.pallas_call(
        functools.partial(block_kernel, n_req, n_mlp),
        out_shape=(
            jax.ShapeDtypeStruct((rows, dim), BF16),
            jax.ShapeDtypeStruct((n_mlp, group, columns), BF16),
        ),
        in_specs=[vmem, vmem, vmem, hbm, hbm, hbm, vmem, vmem, vmem, vmem],
        out_specs=(vmem, hbm),
        scratch_shapes=[
            pltpu.VMEM((n_mlp * rows, dim + 128), BF16),
            pltpu.VMEM((n_mlp * span, dim), BF16),
            pltpu.VMEM((dim, hidden), BF16),
            pltpu.VMEM((dim, hidden), BF16),
            pltpu.VMEM((hidden, columns), BF16),
            pltpu.VMEM((n_req, n_mlp * rows, hidden), BF16),
            pltpu.VMEM((group, columns), F32),
            pltpu.VMEM((group, columns), BF16),
            pltpu.VMEM((n_req, rows, columns), BF16),
            pltpu.VMEM((n_mlp, rows, ranks), BF16),
            pltpu.VMEM((n_mlp, rows, ranks), BF16),
            dma((2, hidden // tile_of(hidden))),
            dma,
            dma,
            dma((n_mlp,)),
            dma((n_mlp,)),
            dma((bits,)),
            dma((bits,)),
            dma((2, n_req - 1, n_mlp)),
            dma((2, n_req - 1, n_mlp)),
            dma((n_mlp,)),
            dma((n_mlp,)),
            dma((n_mlp,)),
            dma((n_mlp,)),
            dma((n_req,)),
            dma((n_req,)),
        ],
        compiler_params=pltpu.CompilerParams(
            collective_id=0, has_side_effects=True, vmem_limit_bytes=67043328
        ),
    )(
        tokens,
        norm_scale.reshape(1, dim),
        token_adapters,
        gate_matrix,
        up_matrix,
        down_matrix,
        adapter_down_maps[0],
        ups,
        adapter_down_proj_in,
        adapter_down_proj_out,
    )
    return out


def solution(mesh):
    per_device = pair_call if (mesh.shape["req"], mesh.shape["mlp"]) == (4, 8) else block_call
    return jax.shard_map(
        per_device,
        mesh=mesh,
        in_specs=(
            P(("req", "mlp"), None),
            P(),
            P(None, "mlp"),
            P(None, "mlp"),
            P("mlp", "req"),
            P("mlp", None, None),
            P(None, None, "mlp"),
            P(None, "mlp"),
            P(),
            P(("req", "mlp"), None),
        ),
        out_specs=P(("req", "mlp"), None),
        check_vma=False,
    )
```

```python
import functools

import jax
import jax.numpy as jnp
from jax import lax
from jax.experimental import pallas as pl
from jax.experimental.pallas import tpu as pltpu
from jax.sharding import PartitionSpec as P

EPS = 1e-06
MESH = pl.DeviceIdType.MESH
F32 = jnp.float32
BF16 = jnp.bfloat16


def tile_of(width):
    return 256 if width % 256 == 0 else 128


def block_kernel(
    n_req,
    n_mlp,
    tokens,
    scale,
    names,
    gate_hbm,
    up_hbm,
    down_hbm,
    maps,
    ups,
    downs_in,
    downs_out,
    out,
    parts,
    x_all,
    a_all,
    w_gate,
    w_up,
    w_down,
    hid,
    acc,
    piece,
    z_in,
    rk_out,
    rk_in,
    w_sem,
    d_sem,
    c_sem,
    a_send,
    a_recv,
    x_send,
    x_recv,
    h_send,
    h_recv,
    p_send,
    p_recv,
    k_send,
    k_recv,
    e_send,
    e_recv,
):
    r = lax.axis_index("req")
    m = lax.axis_index("mlp")
    rows, dim = tokens.shape
    hidden = gate_hbm.shape[1]
    columns = down_hbm.shape[1]
    span = maps.shape[0]
    half = span // 2
    bits = n_mlp.bit_length() - 1
    tile = tile_of(hidden)
    tiles = hidden // tile
    group = n_req * rows

    def flip(index, bit):
        power = 1 << bit
        return index + power * (1 - 2 * ((index // power) % 2))

    def peer(slot):
        index = m
        for stage in range(bits):
            if (slot >> stage) & 1:
                index = flip(index, (stage + 1) % bits)
        return index

    def weight_copies(t):
        at = pl.ds(pl.multiple_of(t * tile, tile), tile)
        return (
            pltpu.make_async_copy(gate_hbm.at[:, at], w_gate.at[:, at], w_sem.at[0, t]),
            pltpu.make_async_copy(up_hbm.at[:, at], w_up.at[:, at], w_sem.at[1, t]),
        )

    for t in range(tiles):
        for copy in weight_copies(t):
            copy.start()
    down_copy = pltpu.make_async_copy(down_hbm, w_down, d_sem)
    down_copy.start()

    barrier = pltpu.get_barrier_semaphore()
    for slot in range(1, n_mlp):
        pl.semaphore_signal(barrier, inc=1, device_id=(r, peer(slot)), device_id_type=MESH)
    for step in range(1, n_req):
        pl.semaphore_signal(
            barrier, inc=1, device_id=((r + step) % n_req, m), device_id_type=MESH
        )
    pl.semaphore_wait(barrier, n_mlp - 1 + n_req - 1)

    def remote(src, dst, send, recv, device):
        return pltpu.make_async_remote_copy(
            src_ref=src,
            dst_ref=dst,
            send_sem=send,
            recv_sem=recv,
            device_id=device,
            device_id_type=MESH,
        )

    own_maps = pl.ds(pl.multiple_of(m * span, span), span)
    map_copies = [
        remote(maps, a_all.at[own_maps, :], a_send.at[s], a_recv.at[s], (r, peer(s)))
        for s in range(1, n_mlp)
    ]
    for copy in map_copies:
        copy.start()
    a_all[own_maps, :] = maps[...]

    def norm_step(i, carry):
        at = pl.ds(pl.multiple_of(i * 16, 16), 16)
        wide = tokens[at, :].astype(F32)
        mean_square = jnp.mean(wide * wide, axis=-1, keepdims=True)
        x_all[at, 0:dim] = (wide * lax.rsqrt(mean_square + EPS) * scale[...]).astype(BF16)
        x_all[at, dim : dim + 128] = jnp.broadcast_to(
            names[at, :].astype(F32), (16, 128)
        ).astype(BF16)
        return carry

    lax.fori_loop(0, rows // 16, norm_step, 0)

    def gather_copy(stage):
        size = rows << stage
        return remote(
            x_all.at[pl.ds(0, size), :],
            x_all.at[pl.ds(size, size), :],
            x_send.at[stage],
            x_recv.at[stage],
            (r, flip(m, (stage + 1) % bits)),
        )

    gather_copy(0).start()
    for copy in map_copies:
        copy.wait_recv()

    def hop(way, step, slot):
        at = pl.ds(slot * rows, rows)
        sign = 1 if way == 0 else -1
        block = r - sign * (step - 1)
        ok = (block >= 0) & (block <= n_req - 1) & (r + sign >= 0) & (r + sign <= n_req - 1)

        def make():
            return remote(
                hid.at[block, at, :],
                hid.at[block, at, :],
                h_send.at[way, step - 1, slot],
                h_recv.at[way, step - 1, slot],
                (r + sign, m),
            )

        return ok, make

    def hop_start(way, step, slot):
        ok, make = hop(way, step, slot)

        @pl.when(ok)
        def _():
            make().start()

    def hop_arrival(way, step, slot):
        at = pl.ds(slot * rows, rows)
        sign = 1 if way == 0 else -1
        block = r - sign * step

        @pl.when((block >= 0) & (block <= n_req - 1))
        def _():
            remote(
                hid.at[block, at, :],
                hid.at[block, at, :],
                h_send.at[way, step - 1, slot],
                h_recv.at[way, step - 1, slot],
                (r - sign, m),
            ).wait_recv()

    middle = n_mlp // 2
    order = [*range(middle), *range(middle + 1, n_mlp), middle]

    def tick(k):
        for step in range(n_req - 1, 0, -1):
            if 0 <= k - step < n_mlp:
                slot = order[k - step]
                for way in (0, 1):
                    hop_arrival(way, step, slot)
                    if step < n_req - 1:
                        hop_start(way, step + 1, slot)

    def rank_copy(slot):
        return remote(
            rk_out.at[slot], rk_in.at[slot], k_send.at[slot], k_recv.at[slot], (r, peer(slot))
        )

    def compute(first, count, wait, ticks):
        size = count * rows
        at = pl.ds(first * rows, size)
        normed = x_all[at, 0:dim]
        adapter = x_all[at, dim : dim + 128].astype(F32)[:, 0:1]
        ranks = lax.dot_general(
            normed, a_all[...], (((1,), (1,)), ((), ())), preferred_element_type=F32
        )
        lane = lax.broadcasted_iota(jnp.int32, ranks.shape, 1)
        mine = adapter == (lane // span).astype(F32)
        low = (lane // half) % 2 == 0
        gate_ranks = jnp.where(mine & low, ranks, 0.0).astype(BF16)
        up_ranks = jnp.where(mine & jnp.logical_not(low), ranks, 0.0).astype(BF16)

        def step(t, carry):
            if wait:
                for copy in weight_copies(t):
                    copy.wait()
            cols = pl.ds(pl.multiple_of(t * tile, tile), tile)
            table = ups[:, cols]
            gate_sum = jnp.dot(
                x_all[at, 0:dim], w_gate[:, cols], preferred_element_type=F32
            ) + jnp.dot(gate_ranks, table, preferred_element_type=F32)
            up_sum = jnp.dot(
                x_all[at, 0:dim], w_up[:, cols], preferred_element_type=F32
            ) + jnp.dot(up_ranks, table, preferred_element_type=F32)
            value = gate_sum / (1.0 + jnp.exp(-gate_sum)) * up_sum
            hid[r, at, cols] = value.astype(BF16)
            return carry

        reached = 0
        for i, k in enumerate(ticks):
            limit = tiles * (i + 1) // (len(ticks) + 1)
            lax.fori_loop(reached, limit, step, 0)
            reached = limit
            tick(k)
        lax.fori_loop(reached, tiles, step, 0)
        for slot in order[first : first + count]:
            hop_start(0, 1, slot)
            hop_start(1, 1, slot)
        terms = lax.dot_general(
            hid[r, at, :], downs_in[...], (((1,), (1,)), ((), ())), preferred_element_type=F32
        )
        lane = lax.broadcasted_iota(jnp.int32, terms.shape, 1)
        terms = jnp.where(adapter == (lane // half).astype(F32), terms, 0.0).astype(BF16)
        for slot in range(first, first + count):
            low_row = (slot - first) * rows
            term = terms[low_row : low_row + rows]
            if slot == 0:
                rk_in[0] = term
            else:
                rk_out[slot] = term
                rank_copy(slot).start()

    gather_copy(0).wait_recv()
    gather_copy(1).start()
    compute(0, 2, True, ())
    done = 0
    for stage in range(1, bits):
        gather_copy(stage).wait_recv()
        if stage + 1 < bits:
            gather_copy(stage + 1).start()
        compute(1 << stage, 1 << stage, False, (done + 1, done + 2))
        done = done + 2

    down_copy.wait()
    narrow = tile_of(columns)

    def staging(slot):
        low_row = slot * group
        if low_row + group <= dim:
            return w_gate.at[pl.ds(low_row, group), pl.ds(0, columns)]
        low_row = (slot - dim // group) * group
        return w_up.at[pl.ds(low_row, group), pl.ds(0, columns)]

    def part_copy(slot):
        return remote(
            staging(slot), parts.at[slot], p_send.at[slot], p_recv.at[slot], (r, peer(slot))
        )

    def down(slot):
        place = staging(slot)
        at = pl.ds(slot * rows, rows)

        def step(t, carry):
            cols = pl.ds(pl.multiple_of(t * narrow, narrow), narrow)
            left = hid[:, at, :].reshape(group, hidden)
            term = jnp.dot(left, w_down[:, cols], preferred_element_type=F32).astype(BF16)
            if slot == 0:
                acc[:, cols] = term.astype(F32)
            else:
                place[:, cols] = term
            return carry

        lax.fori_loop(0, columns // narrow, step, 0)
        if slot > 0:
            part_copy(slot).start()

    def collect(slot):
        part_copy(slot).wait_recv()
        copy = pltpu.make_async_copy(parts.at[slot], piece, c_sem)
        copy.start()
        copy.wait()
        acc[...] += piece[...].astype(F32)

    finished = 0
    for k in range(done, n_mlp + n_req - 1):
        if k > done:
            tick(k)
        while finished <= k - (n_req - 1) and finished < n_mlp:
            down(order[finished])
            if finished >= 3:
                collect(order[finished - 2])
            finished += 1
    for slot in order[n_mlp - 2 :]:
        collect(slot)

    piece[...] = acc[...].astype(BF16)

    def exchange(step):
        target = (r + step) % n_req
        return remote(
            piece.at[pl.ds(pl.multiple_of(target * rows, rows), rows), :],
            z_in.at[r],
            e_send.at[step],
            e_recv.at[step],
            (target, m),
        )

    for step in range(1, n_req):
        exchange(step).start()
    z_in[r] = piece[pl.ds(pl.multiple_of(r * rows, rows), rows), :]
    total = rk_in[0].astype(F32)
    for slot in range(1, n_mlp):
        rank_copy(slot).wait_recv()
        total = total + rk_in[slot].astype(F32)
    total = total.astype(BF16)
    for step in range(1, n_req):
        source = (r + n_req - step) % n_req
        remote(
            piece.at[pl.ds(0, rows), :],
            z_in.at[source],
            e_send.at[step],
            e_recv.at[step],
            (source, m),
        ).wait_recv()
    for c in range(n_req):
        cols = slice(c * columns, (c + 1) * columns)
        out[:, cols] = (
            tokens[:, cols].astype(F32)
            + z_in[c].astype(F32)
            + jnp.dot(total, downs_out[:, cols], preferred_element_type=F32)
        ).astype(BF16)

    for copy in map_copies:
        copy.wait_send()
    for stage in range(bits):
        gather_copy(stage).wait_send()
    for slot in range(n_mlp):
        for way in (0, 1):
            for step in range(1, n_req):
                ok, make = hop(way, step, slot)

                @pl.when(ok)
                def _():
                    make().wait_send()

    for slot in range(1, n_mlp):
        rank_copy(slot).wait_send()
        part_copy(slot).wait_send()
    for step in range(1, n_req):
        exchange(step).wait_send()


def pair_kernel(
    n_req,
    n_mlp,
    tokens_hbm,
    scale,
    names,
    gate_hbm,
    up_hbm,
    down_hbm,
    maps_hbm,
    ups_hbm,
    ins_hbm,
    outs_hbm,
    out,
    far,
    w_gate,
    w_up,
    w_down,
    ups,
    downs_in,
    x_own,
    hid,
    hid_near,
    part,
    core_in,
    one_in,
    two_in,
    z_out,
    z_in,
    pick,
    gate_low,
    up_low,
    rank_in,
    ranks,
    term,
    term_in,
    tail_out,
    w_sem,
    l_sem,
    s_sem,
    r_sem,
):
    r = lax.axis_index("req")
    m = lax.axis_index("mlp")
    rows, dim = tokens_hbm.shape
    hidden = gate_hbm.shape[1]
    columns = down_hbm.shape[1]
    span = maps_hbm.shape[0]
    half = span // 2
    lanes = pick.shape[0]
    chips = n_mlp // 2
    size = chips * rows
    piece = rows // 2
    tile = tile_of(hidden)
    tiles = hidden // tile
    narrow = tile_of(columns)
    early, late = 2, tiles - 2
    c = m % 2
    q = m // 2

    def flip(index, bit):
        power = 1 << bit
        return index + power * (1 - 2 * ((index // power) % 2))

    def apart(index, bits):
        for bit in range(3):
            if (bits >> bit) & 1:
                index = flip(index, bit)
        return index

    qx, qy, qd = flip(q, 0), flip(q, 1), apart(q, 3)
    first = qx * (1 - c) + qy * c
    second = qy * (1 - c) + qx * c
    near = flip(r, 0)
    across = n_req - 1 - r
    skip = flip(r, 1)
    inner = (r == 1) | (r == 2)
    outer = (r == 0) | (r == 3)
    kind = 1 - (r + r // 2) % 2

    hid_own, hid_far = hid.at[0], hid.at[1]
    rank_sum = ranks.at[0]

    ids = {}

    def sid(*key):
        return ids.setdefault(key, len(ids))

    far_base = [sid("rt", i) for i in range(4)][0]
    z_base = [sid("zr", i) for i in range(n_req)][0]
    half_base = [sid("zt", i) for i in range(2 * n_req)][0]

    def remote(src, dst, send, recv, device):
        return pltpu.make_async_remote_copy(
            src_ref=src,
            dst_ref=dst,
            send_sem=s_sem.at[send],
            recv_sem=r_sem.at[recv],
            device_id=device,
            device_id_type=MESH,
        )

    def on(k, fn):
        pl.when(c == k)(fn)

    def at_rows(block, offset=0, count=None):
        return pl.ds(pl.multiple_of(block * rows + offset, piece), count or rows)

    def plane(s, k):
        return x_own.at[k] if s == 0 else far.at[s - 1, k]

    quarter = dim // 4
    tok_copies = [
        pltpu.make_async_copy(
            tokens_hbm.at[:, pl.ds(i * quarter, quarter)],
            part.at[0, 0, pl.ds(i * rows, rows), :],
            l_sem.at[41 + i],
        )
        for i in range(4)
    ]
    ups_copy = pltpu.make_async_copy(ups_hbm, ups, l_sem.at[1])
    ins_copy = pltpu.make_async_copy(ins_hbm, downs_in, l_sem.at[2])
    down_copy = pltpu.make_async_copy(down_hbm, w_down, l_sem.at[3])
    outs_at = x_own.at[0, pl.ds(0, lanes), pl.ds(0, dim)]
    outs_copy = pltpu.make_async_copy(outs_hbm, outs_at, l_sem.at[4])
    tokens = x_own.at[0, pl.ds(lanes, rows), pl.ds(0, dim)]
    tok_again = pltpu.make_async_copy(tokens_hbm, tokens, l_sem.at[0])
    def maps_ref(i):
        return part.at[1, i // 2, pl.ds((i % 2) * lanes, lanes), :]

    map_copies = [
        pltpu.make_async_copy(
            maps_hbm.at[:, pl.ds(i * quarter, quarter)],
            part.at[1, i // 2, pl.ds((i % 2) * lanes + e * span, span), :],
            l_sem.at[9 + i * 4 + e],
        )
        for i in range(4)
        for e in range(4)
    ]

    def load(s, k, i):
        at = at_rows((q, qx, qy, qd)[i])
        return pltpu.make_async_copy(
            far.at[s - 1, k, at, :],
            x_own.at[k, at, :],
            l_sem.at[25 + ((s - 1) * 2 + k) * 4 + i],
        )

    def take_most(s, k):
        for i in range(3):
            load(s, k, i).start()

    def take_rest(s, k):
        load(s, k, 3).start()

    def loaded(s, k):
        for i in range(4):
            load(s, k, i).wait()

    def weight_copies(t):
        at = pl.ds(pl.multiple_of(t * tile, tile), tile)
        return (
            pltpu.make_async_copy(gate_hbm.at[:, at], w_gate.at[:, at], w_sem.at[0, t]),
            pltpu.make_async_copy(up_hbm.at[:, at], w_up.at[:, at], w_sem.at[1, t]),
        )

    for copy in tok_copies:
        copy.start()
    barrier = pltpu.get_barrier_semaphore()
    for d in range(1, n_mlp):
        pl.semaphore_signal(barrier, inc=1, device_id=(r, apart(m, d)), device_id_type=MESH)
    for d in range(1, n_req):
        pl.semaphore_signal(barrier, inc=1, device_id=(apart(r, d), m), device_id_type=MESH)
    for d in (2, 3):
        device = (apart(r, d), flip(m, 0))
        pl.semaphore_signal(barrier, inc=1, device_id=device, device_id_type=MESH)
    for copy in map_copies:
        copy.start()
    ups_copy.start()
    for t in range(tiles):
        for copy in weight_copies(t):
            copy.start()
    ins_copy.start()
    down_copy.start()

    for b in range(2 * chips):
        inside = lax.broadcasted_iota(jnp.int32, (lanes, lanes), 1)
        row = lax.broadcasted_iota(jnp.int32, (lanes, lanes), 0)
        source = (b // 2) * span + half * (b % 2) + inside % half
        pick[:, b * lanes : (b + 1) * lanes] = jnp.where(row == source, 1.0, 0.0).astype(BF16)

    for copy in tok_copies:
        copy.wait()
    eye = lax.broadcasted_iota(jnp.int32, (rows, rows), 0) == lax.broadcasted_iota(
        jnp.int32, (rows, rows), 1
    )
    spread_names = jnp.broadcast_to(names[...].astype(F32), (rows, rows))
    name_column = jnp.sum(jnp.where(eye, spread_names, 0.0), axis=1, keepdims=True)
    x_own[c, at_rows(q), dim : dim + 128] = jnp.broadcast_to(name_column, (rows, 128)).astype(BF16)

    def norm_step(i, carry):
        to = pl.ds(pl.multiple_of(q * rows + i * 16, 16), 16)
        wide = [
            part[0, 0, pl.ds(pl.multiple_of(e * rows + i * 16, 16), 16), :].astype(F32)
            for e in range(4)
        ]
        square = sum(jnp.sum(one * one, axis=-1, keepdims=True) for one in wide)
        gain = lax.rsqrt(square / dim + EPS)
        for e in range(4):
            cols = slice(e * quarter, (e + 1) * quarter)
            x_own[c, to, cols] = (wide[e] * gain * scale[:, cols]).astype(BF16)
        return carry

    lax.fori_loop(0, rows // 16, norm_step, 0)
    pl.semaphore_wait(barrier, n_mlp - 1 + n_req - 1 + 2)

    def gather(s, k, name, landing=False):
        ref = plane(s, k)
        other = (r, q * 2 + 1 - k)
        to_x, to_y = (r, qx * 2 + k), (r, qy * 2 + k)
        at, device, lands = {
            "n1a": (at_rows(q, 0, piece), to_x, at_rows(qx, 0, piece)),
            "n1b": (at_rows(q, piece, piece), to_x, at_rows(qx, piece, piece)),
            "n2a": (at_rows(q, 0, piece), to_y, at_rows(qy, 0, piece)),
            "n2b": (at_rows(q, piece, piece), to_y, at_rows(qy, piece, piece)),
            "f1": (at_rows(qx, 0, piece), to_y, at_rows(qd, 0, piece)),
            "f2": (at_rows(qy, piece, piece), to_x, at_rows(qd, piece, piece)),
            "c0": (at_rows(q), other, at_rows(q)),
            "c1": (at_rows(qx), other, at_rows(qx)),
            "c2": (at_rows(qy), other, at_rows(qy)),
            "c3": (at_rows(qd), other, at_rows(qd)),
        }[name]
        i = sid("g", s, k, name)
        if landing:
            return remote(ref.at[lands, :], ref.at[lands, :], i, i, device)
        return remote(ref.at[at, :], ref.at[at, :], i, i, device)

    names_of_gather = ("n1a", "n2b", "n1b", "n2a", "c0", "f1", "f2", "c1", "c2", "c3")

    def z_wait(w, p):
        at = at_rows(q, p * piece, piece)
        i = sid("z", w, p)
        remote(far.at[w, c, at, :], far.at[w, c, at, :], i, i, (near, m)).wait_recv()

    def lead_start(s, k):
        if s > 0:

            @pl.when(outer)
            def _():
                for p in range(2):
                    z_wait(s - 1, p)

        for name in names_of_gather[:5]:
            gather(s, k, name).start()

    def lead_forward(s, k):
        gather(s, k, "n1a", True).wait_recv()
        gather(s, k, "f1").start()
        gather(s, k, "n2b", True).wait_recv()
        gather(s, k, "f2").start()

    def lead_share(s, k):
        gather(s, k, "n1b", True).wait_recv()
        gather(s, k, "c1").start()
        gather(s, k, "n2a", True).wait_recv()
        gather(s, k, "c2").start()
        if s > 0:
            take_most(s, k)

    def lead_finish(s, k):
        gather(s, k, "f1", True).wait_recv()
        gather(s, k, "f2", True).wait_recv()
        gather(s, k, "c3").start()
        if s > 0:
            take_rest(s, k)

    def follow_most(s, k):
        for name in ("c0", "c1", "c2"):
            gather(s, k, name, True).wait_recv()
        if s > 0:
            take_most(s, k)

    def follow_rest(s, k):
        gather(s, k, "c3", True).wait_recv()
        if s > 0:
            take_rest(s, k)

    def z_own(p, in_inner):
        at = at_rows(q, p * piece, piece)
        w = 0 if in_inner else 1
        target = across if in_inner else skip
        return remote(
            x_own.at[c, at, :], far.at[w, c, at, :], sid("zs", p), sid("z", w, p), (target, m)
        )

    def z_next(w, p):
        at = at_rows(q, p * piece, piece)
        return remote(
            far.at[w, c, at, :], far.at[w, c, at, :], sid("zf", w, p), sid("z", w, p), (near, m)
        )

    def z_forward(w, p):
        @pl.when(inner)
        def _():
            z_wait(w, p)
            z_next(w, p).start()

    def z_send(in_inner):
        @pl.when(inner if in_inner else outer)
        def _():
            for p in range(2):
                z_own(p, in_inner).start()

    def rank_copy(k, d):
        i = sid("rx", k, d)
        return remote(rank_in.at[k, 0], rank_in.at[k, d], i, i, (r, apart(m, d)))

    def project(k):
        total = jnp.zeros((size, lanes), F32)
        for i in range(4):
            total = total + lax.dot_general(
                x_own[k, :, i * quarter : (i + 1) * quarter],
                maps_ref(i)[...],
                (((1,), (1,)), ((), ())),
                preferred_element_type=F32,
            )
        adapter = x_own[k, :, dim : dim + 128].astype(F32)
        at_lane = lax.broadcasted_iota(jnp.int32, (rows, lanes), 1) // span
        packed = jnp.zeros((rows, lanes), F32)
        for b in range(chips):
            low = slice(b * rows, (b + 1) * rows)
            mine = (at_lane == b) & (adapter[low] == m.astype(F32))
            packed = packed + jnp.where(mine, total[low], 0.0)
        rank_in[k, 0] = packed.astype(BF16)
        for d in range(1, n_mlp):
            rank_copy(k, d).start()

    def far_rank_copy(k, e):
        target = across if e == 0 else skip
        return remote(
            rank_sum.at[k],
            ranks.at[1 + kind, k],
            sid("rts", k, e),
            far_base + kind * 2 + k,
            (target, m),
        )

    def sum_ranks(k):
        total = rank_in[k, 0].astype(F32)
        for d in range(1, n_mlp):
            rank_copy(k, d).wait_recv()
            total = total + rank_in[k, d].astype(F32)
        rank_sum[k] = total.astype(BF16)
        for e in range(2):
            far_rank_copy(k, e).start()

    def wait_far_ranks(w, k):
        i = far_base + w * 2 + k
        remote(rank_sum.at[k], ranks.at[1 + w, k], i, i, (across, m)).wait_recv()

    def spread(g, k):
        adapter = x_own[k, :, dim : dim + 128].astype(F32)
        at_lane = lax.broadcasted_iota(jnp.int32, (rows, lanes), 1) // half
        for b in range(chips):
            low = slice(b * rows, (b + 1) * rows)
            mine = adapter[low] == at_lane.astype(F32)
            start = 2 * b * lanes
            values = jnp.dot(
                ranks[g, k], pick[:, start : start + 2 * lanes], preferred_element_type=F32
            )
            gate_low[low, :] = jnp.where(mine, values[:, 0:lanes], 0.0).astype(BF16)
            up_low[low, :] = jnp.where(mine, values[:, lanes:], 0.0).astype(BF16)

    def wide_sums(k, cols):
        return (
            jnp.dot(x_own[k, :, 0:dim], w_gate[:, cols], preferred_element_type=F32),
            jnp.dot(x_own[k, :, 0:dim], w_up[:, cols], preferred_element_type=F32),
        )

    def finish_tile(g, k, cols, sums):
        gate_sum = sums[0] + jnp.dot(gate_low[...], ups[0, :, cols], preferred_element_type=F32)
        up_sum = sums[1] + jnp.dot(up_low[...], ups[1, :, cols], preferred_element_type=F32)
        hid[g, k, :, cols] = (gate_sum / (1.0 + jnp.exp(-gate_sum)) * up_sum).astype(BF16)

    def need_weights(low, high):
        for t in range(low, high):
            for copy in weight_copies(t):
                copy.wait()

    def segment(g, k, low, high):
        for t in range(low, high):
            cols = slice(t * tile, (t + 1) * tile)
            finish_tile(g, k, cols, wide_sums(k, cols))

    def near_copy(k):
        i = sid("h", k)
        return remote(hid_own.at[k], hid_near.at[k], i, i, (near, m))

    def term_copy(k, slot):
        i = sid("k", slot)
        target = apart(q, slot // 2)
        return remote(
            term.at[k, at_rows(target), :], term_in.at[slot], i, i, (r, target * 2 + k)
        )

    def terms(k):
        values = lax.dot_general(
            hid_own[k], downs_in[...], (((1,), (1,)), ((), ())), preferred_element_type=F32
        )
        adapter = x_own[k, :, dim : dim + 128].astype(F32)
        at_lane = lax.broadcasted_iota(jnp.int32, values.shape, 1) // half
        term[k] = jnp.where(adapter == at_lane.astype(F32), values, 0.0).astype(BF16)

        def same():
            term_in[0] = term[k, at_rows(q), :]
            for e in range(1, chips):
                term_copy(k, 2 * e).start()

        def other():
            for e in range(chips):
                term_copy(k, 2 * e + 1).start()

        on(k, same)
        on(1 - k, other)

    def down_near(b):
        for k in range(2):
            for t in range(columns // narrow):
                cols = slice(t * narrow, (t + 1) * narrow)
                value = jnp.dot(hid_near[k], w_down[:, cols], preferred_element_type=F32)
                part[b, k, :, cols] = value.astype(BF16)

    def down_chunk(b, g, k):
        for t in range(columns // narrow):
            cols = slice(t * narrow, (t + 1) * narrow)
            value = jnp.dot(hid[g, k], w_down[:, cols], preferred_element_type=F32)
            part[b, k, :, cols] = value.astype(BF16)

    def core_copy(j):
        i = sid("rc", j)
        return remote(part.at[j % 2, 1 - c], core_in.at[j], i, i, (r, q * 2 + 1 - c))

    def one_copy(j, e):
        i = sid("r1", j, e)
        at = at_rows(first) if e == 0 else at_rows(qd)
        return remote(part.at[j % 2, c, at, :], one_in.at[j, e], i, i, (r, first * 2 + c))

    def two_copy(j):
        i = sid("r2", j)
        return remote(
            part.at[j % 2, c, at_rows(second), :], two_in.at[j], i, i, (r, second * 2 + c)
        )

    def home(j):
        if j == 2:
            return near
        return 2 - r // 2 if j == 1 else 3 * (1 - r // 2)

    def z_copy(j):
        return remote(z_out.at[j - 1], z_in.at[r], sid("zo", j), z_base + r, (home(j), m))

    def sum_cores(j):
        core_copy(j).wait_recv()
        b = j % 2

        def add(e, carry):
            at = pl.ds(pl.multiple_of(e * 16, 16), 16)
            value = part[b, c, at, :].astype(F32) + core_in[j, at, :].astype(F32)
            part[b, c, at, :] = value.astype(BF16)
            return carry

        lax.fori_loop(0, size // 16, add, 0)
        for e in range(2):
            one_copy(j, e).start()

    def sum_first(j):
        one_copy(j, 1).wait_recv()
        b, at = j % 2, at_rows(second)
        part[b, c, at, :] = (part[b, c, at, :].astype(F32) + one_in[j, 1].astype(F32)).astype(BF16)
        two_copy(j).start()

    def sum_second(j):
        one_copy(j, 0).wait_recv()
        two_copy(j).wait_recv()
        value = (
            part[j % 2, c, at_rows(q), :].astype(F32)
            + one_in[j, 0].astype(F32)
            + two_in[j].astype(F32)
        ).astype(BF16)
        if j == 0:
            z_in[r] = value
        else:
            z_out[j - 1] = value
            z_copy(j).start()

    low_half = pl.ds(0, columns // 2)
    tail_in = core_in.at[0, :, low_half]
    tail_one = one_in.at[0, :, :, low_half]
    tail_two = two_in.at[0, :, low_half]

    def half_at(h):
        return pl.ds(pl.multiple_of(h * (columns // 2), columns // 2), columns // 2)

    def tail_down(h):
        value = jnp.dot(hid_far[1], w_down[:, half_at(h)], preferred_element_type=F32)
        part[1, 1, :, half_at(h)] = value.astype(BF16)

    def tail_swap():
        i = sid("tc")
        return remote(part.at[1, 1, :, half_at(1 - c)], tail_in, i, i, (r, q * 2 + 1 - c))

    def tail_one_copy(e):
        i = sid("t1", e)
        at = at_rows(first) if e == 0 else at_rows(qd)
        return remote(part.at[1, 1, at, half_at(c)], tail_one.at[e], i, i, (r, first * 2 + c))

    def tail_two_copy():
        i = sid("t2")
        at = at_rows(second)
        return remote(part.at[1, 1, at, half_at(c)], tail_two, i, i, (r, second * 2 + c))

    def tail_z_copy():
        return remote(
            tail_out,
            z_in.at[r, :, half_at(c)],
            sid("tz"),
            half_base + c * n_req + r,
            (home(3), q * 2 + 1),
        )

    def tail_cores():
        tail_swap().wait_recv()
        at = half_at(c)
        part[1, 1, :, at] = (part[1, 1, :, at].astype(F32) + tail_in[...].astype(F32)).astype(BF16)
        for e in range(2):
            tail_one_copy(e).start()

    def tail_first():
        tail_one_copy(1).wait_recv()
        rows_at, at = at_rows(second), half_at(c)
        part[1, 1, rows_at, at] = (
            part[1, 1, rows_at, at].astype(F32) + tail_one[1].astype(F32)
        ).astype(BF16)
        tail_two_copy().start()

    def tail_second():
        tail_one_copy(0).wait_recv()
        tail_two_copy().wait_recv()
        tail_out[...] = (
            part[1, 1, at_rows(q), half_at(c)].astype(F32)
            + tail_one[0].astype(F32)
            + tail_two[...].astype(F32)
        ).astype(BF16)
        tail_z_copy().start()

    def sum_terms():
        total = term_in[0].astype(F32)
        for slot in range(1, n_mlp):
            term_copy(0, slot).wait_recv()
            total = total + term_in[slot].astype(F32)
        term_in[0] = total.astype(BF16)
        outs_copy.wait()
        tok_again.wait()

    def z_arrival(step):
        source = apart(r, step)
        whole = z_in.at[source]

        def wait_whole():
            i = z_base + source
            remote(whole, whole, i, i, (source, m)).wait_recv()

        def wait_halves():
            for h in range(2):
                i = half_base + h * n_req + source
                part_of = z_in.at[source, :, half_at(h)]
                remote(part_of, part_of, i, i, (source, m)).wait_recv()

        if step == 1:
            wait_whole()
        else:
            pl.when(outer & (c == 1))(wait_halves)
            pl.when(inner | (c == 0))(wait_whole)

    def part_free(j):
        core_copy(j).wait_send()
        for e in range(2):
            one_copy(j, e).wait_send()
        two_copy(j).wait_send()

    def own_free(k):
        def fn():
            for name in names_of_gather:
                gather(0, k, name).wait_send()
            for p in range(2):

                @pl.when(inner)
                def _(p=p):
                    z_own(p, True).wait_send()

                @pl.when(outer)
                def _(p=p):
                    z_own(p, False).wait_send()

        on(k, fn)

    def tick(fn, *args):
        return lambda: fn(*args)

    def tick_on(core, fn, *args):
        return lambda: on(core, lambda: fn(*args))

    def lead_first():
        lead_start(0, 0)
        lead_forward(0, 0)
        z_send(True)
        lead_share(0, 0)
        lead_finish(0, 0)

    def follow_first():
        z_send(True)
        follow_most(0, 0)
        follow_rest(0, 0)

    on(0, lead_first)
    on(1, follow_first)
    for copy in map_copies:
        copy.wait()
    project(0)
    tick_on(1, lead_start, 0, 1)()
    z_send(False)
    z_forward(0, 0)
    ups_copy.wait()
    z_forward(0, 1)
    sum_ranks(0)
    need_weights(0, early)

    events = {
        0: (
            [],
            [tick(need_weights, early, late)],
            [
                tick(need_weights, late, tiles),
                tick_on(1, lead_forward, 0, 1),
                tick_on(1, lead_share, 0, 1),
            ],
            [
                ins_copy.wait,
                tick(terms, 0),
                tick_on(1, lead_finish, 0, 1),
                tick_on(0, follow_most, 0, 1),
                tick_on(0, follow_rest, 0, 1),
                tick(project, 1),
                tick_on(0, lead_start, 1, 0),
                down_copy.wait,
            ],
            [tick(sum_ranks, 1)],
        ),
        1: (
            [tick(z_forward, 1, 0), tick(z_forward, 1, 1)],
            [tick_on(0, lead_forward, 1, 0)],
            [
                tick(own_free, 0),
                tick_on(0, lead_share, 1, 0),
                tick_on(1, lead_start, 1, 1),
                lambda: near_copy(0).start(),
            ],
            [
                tick_on(1, follow_most, 1, 0),
                tick_on(0, lead_finish, 1, 0),
                lambda: near_copy(1).start(),
                tick(terms, 1),
            ],
            [
                lambda: core_copy(0).start(),
                tick_on(1, follow_rest, 1, 0),
                tick(wait_far_ranks, 0, 0),
                tick(loaded, 1, 0),
            ],
        ),
        2: (
            [tick(own_free, 1), tick_on(1, lead_forward, 1, 1)],
            [tick_on(1, lead_share, 1, 1), tick(sum_cores, 0)],
            [
                tick_on(1, lead_finish, 1, 1),
                tick_on(0, follow_most, 1, 1),
                tick_on(0, lead_start, 2, 0),
            ],
            [tick_on(0, follow_rest, 1, 1), tick(sum_first, 0)],
            [tick(wait_far_ranks, 0, 1), tick(loaded, 1, 1)],
        ),
        3: (
            [],
            [tick_on(0, lead_forward, 2, 0), tick_on(0, lead_share, 2, 0)],
            [
                tick(sum_second, 0),
                tick_on(1, follow_most, 2, 0),
                tick_on(1, lead_start, 2, 1),
            ],
            [tick_on(0, lead_finish, 2, 0)],
            [
                lambda: core_copy(1).start(),
                tick_on(1, follow_rest, 2, 0),
                tick(wait_far_ranks, 1, 0),
                tick(loaded, 2, 0),
            ],
        ),
        4: (
            [],
            [
                tick(sum_cores, 1),
                tick_on(1, lead_forward, 2, 1),
                tick_on(1, lead_share, 2, 1),
            ],
            [tick_on(0, follow_most, 2, 1)],
            [
                tick(sum_first, 1),
                tick_on(1, lead_finish, 2, 1),
                outs_copy.start,
                tok_again.start,
                tick(part_free, 0),
                lambda: near_copy(0).wait_recv(),
                lambda: near_copy(1).wait_recv(),
                tick(down_near, 0),
                lambda: core_copy(2).start(),
                tick_on(0, follow_rest, 2, 1),
                tick(sum_second, 1),
                tick(part_free, 1),
            ],
            [
                tick_on(1, lambda: core_copy(3).start()),
                tick(wait_far_ranks, 1, 1),
                tick(loaded, 2, 1),
            ],
        ),
        5: (
            [],
            [tick(sum_cores, 2)],
            [tick(sum_first, 2), tick_on(0, sum_cores, 3)],
            [],
            [],
        ),
    }
    chunks = len(events)

    def chunk_step(i, carry):
        k, group = i % 2, i // 2
        g = (group + 1) // 2

        def happen(place):
            for number in range(chunks):
                if events[number][place]:

                    @pl.when(i == number)
                    def _(number=number):
                        for fn in events[number][place]:
                            fn()

        happen(0)

        spread(group, k)
        segment(g, k, 0, early)
        happen(1)
        segment(g, k, early, late)
        happen(2)
        segment(g, k, late, tiles)
        happen(3)

        @pl.when(i < chunks - 1)
        def _():
            down_chunk(g, g, k)

        happen(4)
        return carry

    lax.fori_loop(0, chunks, chunk_step, 0)
    tail_down(1 - c)
    tail_swap().start()
    tail_down(c)
    tail_cores()
    sum_second(2)
    tick_on(0, sum_first, 3)()
    sum_terms()
    tail_first()
    tick_on(0, sum_second, 3)()
    tail_second()

    def gather_sent(s, k):
        for name in names_of_gather:
            gather(s, k, name).wait_send()

    def terms_sent(k, slots):
        for slot in slots:
            term_copy(k, slot).wait_send()

    for s in (1, 2):
        for k in range(2):
            tick_on(k, gather_sent, s, k)()

    @pl.when(inner)
    def _():
        for w in range(2):
            for p in range(2):
                z_next(w, p).wait_send()

    for k in range(2):
        for d in range(1, n_mlp):
            rank_copy(k, d).wait_send()
        for e in range(2):
            far_rank_copy(k, e).wait_send()
        near_copy(k).wait_send()
        tick_on(k, terms_sent, k, range(2, n_mlp, 2))()
        tick_on(1 - k, terms_sent, k, range(1, n_mlp, 2))()
    part_free(2)
    on(1, lambda: core_copy(3).wait_send())

    def last_sent():
        for e in range(2):
            one_copy(3, e).wait_send()
        two_copy(3).wait_send()
        z_copy(3).wait_send()

    on(0, last_sent)
    z_copy(1).wait_send()
    z_copy(2).wait_send()
    def finish(b):
        cols = pl.ds(pl.multiple_of(b * columns, columns), columns)
        out[:, cols] = (
            tokens[:, cols].astype(F32)
            + z_in[b].astype(F32)
            + jnp.dot(term_in[0], outs_at[:, cols], preferred_element_type=F32)
        ).astype(BF16)

    finish(r)
    for step in range(1, n_req):
        z_arrival(step)
        finish(apart(r, step))
    tail_swap().wait_send()
    for e in range(2):
        tail_one_copy(e).wait_send()
    tail_two_copy().wait_send()
    tail_z_copy().wait_send()
    assert len(ids) <= s_sem.shape[0], len(ids)


def pair_call(
    tokens,
    norm_scale,
    gate_matrix,
    up_matrix,
    down_matrix,
    adapter_down_maps,
    adapter_gate_up_out,
    adapter_down_proj_in,
    adapter_down_proj_out,
    token_adapters,
):
    n_req, n_mlp = lax.axis_size("req"), lax.axis_size("mlp")
    rows, dim = tokens.shape
    hidden = gate_matrix.shape[1]
    columns = down_matrix.shape[1]
    lanes = adapter_down_proj_in.shape[0]
    chips = n_mlp // 2
    size = chips * rows
    vmem = pl.BlockSpec(memory_space=pltpu.VMEM)
    hbm = pl.BlockSpec(memory_space=pltpu.HBM)
    dma = pltpu.SemaphoreType.DMA
    out, _ = pl.pallas_call(
        functools.partial(pair_kernel, n_req, n_mlp),
        out_shape=(
            jax.ShapeDtypeStruct((rows, dim), BF16),
            jax.ShapeDtypeStruct((2, 2, size, dim + 128), BF16),
        ),
        in_specs=[hbm, vmem, vmem, hbm, hbm, hbm, hbm, hbm, hbm, hbm],
        out_specs=(vmem, hbm),
        scratch_shapes=[
            pltpu.VMEM((dim, hidden), BF16),
            pltpu.VMEM((dim, hidden), BF16),
            pltpu.VMEM((hidden, columns), BF16),
            pltpu.VMEM((2, lanes, hidden), BF16),
            pltpu.VMEM((lanes, hidden), BF16),
            pltpu.VMEM((2, size, dim + 128), BF16),
            pltpu.VMEM((2, 2, size, hidden), BF16),
            pltpu.VMEM((2, size, hidden), BF16),
            pltpu.VMEM((2, 2, size, columns), BF16),
            pltpu.VMEM((4, size, columns), BF16),
            pltpu.VMEM((4, 2, rows, columns), BF16),
            pltpu.VMEM((4, rows, columns), BF16),
            pltpu.VMEM((3, rows, columns), BF16),
            pltpu.VMEM((n_req, rows, columns), BF16),
            pltpu.VMEM((lanes, 2 * chips * lanes), BF16),
            pltpu.VMEM((size, lanes), BF16),
            pltpu.VMEM((size, lanes), BF16),
            pltpu.VMEM((2, n_mlp, rows, lanes), BF16),
            pltpu.VMEM((3, 2, rows, lanes), BF16),
            pltpu.VMEM((2, size, lanes), BF16),
            pltpu.VMEM((n_mlp, rows, lanes), BF16),
            pltpu.VMEM((rows, columns // 2), BF16),
            dma((2, hidden // tile_of(hidden))),
            dma((45,)),
            dma((144,)),
            dma((144,)),
        ],
        compiler_params=pltpu.CompilerParams(
            collective_id=0, has_side_effects=True, vmem_limit_bytes=67043328
        ),
    )(
        tokens,
        norm_scale.reshape(1, dim),
        token_adapters.reshape(1, rows),
        gate_matrix,
        up_matrix,
        down_matrix,
        adapter_down_maps[0],
        adapter_gate_up_out,
        adapter_down_proj_in,
        adapter_down_proj_out,
    )
    return out


def block_call(
    tokens,
    norm_scale,
    gate_matrix,
    up_matrix,
    down_matrix,
    adapter_down_maps,
    adapter_gate_up_out,
    adapter_down_proj_in,
    adapter_down_proj_out,
    token_adapters,
):
    n_req, n_mlp = lax.axis_size("req"), lax.axis_size("mlp")
    rows, dim = tokens.shape
    hidden = gate_matrix.shape[1]
    columns = down_matrix.shape[1]
    span = adapter_down_maps.shape[1]
    half = span // 2
    ranks = adapter_down_proj_in.shape[0]
    bits = n_mlp.bit_length() - 1
    group = n_req * rows
    ups = adapter_gate_up_out.reshape(2, n_mlp, half, hidden)
    ups = ups.transpose(1, 0, 2, 3).reshape(n_mlp * span, hidden)
    vmem = pl.BlockSpec(memory_space=pltpu.VMEM)
    hbm = pl.BlockSpec(memory_space=pltpu.HBM)
    dma = pltpu.SemaphoreType.DMA
    out, _ = pl.pallas_call(
        functools.partial(block_kernel, n_req, n_mlp),
        out_shape=(
            jax.ShapeDtypeStruct((rows, dim), BF16),
            jax.ShapeDtypeStruct((n_mlp, group, columns), BF16),
        ),
        in_specs=[vmem, vmem, vmem, hbm, hbm, hbm, vmem, vmem, vmem, vmem],
        out_specs=(vmem, hbm),
        scratch_shapes=[
            pltpu.VMEM((n_mlp * rows, dim + 128), BF16),
            pltpu.VMEM((n_mlp * span, dim), BF16),
            pltpu.VMEM((dim, hidden), BF16),
            pltpu.VMEM((dim, hidden), BF16),
            pltpu.VMEM((hidden, columns), BF16),
            pltpu.VMEM((n_req, n_mlp * rows, hidden), BF16),
            pltpu.VMEM((group, columns), F32),
            pltpu.VMEM((group, columns), BF16),
            pltpu.VMEM((n_req, rows, columns), BF16),
            pltpu.VMEM((n_mlp, rows, ranks), BF16),
            pltpu.VMEM((n_mlp, rows, ranks), BF16),
            dma((2, hidden // tile_of(hidden))),
            dma,
            dma,
            dma((n_mlp,)),
            dma((n_mlp,)),
            dma((bits,)),
            dma((bits,)),
            dma((2, n_req - 1, n_mlp)),
            dma((2, n_req - 1, n_mlp)),
            dma((n_mlp,)),
            dma((n_mlp,)),
            dma((n_mlp,)),
            dma((n_mlp,)),
            dma((n_req,)),
            dma((n_req,)),
        ],
        compiler_params=pltpu.CompilerParams(
            collective_id=0, has_side_effects=True, vmem_limit_bytes=67043328
        ),
    )(
        tokens,
        norm_scale.reshape(1, dim),
        token_adapters,
        gate_matrix,
        up_matrix,
        down_matrix,
        adapter_down_maps[0],
        ups,
        adapter_down_proj_in,
        adapter_down_proj_out,
    )
    return out


def solution(mesh):
    per_device = pair_call if (mesh.shape["req"], mesh.shape["mlp"]) == (4, 8) else block_call
    return jax.shard_map(
        per_device,
        mesh=mesh,
        in_specs=(
            P(("req", "mlp"), None),
            P(),
            P(None, "mlp"),
            P(None, "mlp"),
            P("mlp", "req"),
            P("mlp", None, None),
            P(None, None, "mlp"),
            P(None, "mlp"),
            P(),
            P(("req", "mlp"), None),
        ),
        out_specs=P(("req", "mlp"), None),
        check_vma=False,
    )
```

```python
import functools

import jax
import jax.numpy as jnp
from jax import lax
from jax.experimental import pallas as pl
from jax.experimental.pallas import tpu as pltpu
from jax.sharding import PartitionSpec as P

EPS = 1e-06
MESH = pl.DeviceIdType.MESH
F32 = jnp.float32
BF16 = jnp.bfloat16


def tile_of(width):
    return 256 if width % 256 == 0 else 128


def block_kernel(
    n_req,
    n_mlp,
    tokens,
    scale,
    names,
    gate_hbm,
    up_hbm,
    down_hbm,
    maps,
    ups,
    downs_in,
    downs_out,
    out,
    parts,
    x_all,
    a_all,
    w_gate,
    w_up,
    w_down,
    hid,
    acc,
    piece,
    z_in,
    rk_out,
    rk_in,
    w_sem,
    d_sem,
    c_sem,
    a_send,
    a_recv,
    x_send,
    x_recv,
    h_send,
    h_recv,
    p_send,
    p_recv,
    k_send,
    k_recv,
    e_send,
    e_recv,
):
    r = lax.axis_index("req")
    m = lax.axis_index("mlp")
    rows, dim = tokens.shape
    hidden = gate_hbm.shape[1]
    columns = down_hbm.shape[1]
    span = maps.shape[0]
    half = span // 2
    bits = n_mlp.bit_length() - 1
    tile = tile_of(hidden)
    tiles = hidden // tile
    group = n_req * rows

    def flip(index, bit):
        power = 1 << bit
        return index + power * (1 - 2 * ((index // power) % 2))

    def peer(slot):
        index = m
        for stage in range(bits):
            if (slot >> stage) & 1:
                index = flip(index, (stage + 1) % bits)
        return index

    def weight_copies(t):
        at = pl.ds(pl.multiple_of(t * tile, tile), tile)
        return (
            pltpu.make_async_copy(gate_hbm.at[:, at], w_gate.at[:, at], w_sem.at[0, t]),
            pltpu.make_async_copy(up_hbm.at[:, at], w_up.at[:, at], w_sem.at[1, t]),
        )

    for t in range(tiles):
        for copy in weight_copies(t):
            copy.start()
    down_copy = pltpu.make_async_copy(down_hbm, w_down, d_sem)
    down_copy.start()

    barrier = pltpu.get_barrier_semaphore()
    for slot in range(1, n_mlp):
        pl.semaphore_signal(barrier, inc=1, device_id=(r, peer(slot)), device_id_type=MESH)
    for step in range(1, n_req):
        pl.semaphore_signal(
            barrier, inc=1, device_id=((r + step) % n_req, m), device_id_type=MESH
        )
    pl.semaphore_wait(barrier, n_mlp - 1 + n_req - 1)

    def remote(src, dst, send, recv, device):
        return pltpu.make_async_remote_copy(
            src_ref=src,
            dst_ref=dst,
            send_sem=send,
            recv_sem=recv,
            device_id=device,
            device_id_type=MESH,
        )

    own_maps = pl.ds(pl.multiple_of(m * span, span), span)
    map_copies = [
        remote(maps, a_all.at[own_maps, :], a_send.at[s], a_recv.at[s], (r, peer(s)))
        for s in range(1, n_mlp)
    ]
    for copy in map_copies:
        copy.start()
    a_all[own_maps, :] = maps[...]

    def norm_step(i, carry):
        at = pl.ds(pl.multiple_of(i * 16, 16), 16)
        wide = tokens[at, :].astype(F32)
        mean_square = jnp.mean(wide * wide, axis=-1, keepdims=True)
        x_all[at, 0:dim] = (wide * lax.rsqrt(mean_square + EPS) * scale[...]).astype(BF16)
        x_all[at, dim : dim + 128] = jnp.broadcast_to(
            names[at, :].astype(F32), (16, 128)
        ).astype(BF16)
        return carry

    lax.fori_loop(0, rows // 16, norm_step, 0)

    def gather_copy(stage):
        size = rows << stage
        return remote(
            x_all.at[pl.ds(0, size), :],
            x_all.at[pl.ds(size, size), :],
            x_send.at[stage],
            x_recv.at[stage],
            (r, flip(m, (stage + 1) % bits)),
        )

    gather_copy(0).start()
    for copy in map_copies:
        copy.wait_recv()

    def hop(way, step, slot):
        at = pl.ds(slot * rows, rows)
        sign = 1 if way == 0 else -1
        block = r - sign * (step - 1)
        ok = (block >= 0) & (block <= n_req - 1) & (r + sign >= 0) & (r + sign <= n_req - 1)

        def make():
            return remote(
                hid.at[block, at, :],
                hid.at[block, at, :],
                h_send.at[way, step - 1, slot],
                h_recv.at[way, step - 1, slot],
                (r + sign, m),
            )

        return ok, make

    def hop_start(way, step, slot):
        ok, make = hop(way, step, slot)

        @pl.when(ok)
        def _():
            make().start()

    def hop_arrival(way, step, slot):
        at = pl.ds(slot * rows, rows)
        sign = 1 if way == 0 else -1
        block = r - sign * step

        @pl.when((block >= 0) & (block <= n_req - 1))
        def _():
            remote(
                hid.at[block, at, :],
                hid.at[block, at, :],
                h_send.at[way, step - 1, slot],
                h_recv.at[way, step - 1, slot],
                (r - sign, m),
            ).wait_recv()

    middle = n_mlp // 2
    order = [*range(middle), *range(middle + 1, n_mlp), middle]

    def tick(k):
        for step in range(n_req - 1, 0, -1):
            if 0 <= k - step < n_mlp:
                slot = order[k - step]
                for way in (0, 1):
                    hop_arrival(way, step, slot)
                    if step < n_req - 1:
                        hop_start(way, step + 1, slot)

    def rank_copy(slot):
        return remote(
            rk_out.at[slot], rk_in.at[slot], k_send.at[slot], k_recv.at[slot], (r, peer(slot))
        )

    def compute(first, count, wait, ticks):
        size = count * rows
        at = pl.ds(first * rows, size)
        normed = x_all[at, 0:dim]
        adapter = x_all[at, dim : dim + 128].astype(F32)[:, 0:1]
        ranks = lax.dot_general(
            normed, a_all[...], (((1,), (1,)), ((), ())), preferred_element_type=F32
        )
        lane = lax.broadcasted_iota(jnp.int32, ranks.shape, 1)
        mine = adapter == (lane // span).astype(F32)
        low = (lane // half) % 2 == 0
        gate_ranks = jnp.where(mine & low, ranks, 0.0).astype(BF16)
        up_ranks = jnp.where(mine & jnp.logical_not(low), ranks, 0.0).astype(BF16)

        def step(t, carry):
            if wait:
                for copy in weight_copies(t):
                    copy.wait()
            cols = pl.ds(pl.multiple_of(t * tile, tile), tile)
            table = ups[:, cols]
            gate_sum = jnp.dot(
                x_all[at, 0:dim], w_gate[:, cols], preferred_element_type=F32
            ) + jnp.dot(gate_ranks, table, preferred_element_type=F32)
            up_sum = jnp.dot(
                x_all[at, 0:dim], w_up[:, cols], preferred_element_type=F32
            ) + jnp.dot(up_ranks, table, preferred_element_type=F32)
            value = gate_sum / (1.0 + jnp.exp(-gate_sum)) * up_sum
            hid[r, at, cols] = value.astype(BF16)
            return carry

        reached = 0
        for i, k in enumerate(ticks):
            limit = tiles * (i + 1) // (len(ticks) + 1)
            lax.fori_loop(reached, limit, step, 0)
            reached = limit
            tick(k)
        lax.fori_loop(reached, tiles, step, 0)
        for slot in order[first : first + count]:
            hop_start(0, 1, slot)
            hop_start(1, 1, slot)
        terms = lax.dot_general(
            hid[r, at, :], downs_in[...], (((1,), (1,)), ((), ())), preferred_element_type=F32
        )
        lane = lax.broadcasted_iota(jnp.int32, terms.shape, 1)
        terms = jnp.where(adapter == (lane // half).astype(F32), terms, 0.0).astype(BF16)
        for slot in range(first, first + count):
            low_row = (slot - first) * rows
            term = terms[low_row : low_row + rows]
            if slot == 0:
                rk_in[0] = term
            else:
                rk_out[slot] = term
                rank_copy(slot).start()

    gather_copy(0).wait_recv()
    gather_copy(1).start()
    compute(0, 2, True, ())
    done = 0
    for stage in range(1, bits):
        gather_copy(stage).wait_recv()
        if stage + 1 < bits:
            gather_copy(stage + 1).start()
        compute(1 << stage, 1 << stage, False, (done + 1, done + 2))
        done = done + 2

    down_copy.wait()
    narrow = tile_of(columns)

    def staging(slot):
        low_row = slot * group
        if low_row + group <= dim:
            return w_gate.at[pl.ds(low_row, group), pl.ds(0, columns)]
        low_row = (slot - dim // group) * group
        return w_up.at[pl.ds(low_row, group), pl.ds(0, columns)]

    def part_copy(slot):
        return remote(
            staging(slot), parts.at[slot], p_send.at[slot], p_recv.at[slot], (r, peer(slot))
        )

    def down(slot):
        place = staging(slot)
        at = pl.ds(slot * rows, rows)

        def step(t, carry):
            cols = pl.ds(pl.multiple_of(t * narrow, narrow), narrow)
            left = hid[:, at, :].reshape(group, hidden)
            term = jnp.dot(left, w_down[:, cols], preferred_element_type=F32).astype(BF16)
            if slot == 0:
                acc[:, cols] = term.astype(F32)
            else:
                place[:, cols] = term
            return carry

        lax.fori_loop(0, columns // narrow, step, 0)
        if slot > 0:
            part_copy(slot).start()

    def collect(slot):
        part_copy(slot).wait_recv()
        copy = pltpu.make_async_copy(parts.at[slot], piece, c_sem)
        copy.start()
        copy.wait()
        acc[...] += piece[...].astype(F32)

    finished = 0
    for k in range(done, n_mlp + n_req - 1):
        if k > done:
            tick(k)
        while finished <= k - (n_req - 1) and finished < n_mlp:
            down(order[finished])
            if finished >= 3:
                collect(order[finished - 2])
            finished += 1
    for slot in order[n_mlp - 2 :]:
        collect(slot)

    piece[...] = acc[...].astype(BF16)

    def exchange(step):
        target = (r + step) % n_req
        return remote(
            piece.at[pl.ds(pl.multiple_of(target * rows, rows), rows), :],
            z_in.at[r],
            e_send.at[step],
            e_recv.at[step],
            (target, m),
        )

    for step in range(1, n_req):
        exchange(step).start()
    z_in[r] = piece[pl.ds(pl.multiple_of(r * rows, rows), rows), :]
    total = rk_in[0].astype(F32)
    for slot in range(1, n_mlp):
        rank_copy(slot).wait_recv()
        total = total + rk_in[slot].astype(F32)
    total = total.astype(BF16)
    for step in range(1, n_req):
        source = (r + n_req - step) % n_req
        remote(
            piece.at[pl.ds(0, rows), :],
            z_in.at[source],
            e_send.at[step],
            e_recv.at[step],
            (source, m),
        ).wait_recv()
    for c in range(n_req):
        cols = slice(c * columns, (c + 1) * columns)
        out[:, cols] = (
            tokens[:, cols].astype(F32)
            + z_in[c].astype(F32)
            + jnp.dot(total, downs_out[:, cols], preferred_element_type=F32)
        ).astype(BF16)

    for copy in map_copies:
        copy.wait_send()
    for stage in range(bits):
        gather_copy(stage).wait_send()
    for slot in range(n_mlp):
        for way in (0, 1):
            for step in range(1, n_req):
                ok, make = hop(way, step, slot)

                @pl.when(ok)
                def _():
                    make().wait_send()

    for slot in range(1, n_mlp):
        rank_copy(slot).wait_send()
        part_copy(slot).wait_send()
    for step in range(1, n_req):
        exchange(step).wait_send()


def pair_kernel(
    n_req,
    n_mlp,
    tokens_hbm,
    scale,
    names,
    gate_hbm,
    up_hbm,
    down_hbm,
    maps_hbm,
    ups_hbm,
    ins_hbm,
    outs_hbm,
    out,
    far,
    w_gate,
    w_up,
    w_down,
    ups,
    downs_in,
    x_own,
    hid,
    hid_near,
    part,
    core_in,
    one_in,
    two_in,
    z_out,
    z_in,
    pick,
    gate_low,
    up_low,
    rank_in,
    ranks,
    term,
    term_in,
    tail_out,
    w_sem,
    l_sem,
    s_sem,
    r_sem,
):
    r = lax.axis_index("req")
    m = lax.axis_index("mlp")
    rows, dim = tokens_hbm.shape
    hidden = gate_hbm.shape[1]
    columns = down_hbm.shape[1]
    span = maps_hbm.shape[0]
    half = span // 2
    lanes = pick.shape[0]
    chips = n_mlp // 2
    size = chips * rows
    piece = rows // 2
    tile = tile_of(hidden)
    tiles = hidden // tile
    narrow = tile_of(columns)
    early, late = 2, tiles - 2
    c = m % 2
    q = m // 2

    def flip(index, bit):
        power = 1 << bit
        return index + power * (1 - 2 * ((index // power) % 2))

    def apart(index, bits):
        for bit in range(3):
            if (bits >> bit) & 1:
                index = flip(index, bit)
        return index

    qx, qy, qd = flip(q, 0), flip(q, 1), apart(q, 3)
    first = qx * (1 - c) + qy * c
    second = qy * (1 - c) + qx * c
    near = flip(r, 0)
    across = n_req - 1 - r
    skip = flip(r, 1)
    inner = (r == 1) | (r == 2)
    outer = (r == 0) | (r == 3)
    kind = 1 - (r + r // 2) % 2

    hid_own, hid_far = hid.at[0], hid.at[1]
    rank_sum = ranks.at[0]

    ids = {}

    def sid(*key):
        return ids.setdefault(key, len(ids))

    far_base = [sid("rt", i) for i in range(4)][0]
    z_base = [sid("zr", i) for i in range(n_req)][0]
    half_base = [sid("zt", i) for i in range(2 * n_req)][0]

    def remote(src, dst, send, recv, device):
        return pltpu.make_async_remote_copy(
            src_ref=src,
            dst_ref=dst,
            send_sem=s_sem.at[send],
            recv_sem=r_sem.at[recv],
            device_id=device,
            device_id_type=MESH,
        )

    def on(k, fn):
        pl.when(c == k)(fn)

    def at_rows(block, offset=0, count=None):
        return pl.ds(pl.multiple_of(block * rows + offset, piece), count or rows)

    def plane(s, k):
        return x_own.at[k] if s == 0 else far.at[s - 1, k]

    quarter = dim // 4
    tok_copies = [
        pltpu.make_async_copy(
            tokens_hbm.at[:, pl.ds(i * quarter, quarter)],
            part.at[0, 0, pl.ds(i * rows, rows), :],
            l_sem.at[41 + i],
        )
        for i in range(4)
    ]
    ups_copy = pltpu.make_async_copy(ups_hbm, ups, l_sem.at[1])
    ins_copy = pltpu.make_async_copy(ins_hbm, downs_in, l_sem.at[2])
    down_copy = pltpu.make_async_copy(down_hbm, w_down, l_sem.at[3])
    outs_at = x_own.at[0, pl.ds(0, lanes), pl.ds(0, dim)]
    outs_copy = pltpu.make_async_copy(outs_hbm, outs_at, l_sem.at[4])
    tokens = x_own.at[0, pl.ds(lanes, rows), pl.ds(0, dim)]
    tok_again = pltpu.make_async_copy(tokens_hbm, tokens, l_sem.at[0])
    def maps_ref(i):
        return part.at[1, i // 2, pl.ds((i % 2) * lanes, lanes), :]

    map_copies = [
        pltpu.make_async_copy(
            maps_hbm.at[:, pl.ds(i * quarter, quarter)],
            part.at[1, i // 2, pl.ds((i % 2) * lanes + e * span, span), :],
            l_sem.at[9 + i * 4 + e],
        )
        for i in range(4)
        for e in range(4)
    ]

    def load(s, k, i):
        at = at_rows((q, qx, qy, qd)[i])
        return pltpu.make_async_copy(
            far.at[s - 1, k, at, :],
            x_own.at[k, at, :],
            l_sem.at[25 + ((s - 1) * 2 + k) * 4 + i],
        )

    def take_most(s, k):
        for i in range(3):
            load(s, k, i).start()

    def take_rest(s, k):
        load(s, k, 3).start()

    def loaded(s, k):
        for i in range(4):
            load(s, k, i).wait()

    def weight_copies(t):
        at = pl.ds(pl.multiple_of(t * tile, tile), tile)
        return (
            pltpu.make_async_copy(gate_hbm.at[:, at], w_gate.at[:, at], w_sem.at[0, t]),
            pltpu.make_async_copy(up_hbm.at[:, at], w_up.at[:, at], w_sem.at[1, t]),
        )

    for copy in tok_copies:
        copy.start()
    barrier = pltpu.get_barrier_semaphore()
    for d in range(1, n_mlp):
        pl.semaphore_signal(barrier, inc=1, device_id=(r, apart(m, d)), device_id_type=MESH)
    for d in range(1, n_req):
        pl.semaphore_signal(barrier, inc=1, device_id=(apart(r, d), m), device_id_type=MESH)
    for d in (2, 3):
        device = (apart(r, d), flip(m, 0))
        pl.semaphore_signal(barrier, inc=1, device_id=device, device_id_type=MESH)
    for copy in map_copies:
        copy.start()
    ups_copy.start()
    for t in range(tiles):
        for copy in weight_copies(t):
            copy.start()
    ins_copy.start()
    down_copy.start()

    for b in range(2 * chips):
        inside = lax.broadcasted_iota(jnp.int32, (lanes, lanes), 1)
        row = lax.broadcasted_iota(jnp.int32, (lanes, lanes), 0)
        source = (b // 2) * span + half * (b % 2) + inside % half
        pick[:, b * lanes : (b + 1) * lanes] = jnp.where(row == source, 1.0, 0.0).astype(BF16)

    for copy in tok_copies:
        copy.wait()
    eye = lax.broadcasted_iota(jnp.int32, (rows, rows), 0) == lax.broadcasted_iota(
        jnp.int32, (rows, rows), 1
    )
    spread_names = jnp.broadcast_to(names[...].astype(F32), (rows, rows))
    name_column = jnp.sum(jnp.where(eye, spread_names, 0.0), axis=1, keepdims=True)
    x_own[c, at_rows(q), dim : dim + 128] = jnp.broadcast_to(name_column, (rows, 128)).astype(BF16)

    def norm_step(i, carry):
        to = pl.ds(pl.multiple_of(q * rows + i * 16, 16), 16)
        wide = [
            part[0, 0, pl.ds(pl.multiple_of(e * rows + i * 16, 16), 16), :].astype(F32)
            for e in range(4)
        ]
        square = sum(jnp.sum(one * one, axis=-1, keepdims=True) for one in wide)
        gain = lax.rsqrt(square / dim + EPS)
        for e in range(4):
            cols = slice(e * quarter, (e + 1) * quarter)
            x_own[c, to, cols] = (wide[e] * gain * scale[:, cols]).astype(BF16)
        return carry

    lax.fori_loop(0, rows // 16, norm_step, 0)
    pl.semaphore_wait(barrier, n_mlp - 1 + n_req - 1 + 2)

    def gather(s, k, name, landing=False):
        ref = plane(s, k)
        other = (r, q * 2 + 1 - k)
        to_x, to_y = (r, qx * 2 + k), (r, qy * 2 + k)
        at, device, lands = {
            "n1a": (at_rows(q, 0, piece), to_x, at_rows(qx, 0, piece)),
            "n1b": (at_rows(q, piece, piece), to_x, at_rows(qx, piece, piece)),
            "n2a": (at_rows(q, 0, piece), to_y, at_rows(qy, 0, piece)),
            "n2b": (at_rows(q, piece, piece), to_y, at_rows(qy, piece, piece)),
            "f1": (at_rows(qx, 0, piece), to_y, at_rows(qd, 0, piece)),
            "f2": (at_rows(qy, piece, piece), to_x, at_rows(qd, piece, piece)),
            "c0": (at_rows(q), other, at_rows(q)),
            "c1": (at_rows(qx), other, at_rows(qx)),
            "c2": (at_rows(qy), other, at_rows(qy)),
            "c3": (at_rows(qd), other, at_rows(qd)),
        }[name]
        i = sid("g", s, k, name)
        if landing:
            return remote(ref.at[lands, :], ref.at[lands, :], i, i, device)
        return remote(ref.at[at, :], ref.at[at, :], i, i, device)

    names_of_gather = ("n1a", "n2b", "n1b", "n2a", "c0", "f1", "f2", "c1", "c2", "c3")

    def z_wait(w, p):
        at = at_rows(q, p * piece, piece)
        i = sid("z", w, p)
        remote(far.at[w, c, at, :], far.at[w, c, at, :], i, i, (near, m)).wait_recv()

    def lead_start(s, k):
        if s > 0:

            @pl.when(outer)
            def _():
                for p in range(2):
                    z_wait(s - 1, p)

        for name in names_of_gather[:5]:
            gather(s, k, name).start()

    def lead_forward(s, k):
        gather(s, k, "n1a", True).wait_recv()
        gather(s, k, "f1").start()
        gather(s, k, "n2b", True).wait_recv()
        gather(s, k, "f2").start()

    def lead_share(s, k):
        gather(s, k, "n1b", True).wait_recv()
        gather(s, k, "c1").start()
        gather(s, k, "n2a", True).wait_recv()
        gather(s, k, "c2").start()
        if s > 0:
            take_most(s, k)

    def lead_finish(s, k):
        gather(s, k, "f1", True).wait_recv()
        gather(s, k, "f2", True).wait_recv()
        gather(s, k, "c3").start()
        if s > 0:
            take_rest(s, k)

    def follow_most(s, k):
        for name in ("c0", "c1", "c2"):
            gather(s, k, name, True).wait_recv()
        if s > 0:
            take_most(s, k)

    def follow_rest(s, k):
        gather(s, k, "c3", True).wait_recv()
        if s > 0:
            take_rest(s, k)

    def z_own(p, in_inner):
        at = at_rows(q, p * piece, piece)
        w = 0 if in_inner else 1
        target = across if in_inner else skip
        return remote(
            x_own.at[c, at, :], far.at[w, c, at, :], sid("zs", p), sid("z", w, p), (target, m)
        )

    def z_next(w, p):
        at = at_rows(q, p * piece, piece)
        return remote(
            far.at[w, c, at, :], far.at[w, c, at, :], sid("zf", w, p), sid("z", w, p), (near, m)
        )

    def z_forward(w, p):
        @pl.when(inner)
        def _():
            z_wait(w, p)
            z_next(w, p).start()

    def z_send(in_inner):
        @pl.when(inner if in_inner else outer)
        def _():
            for p in range(2):
                z_own(p, in_inner).start()

    def rank_copy(k, d):
        i = sid("rx", k, d)
        return remote(rank_in.at[k, 0], rank_in.at[k, d], i, i, (r, apart(m, d)))

    def project(k):
        total = jnp.zeros((size, lanes), F32)
        for i in range(4):
            total = total + lax.dot_general(
                x_own[k, :, i * quarter : (i + 1) * quarter],
                maps_ref(i)[...],
                (((1,), (1,)), ((), ())),
                preferred_element_type=F32,
            )
        adapter = x_own[k, :, dim : dim + 128].astype(F32)
        at_lane = lax.broadcasted_iota(jnp.int32, (rows, lanes), 1) // span
        packed = jnp.zeros((rows, lanes), F32)
        for b in range(chips):
            low = slice(b * rows, (b + 1) * rows)
            mine = (at_lane == b) & (adapter[low] == m.astype(F32))
            packed = packed + jnp.where(mine, total[low], 0.0)
        rank_in[k, 0] = packed.astype(BF16)
        for d in range(1, n_mlp):
            rank_copy(k, d).start()

    def far_rank_copy(k, e):
        target = across if e == 0 else skip
        return remote(
            rank_sum.at[k],
            ranks.at[1 + kind, k],
            sid("rts", k, e),
            far_base + kind * 2 + k,
            (target, m),
        )

    def sum_ranks(k):
        total = rank_in[k, 0].astype(F32)
        for d in range(1, n_mlp):
            rank_copy(k, d).wait_recv()
            total = total + rank_in[k, d].astype(F32)
        rank_sum[k] = total.astype(BF16)
        for e in range(2):
            far_rank_copy(k, e).start()

    def wait_far_ranks(w, k):
        i = far_base + w * 2 + k
        remote(rank_sum.at[k], ranks.at[1 + w, k], i, i, (across, m)).wait_recv()

    def spread(g, k):
        adapter = x_own[k, :, dim : dim + 128].astype(F32)
        at_lane = lax.broadcasted_iota(jnp.int32, (rows, lanes), 1) // half
        for b in range(chips):
            low = slice(b * rows, (b + 1) * rows)
            mine = adapter[low] == at_lane.astype(F32)
            start = 2 * b * lanes
            values = jnp.dot(
                ranks[g, k], pick[:, start : start + 2 * lanes], preferred_element_type=F32
            )
            gate_low[low, :] = jnp.where(mine, values[:, 0:lanes], 0.0).astype(BF16)
            up_low[low, :] = jnp.where(mine, values[:, lanes:], 0.0).astype(BF16)

    def wide_sums(k, cols):
        return (
            jnp.dot(x_own[k, :, 0:dim], w_gate[:, cols], preferred_element_type=F32),
            jnp.dot(x_own[k, :, 0:dim], w_up[:, cols], preferred_element_type=F32),
        )

    def finish_tile(g, k, cols, sums):
        gate_sum = sums[0] + jnp.dot(gate_low[...], ups[0, :, cols], preferred_element_type=F32)
        up_sum = sums[1] + jnp.dot(up_low[...], ups[1, :, cols], preferred_element_type=F32)
        hid[g, k, :, cols] = (gate_sum / (1.0 + jnp.exp(-gate_sum)) * up_sum).astype(BF16)

    def need_weights(low, high):
        for t in range(low, high):
            for copy in weight_copies(t):
                copy.wait()

    def segment(g, k, low, high):
        for t in range(low, high):
            cols = slice(t * tile, (t + 1) * tile)
            finish_tile(g, k, cols, wide_sums(k, cols))

    def near_copy(k):
        i = sid("h", k)
        return remote(hid_own.at[k], hid_near.at[k], i, i, (near, m))

    def term_copy(k, slot):
        i = sid("k", slot)
        target = apart(q, slot // 2)
        return remote(
            term.at[k, at_rows(target), :], term_in.at[slot], i, i, (r, target * 2 + k)
        )

    def terms(k):
        values = lax.dot_general(
            hid_own[k], downs_in[...], (((1,), (1,)), ((), ())), preferred_element_type=F32
        )
        adapter = x_own[k, :, dim : dim + 128].astype(F32)
        at_lane = lax.broadcasted_iota(jnp.int32, values.shape, 1) // half
        term[k] = jnp.where(adapter == at_lane.astype(F32), values, 0.0).astype(BF16)

        def same():
            term_in[0] = term[k, at_rows(q), :]
            for e in range(1, chips):
                term_copy(k, 2 * e).start()

        def other():
            for e in range(chips):
                term_copy(k, 2 * e + 1).start()

        on(k, same)
        on(1 - k, other)

    def down_near(b):
        for k in range(2):
            for t in range(columns // narrow):
                cols = slice(t * narrow, (t + 1) * narrow)
                value = jnp.dot(hid_near[k], w_down[:, cols], preferred_element_type=F32)
                part[b, k, :, cols] = value.astype(BF16)

    def down_chunk(b, g, k):
        for t in range(columns // narrow):
            cols = slice(t * narrow, (t + 1) * narrow)
            value = jnp.dot(hid[g, k], w_down[:, cols], preferred_element_type=F32)
            part[b, k, :, cols] = value.astype(BF16)

    def core_copy(j):
        i = sid("rc", j)
        return remote(part.at[j % 2, 1 - c], core_in.at[j], i, i, (r, q * 2 + 1 - c))

    def one_copy(j, e):
        i = sid("r1", j, e)
        at = at_rows(first) if e == 0 else at_rows(qd)
        return remote(part.at[j % 2, c, at, :], one_in.at[j, e], i, i, (r, first * 2 + c))

    def two_copy(j):
        i = sid("r2", j)
        return remote(
            part.at[j % 2, c, at_rows(second), :], two_in.at[j], i, i, (r, second * 2 + c)
        )

    def home(j):
        if j == 2:
            return near
        return 2 - r // 2 if j == 1 else 3 * (1 - r // 2)

    def z_copy(j):
        return remote(z_out.at[j - 1], z_in.at[r], sid("zo", j), z_base + r, (home(j), m))

    def sum_cores(j):
        core_copy(j).wait_recv()
        b = j % 2

        def add(e, carry):
            at = pl.ds(pl.multiple_of(e * 16, 16), 16)
            value = part[b, c, at, :].astype(F32) + core_in[j, at, :].astype(F32)
            part[b, c, at, :] = value.astype(BF16)
            return carry

        lax.fori_loop(0, size // 16, add, 0)
        for e in range(2):
            one_copy(j, e).start()

    def sum_first(j):
        one_copy(j, 1).wait_recv()
        b, at = j % 2, at_rows(second)
        part[b, c, at, :] = (part[b, c, at, :].astype(F32) + one_in[j, 1].astype(F32)).astype(BF16)
        two_copy(j).start()

    def sum_second(j):
        one_copy(j, 0).wait_recv()
        two_copy(j).wait_recv()
        value = (
            part[j % 2, c, at_rows(q), :].astype(F32)
            + one_in[j, 0].astype(F32)
            + two_in[j].astype(F32)
        ).astype(BF16)
        if j == 0:
            z_in[r] = value
        else:
            z_out[j - 1] = value
            z_copy(j).start()

    low_half = pl.ds(0, columns // 2)
    tail_in = core_in.at[0, :, low_half]
    tail_one = one_in.at[0, :, :, low_half]
    tail_two = two_in.at[0, :, low_half]

    def half_at(h):
        return pl.ds(pl.multiple_of(h * (columns // 2), columns // 2), columns // 2)

    def tail_down(h):
        value = jnp.dot(hid_far[1], w_down[:, half_at(h)], preferred_element_type=F32)
        part[1, 1, :, half_at(h)] = value.astype(BF16)

    def tail_swap():
        i = sid("tc")
        return remote(part.at[1, 1, :, half_at(1 - c)], tail_in, i, i, (r, q * 2 + 1 - c))

    def tail_one_copy(e):
        i = sid("t1", e)
        at = at_rows(first) if e == 0 else at_rows(qd)
        return remote(part.at[1, 1, at, half_at(c)], tail_one.at[e], i, i, (r, first * 2 + c))

    def tail_two_copy():
        i = sid("t2")
        at = at_rows(second)
        return remote(part.at[1, 1, at, half_at(c)], tail_two, i, i, (r, second * 2 + c))

    def tail_z_copy():
        return remote(
            tail_out,
            z_in.at[r, :, half_at(c)],
            sid("tz"),
            half_base + c * n_req + r,
            (home(3), q * 2 + 1),
        )

    def tail_cores():
        tail_swap().wait_recv()
        at = half_at(c)
        part[1, 1, :, at] = (part[1, 1, :, at].astype(F32) + tail_in[...].astype(F32)).astype(BF16)
        for e in range(2):
            tail_one_copy(e).start()

    def tail_first():
        tail_one_copy(1).wait_recv()
        rows_at, at = at_rows(second), half_at(c)
        part[1, 1, rows_at, at] = (
            part[1, 1, rows_at, at].astype(F32) + tail_one[1].astype(F32)
        ).astype(BF16)
        tail_two_copy().start()

    def tail_second():
        tail_one_copy(0).wait_recv()
        tail_two_copy().wait_recv()
        tail_out[...] = (
            part[1, 1, at_rows(q), half_at(c)].astype(F32)
            + tail_one[0].astype(F32)
            + tail_two[...].astype(F32)
        ).astype(BF16)
        tail_z_copy().start()

    def sum_terms():
        total = term_in[0].astype(F32)
        for slot in range(1, n_mlp):
            term_copy(0, slot).wait_recv()
            total = total + term_in[slot].astype(F32)
        term_in[0] = total.astype(BF16)
        outs_copy.wait()
        tok_again.wait()

    def z_arrival(step):
        source = apart(r, step)
        whole = z_in.at[source]

        def wait_whole():
            i = z_base + source
            remote(whole, whole, i, i, (source, m)).wait_recv()

        def wait_halves():
            for h in range(2):
                i = half_base + h * n_req + source
                part_of = z_in.at[source, :, half_at(h)]
                remote(part_of, part_of, i, i, (source, m)).wait_recv()

        if step == 1:
            wait_whole()
        else:
            pl.when(outer & (c == 1))(wait_halves)
            pl.when(inner | (c == 0))(wait_whole)

    def part_free(j):
        core_copy(j).wait_send()
        for e in range(2):
            one_copy(j, e).wait_send()
        two_copy(j).wait_send()

    def own_free(k):
        def fn():
            for name in names_of_gather:
                gather(0, k, name).wait_send()
            for p in range(2):

                @pl.when(inner)
                def _(p=p):
                    z_own(p, True).wait_send()

                @pl.when(outer)
                def _(p=p):
                    z_own(p, False).wait_send()

        on(k, fn)

    def tick(fn, *args):
        return lambda: fn(*args)

    def tick_on(core, fn, *args):
        return lambda: on(core, lambda: fn(*args))

    def lead_first():
        lead_start(0, 0)
        lead_forward(0, 0)
        z_send(True)
        lead_share(0, 0)
        lead_finish(0, 0)

    def follow_first():
        z_send(True)
        follow_most(0, 0)
        follow_rest(0, 0)

    on(0, lead_first)
    on(1, follow_first)
    for copy in map_copies:
        copy.wait()
    project(0)
    tick_on(1, lead_start, 0, 1)()
    z_send(False)
    z_forward(0, 0)
    ups_copy.wait()
    z_forward(0, 1)
    sum_ranks(0)
    need_weights(0, early)

    events = {
        0: (
            [],
            [tick(need_weights, early, late)],
            [
                tick(need_weights, late, tiles),
                tick_on(1, lead_forward, 0, 1),
                tick_on(1, lead_share, 0, 1),
            ],
            [
                ins_copy.wait,
                tick(terms, 0),
                tick_on(1, lead_finish, 0, 1),
                tick_on(0, follow_most, 0, 1),
                tick_on(0, follow_rest, 0, 1),
                tick(project, 1),
                tick_on(0, lead_start, 1, 0),
                down_copy.wait,
            ],
            [tick(sum_ranks, 1)],
        ),
        1: (
            [tick(z_forward, 1, 0), tick(z_forward, 1, 1)],
            [tick_on(0, lead_forward, 1, 0)],
            [
                tick(own_free, 0),
                tick_on(0, lead_share, 1, 0),
                tick_on(1, lead_start, 1, 1),
                lambda: near_copy(0).start(),
            ],
            [
                tick_on(1, follow_most, 1, 0),
                tick_on(0, lead_finish, 1, 0),
                lambda: near_copy(1).start(),
                tick(terms, 1),
            ],
            [
                lambda: core_copy(0).start(),
                tick_on(1, follow_rest, 1, 0),
                tick(wait_far_ranks, 0, 0),
                tick(loaded, 1, 0),
            ],
        ),
        2: (
            [tick(own_free, 1), tick_on(1, lead_forward, 1, 1)],
            [tick_on(1, lead_share, 1, 1), tick(sum_cores, 0)],
            [
                tick_on(1, lead_finish, 1, 1),
                tick_on(0, follow_most, 1, 1),
                tick_on(0, lead_start, 2, 0),
            ],
            [tick_on(0, follow_rest, 1, 1), tick(sum_first, 0)],
            [tick(wait_far_ranks, 0, 1), tick(loaded, 1, 1)],
        ),
        3: (
            [],
            [tick_on(0, lead_forward, 2, 0)],
            [
                tick_on(0, lead_share, 2, 0),
                tick(sum_second, 0),
                tick_on(1, lead_start, 2, 1),
            ],
            [tick_on(0, lead_finish, 2, 0), tick_on(1, follow_most, 2, 0)],
            [
                lambda: core_copy(1).start(),
                tick_on(1, follow_rest, 2, 0),
                tick(wait_far_ranks, 1, 0),
                tick(loaded, 2, 0),
            ],
        ),
        4: (
            [],
            [
                tick(sum_cores, 1),
                tick_on(1, lead_forward, 2, 1),
                tick_on(1, lead_share, 2, 1),
            ],
            [tick_on(0, follow_most, 2, 1)],
            [
                tick(sum_first, 1),
                tick_on(1, lead_finish, 2, 1),
                outs_copy.start,
                tok_again.start,
                tick(part_free, 0),
                lambda: near_copy(0).wait_recv(),
                lambda: near_copy(1).wait_recv(),
                tick(down_near, 0),
                lambda: core_copy(2).start(),
                tick_on(0, follow_rest, 2, 1),
                tick(sum_second, 1),
                tick(part_free, 1),
            ],
            [
                tick_on(1, lambda: core_copy(3).start()),
                tick(wait_far_ranks, 1, 1),
                tick(loaded, 2, 1),
            ],
        ),
        5: (
            [],
            [tick(sum_cores, 2)],
            [tick(sum_first, 2), tick_on(0, sum_cores, 3)],
            [],
            [],
        ),
    }
    chunks = len(events)

    def chunk_step(i, carry):
        k, group = i % 2, i // 2
        g = (group + 1) // 2

        def happen(place):
            for number in range(chunks):
                if events[number][place]:

                    @pl.when(i == number)
                    def _(number=number):
                        for fn in events[number][place]:
                            fn()

        happen(0)

        spread(group, k)
        segment(g, k, 0, early)
        happen(1)
        segment(g, k, early, late)
        happen(2)
        segment(g, k, late, tiles)
        happen(3)

        @pl.when(i < chunks - 1)
        def _():
            down_chunk(g, g, k)

        happen(4)
        return carry

    lax.fori_loop(0, chunks, chunk_step, 0)
    tail_down(1 - c)
    tail_swap().start()
    tail_down(c)
    tail_cores()
    sum_second(2)
    tick_on(0, sum_first, 3)()
    sum_terms()
    tail_first()
    tick_on(0, sum_second, 3)()
    tail_second()

    def gather_sent(s, k):
        for name in names_of_gather:
            gather(s, k, name).wait_send()

    def terms_sent(k, slots):
        for slot in slots:
            term_copy(k, slot).wait_send()

    for s in (1, 2):
        for k in range(2):
            tick_on(k, gather_sent, s, k)()

    @pl.when(inner)
    def _():
        for w in range(2):
            for p in range(2):
                z_next(w, p).wait_send()

    for k in range(2):
        for d in range(1, n_mlp):
            rank_copy(k, d).wait_send()
        for e in range(2):
            far_rank_copy(k, e).wait_send()
        near_copy(k).wait_send()
        tick_on(k, terms_sent, k, range(2, n_mlp, 2))()
        tick_on(1 - k, terms_sent, k, range(1, n_mlp, 2))()
    part_free(2)
    on(1, lambda: core_copy(3).wait_send())

    def last_sent():
        for e in range(2):
            one_copy(3, e).wait_send()
        two_copy(3).wait_send()
        z_copy(3).wait_send()

    on(0, last_sent)
    z_copy(1).wait_send()
    z_copy(2).wait_send()
    for step in range(1, n_req):
        z_arrival(step)
    for b in range(n_req):
        cols = slice(b * columns, (b + 1) * columns)
        out[:, cols] = (
            tokens[:, cols].astype(F32)
            + z_in[b].astype(F32)
            + jnp.dot(term_in[0], outs_at[:, cols], preferred_element_type=F32)
        ).astype(BF16)
    tail_swap().wait_send()
    for e in range(2):
        tail_one_copy(e).wait_send()
    tail_two_copy().wait_send()
    tail_z_copy().wait_send()
    assert len(ids) <= s_sem.shape[0], len(ids)


def pair_call(
    tokens,
    norm_scale,
    gate_matrix,
    up_matrix,
    down_matrix,
    adapter_down_maps,
    adapter_gate_up_out,
    adapter_down_proj_in,
    adapter_down_proj_out,
    token_adapters,
):
    n_req, n_mlp = lax.axis_size("req"), lax.axis_size("mlp")
    rows, dim = tokens.shape
    hidden = gate_matrix.shape[1]
    columns = down_matrix.shape[1]
    lanes = adapter_down_proj_in.shape[0]
    chips = n_mlp // 2
    size = chips * rows
    vmem = pl.BlockSpec(memory_space=pltpu.VMEM)
    hbm = pl.BlockSpec(memory_space=pltpu.HBM)
    dma = pltpu.SemaphoreType.DMA
    out, _ = pl.pallas_call(
        functools.partial(pair_kernel, n_req, n_mlp),
        out_shape=(
            jax.ShapeDtypeStruct((rows, dim), BF16),
            jax.ShapeDtypeStruct((2, 2, size, dim + 128), BF16),
        ),
        in_specs=[hbm, vmem, vmem, hbm, hbm, hbm, hbm, hbm, hbm, hbm],
        out_specs=(vmem, hbm),
        scratch_shapes=[
            pltpu.VMEM((dim, hidden), BF16),
            pltpu.VMEM((dim, hidden), BF16),
            pltpu.VMEM((hidden, columns), BF16),
            pltpu.VMEM((2, lanes, hidden), BF16),
            pltpu.VMEM((lanes, hidden), BF16),
            pltpu.VMEM((2, size, dim + 128), BF16),
            pltpu.VMEM((2, 2, size, hidden), BF16),
            pltpu.VMEM((2, size, hidden), BF16),
            pltpu.VMEM((2, 2, size, columns), BF16),
            pltpu.VMEM((4, size, columns), BF16),
            pltpu.VMEM((4, 2, rows, columns), BF16),
            pltpu.VMEM((4, rows, columns), BF16),
            pltpu.VMEM((3, rows, columns), BF16),
            pltpu.VMEM((n_req, rows, columns), BF16),
            pltpu.VMEM((lanes, 2 * chips * lanes), BF16),
            pltpu.VMEM((size, lanes), BF16),
            pltpu.VMEM((size, lanes), BF16),
            pltpu.VMEM((2, n_mlp, rows, lanes), BF16),
            pltpu.VMEM((3, 2, rows, lanes), BF16),
            pltpu.VMEM((2, size, lanes), BF16),
            pltpu.VMEM((n_mlp, rows, lanes), BF16),
            pltpu.VMEM((rows, columns // 2), BF16),
            dma((2, hidden // tile_of(hidden))),
            dma((45,)),
            dma((144,)),
            dma((144,)),
        ],
        compiler_params=pltpu.CompilerParams(
            collective_id=0, has_side_effects=True, vmem_limit_bytes=67043328
        ),
    )(
        tokens,
        norm_scale.reshape(1, dim),
        token_adapters.reshape(1, rows),
        gate_matrix,
        up_matrix,
        down_matrix,
        adapter_down_maps[0],
        adapter_gate_up_out,
        adapter_down_proj_in,
        adapter_down_proj_out,
    )
    return out


def block_call(
    tokens,
    norm_scale,
    gate_matrix,
    up_matrix,
    down_matrix,
    adapter_down_maps,
    adapter_gate_up_out,
    adapter_down_proj_in,
    adapter_down_proj_out,
    token_adapters,
):
    n_req, n_mlp = lax.axis_size("req"), lax.axis_size("mlp")
    rows, dim = tokens.shape
    hidden = gate_matrix.shape[1]
    columns = down_matrix.shape[1]
    span = adapter_down_maps.shape[1]
    half = span // 2
    ranks = adapter_down_proj_in.shape[0]
    bits = n_mlp.bit_length() - 1
    group = n_req * rows
    ups = adapter_gate_up_out.reshape(2, n_mlp, half, hidden)
    ups = ups.transpose(1, 0, 2, 3).reshape(n_mlp * span, hidden)
    vmem = pl.BlockSpec(memory_space=pltpu.VMEM)
    hbm = pl.BlockSpec(memory_space=pltpu.HBM)
    dma = pltpu.SemaphoreType.DMA
    out, _ = pl.pallas_call(
        functools.partial(block_kernel, n_req, n_mlp),
        out_shape=(
            jax.ShapeDtypeStruct((rows, dim), BF16),
            jax.ShapeDtypeStruct((n_mlp, group, columns), BF16),
        ),
        in_specs=[vmem, vmem, vmem, hbm, hbm, hbm, vmem, vmem, vmem, vmem],
        out_specs=(vmem, hbm),
        scratch_shapes=[
            pltpu.VMEM((n_mlp * rows, dim + 128), BF16),
            pltpu.VMEM((n_mlp * span, dim), BF16),
            pltpu.VMEM((dim, hidden), BF16),
            pltpu.VMEM((dim, hidden), BF16),
            pltpu.VMEM((hidden, columns), BF16),
            pltpu.VMEM((n_req, n_mlp * rows, hidden), BF16),
            pltpu.VMEM((group, columns), F32),
            pltpu.VMEM((group, columns), BF16),
            pltpu.VMEM((n_req, rows, columns), BF16),
            pltpu.VMEM((n_mlp, rows, ranks), BF16),
            pltpu.VMEM((n_mlp, rows, ranks), BF16),
            dma((2, hidden // tile_of(hidden))),
            dma,
            dma,
            dma((n_mlp,)),
            dma((n_mlp,)),
            dma((bits,)),
            dma((bits,)),
            dma((2, n_req - 1, n_mlp)),
            dma((2, n_req - 1, n_mlp)),
            dma((n_mlp,)),
            dma((n_mlp,)),
            dma((n_mlp,)),
            dma((n_mlp,)),
            dma((n_req,)),
            dma((n_req,)),
        ],
        compiler_params=pltpu.CompilerParams(
            collective_id=0, has_side_effects=True, vmem_limit_bytes=67043328
        ),
    )(
        tokens,
        norm_scale.reshape(1, dim),
        token_adapters,
        gate_matrix,
        up_matrix,
        down_matrix,
        adapter_down_maps[0],
        ups,
        adapter_down_proj_in,
        adapter_down_proj_out,
    )
    return out


def solution(mesh):
    per_device = pair_call if (mesh.shape["req"], mesh.shape["mlp"]) == (4, 8) else block_call
    return jax.shard_map(
        per_device,
        mesh=mesh,
        in_specs=(
            P(("req", "mlp"), None),
            P(),
            P(None, "mlp"),
            P(None, "mlp"),
            P("mlp", "req"),
            P("mlp", None, None),
            P(None, None, "mlp"),
            P(None, "mlp"),
            P(),
            P(("req", "mlp"), None),
        ),
        out_specs=P(("req", "mlp"), None),
        check_vma=False,
    )
```
